256 devices in a mesh: seq: 64 (over z, y, core), fsdp: 4 (over x).
Axes of the slice: x: 4, y: 4, z: 8, core: 2. Of those that a mesh axis runs over, the one named last changes fastest.
Arguments:
- inputs: bfloat16 [4, 8192, 3584], P('fsdp', 'seq'), may hold values from -36 to 36
- keys_queries: bfloat16 [4, 8192, 256], P('fsdp', 'seq'), may hold values from -0.29882812 to 0.29882812
- log_decay: float32 [4, 56, 8192], P('fsdp', None, 'seq'), may hold values from -1.5 to 0, as said below
- skip: float32 [56], replicated, may hold values from 0.5 to 1.5
- classifier: bfloat16 [3584, 128], P('fsdp'), may hold values from -0.09375 to 0.09375
Outputs:
- mixed: bfloat16 [4, 8192, 3584], P('fsdp', 'seq')
- logits: float32 [4, 128], P('fsdp')
The draws below stay inside these ranges and needn't reach their ends.
Inputs may be any that keep to these rules, and one draw needn't show every extreme that they name: `log_decay`: log-decays are negative.
All inputs are finite; a program needn't handle non-finite values.
Results may differ from the reference program's by a relative error of at most 0.0051.
Values may be sent and summed in bfloat16 or wider, within the bound.
A program may use at most 256 MiB of HBM per device.

```python
import math
import jax
import jax.numpy as jnp
from jax import lax

H = 56
N = 128
K = 128
GROUP = 128
TOK_DEV = 128
HP = 3584
COPIES = 4
LEN = 8192


def draw_inputs(key, part):
    first, second, third = jax.random.split(key, 3)
    shape = (COPIES, LEN, HP)
    row_scale = jnp.exp(jax.random.uniform(second, (COPIES, LEN, 1), jnp.float32, math.log(0.3), math.log(3.0)))
    column_scale = jnp.exp(jax.random.uniform(third, (1, 1, HP), jnp.float32, math.log(0.3), math.log(3.0)))
    base = jnp.clip(jax.random.normal(first, shape, jnp.float32), -4.0, 4.0)
    return (base * row_scale * column_scale).astype(jnp.bfloat16)


def draw_log_decay(key, part):
    pieces = jax.random.split(key, 7)
    share_fast = 0.5
    chooser = jax.random.uniform(pieces[0], (COPIES, H, 1), jnp.float32)
    fast_rate = jax.random.uniform(pieces[1], (COPIES, H, 1), jnp.float32, 1.0 / 50.0, 1.0 / 30.0)
    slow_rate = jax.random.uniform(pieces[2], (COPIES, H, 1), jnp.float32, 0.05, 0.25) / LEN
    default_fading_speed = jnp.where(chooser < share_fast, fast_rate, slow_rate)
    block_count = LEN // TOK_DEV
    segment_fading_multiplier = jnp.exp(jax.random.uniform(pieces[3], (COPIES, H, block_count, 1), jnp.float32, math.log(0.5), math.log(2.0)))
    segment_fading_multiplier = jnp.broadcast_to(segment_fading_multiplier, (COPIES, H, block_count, TOK_DEV)).reshape(COPIES, H, LEN)
    offset_fading_multiplier = jnp.exp(jax.random.uniform(pieces[4], (COPIES, H, LEN), jnp.float32, math.log(0.5), math.log(2.0)))
    places = jax.random.randint(pieces[5], (COPIES, 3, 1), 0, LEN)
    damaged_symbols = (jnp.arange(LEN)[None, None, :] == places).astype(jnp.float32)
    objective_entries = jnp.log(jax.random.uniform(pieces[6], (COPIES, H, 3), jnp.float32, 0.65, 0.8))
    random_spikes = jnp.sum(damaged_symbols[:, None, :, :] * objective_entries[:, :, :, None], axis=2)
    return -default_fading_speed * segment_fading_multiplier * offset_fading_multiplier + random_spikes


def levels(rng, extent, shards, low, top_value):
    gain, own = 1.0, jax.random.fold_in(rng, 6)
    for axis_at, blocks in shards:
        heights = jnp.exp(jax.random.uniform(jax.random.fold_in(own, axis_at), (blocks,), jnp.float32, low / len(shards), top_value / len(shards)))
        gain = gain * jnp.repeat(heights, extent[axis_at] // blocks).reshape([-1 if axis == axis_at else 1 for axis in range(len(extent))])
    return gain


def centred(own_key, shape, spread, most, shards=(), kind=jnp.bfloat16):
    array = spread * jax.random.normal(own_key, shape, jnp.float32)
    if shards:
        array = array * levels(own_key, shape, shards, -0.22, 0.18)
    return jnp.clip(array, -most, most).astype(kind)


def setup_inputs(seed: int = 0) -> dict:
    seeds = jax.random.split(jax.random.key(seed), 6)
    inputs = draw_inputs(jax.random.fold_in(seeds[5], 71), 0)
    keys_queries = centred(seeds[1], (COPIES, LEN, 2 * N), 0.05, 0.29882812, ((0, 4), (1, 64)))
    log_decay = draw_log_decay(jax.random.fold_in(seeds[5], 71), 0)
    skip = jnp.clip(jax.random.uniform(seeds[3], (H,), jnp.float32, 0.5, 1.5), 0.5, 1.5)
    classifier = centred(seeds[4], (HP, K), HP ** -0.5, 0.09375, ((0, 4),))
    return dict(inputs=inputs, keys_queries=keys_queries, log_decay=log_decay, skip=skip, classifier=classifier)


epsilon = 1e-06

def reference(inputs, keys_queries, log_decay, skip, classifier):
    copies, positions, channels = inputs.shape
    head_count = log_decay.shape[1]
    head_dim = channels // head_count
    blocks = positions // GROUP
    causal = jnp.arange(GROUP)[:, None] >= jnp.arange(GROUP)[None, :]

    def group_step(carry, block_index):
        carry_state, pooled_sum = carry
        leading_row = (block_index * GROUP).astype(jnp.int32)
        value_block = lax.dynamic_slice_in_dim(inputs, leading_row, GROUP, 1)
        paired_block_matrix = lax.dynamic_slice_in_dim(keys_queries, leading_row, GROUP, 1)
        decay_block = lax.dynamic_slice_in_dim(log_decay, leading_row, GROUP, 2)
        keys = paired_block_matrix[:, :, :N].astype(jnp.float32)
        queries = paired_block_matrix[:, :, N:].astype(jnp.float32)
        values = value_block.reshape(copies, GROUP, head_count, head_dim).astype(jnp.float32)
        cumulative = jnp.cumsum(decay_block, axis=-1)
        scores = jnp.einsum('ctn,cun->ctu', queries, keys)
        decay_gap = jnp.where(causal, cumulative[:, :, :, None] - cumulative[:, :, None, :], -jnp.inf)
        mixing = (scores[:, None] * jnp.exp(decay_gap)).astype(jnp.bfloat16)
        mixing = lax.optimization_barrier(mixing).astype(jnp.float32)
        diagonal = jnp.einsum('chtu,cuhp->cthp', mixing, values)
        carried = lax.optimization_barrier(carry_state.astype(jnp.bfloat16)).astype(jnp.float32)
        growth = jnp.exp(cumulative).transpose(0, 2, 1)[..., None]
        carried_out = jnp.einsum('ctn,chnp->cthp', queries, carried) * growth
        result = diagonal + carried_out + skip[None, None, :, None] * values
        final_log = cumulative[:, :, -1:]
        weighted = (keys[:, None] * jnp.exp(final_log - cumulative)[..., None]).astype(jnp.bfloat16)
        weighted = lax.optimization_barrier(weighted).astype(jnp.float32)
        block_state = jnp.einsum('chun,cuhp->chnp', weighted, values)
        carry_state = jnp.exp(final_log)[..., None] * carry_state + block_state
        pooled_sum = pooled_sum + lax.optimization_barrier(jnp.sum(result, axis=1)).reshape(copies, channels)
        return ((carry_state, pooled_sum), result.reshape(copies, GROUP, channels).astype(jnp.bfloat16))
    initial = (jnp.zeros((copies, head_count, N, head_dim), jnp.float32), jnp.zeros((copies, channels), jnp.float32))
    (final_state, pooled_sum), outputs = lax.scan(group_step, initial, jnp.arange(blocks, dtype=jnp.int32))
    mixed = outputs.transpose(1, 0, 2, 3).reshape(copies, positions, channels)
    pooled = pooled_sum / positions
    normed = (pooled / jnp.sqrt(lax.optimization_barrier(jnp.mean(pooled * pooled, axis=-1, keepdims=True)) + epsilon)).astype(jnp.bfloat16)
    logits = jnp.dot(normed, classifier, preferred_element_type=jnp.float32)
    return (mixed, logits)
```

```python
import jax
import jax.numpy as jnp
from jax import lax
from jax.experimental import pallas as pl
from jax.experimental.pallas import tpu as pltpu
from jax.sharding import PartitionSpec as P

MESH = pl.DeviceIdType.MESH
F32, BF16 = jnp.float32, jnp.bfloat16

N = 128
G = 128
L = 128
NZ, NY, NC, NX = 8, 4, 2, 4
TILES = 28
M = TILES // NY
ROWS = M * 8
EPS = 1e-06


def spread(x):
    return jnp.concatenate(
        [jnp.broadcast_to(x[m : m + 1, :], (8, L)) for m in range(M)], axis=0
    )


def kernel(
    v_ref, kq_ref, ld_ref, skip_ref, cls_ref, mixed_ref, logits_ref,
    grow, local_out, own_state, pair_recv, pair_total, plane_recv, plane_prefix,
    axis_send, axis_recv, axis_prefix, start_plane, start_send, start_chip,
    carried, carried_send, table,
    decay_own, decay_pair, decay_chip, decay_plane, decay_sum, decay_axis, factor, factor_chip,
    pool_own, pool_pair, pool_pair_sum, pool_plane, pool_plane_sum, pool_axis,
    pair_s, pair_r, plane_s, plane_r, axis_s, axis_r, table_s, table_r, local_sem,
):
    me, x = lax.axis_index("seq"), lax.axis_index("fsdp")
    c = lax.rem(me, NC)
    y = lax.rem(me // NC, NY)
    z = me // (NC * NY)
    other = 1 - c
    partner = me + 1 - 2 * c
    ys = [lax.rem(y + k, NY) for k in range(NY)]
    zs = [lax.rem(z + k, NZ) for k in range(NZ)]

    def at(z_, y_, c_):
        return (z_ * NY + y_) * NC + c_

    to_y = [at(z, ys[k], c) for k in range(NY)]
    to_z = [at(zs[k], y, c) for k in range(NZ)]

    barrier = pltpu.get_barrier_semaphore()

    def greet(who):
        pl.semaphore_signal(barrier, inc=1, device_id=who, device_id_type=MESH)

    greet({"seq": partner})
    for k in range(1, NY):
        greet({"seq": to_y[k]})
    for k in range(1, NZ):
        greet({"seq": to_z[k]})
    for k in range(1, NX):
        greet({"fsdp": lax.rem(x + k, NX)})

    sends = []

    def push(src, dst, send, recv, who):
        copy = pltpu.make_async_remote_copy(
            src_ref=src, dst_ref=dst, send_sem=send, recv_sem=recv,
            device_id=who, device_id_type=MESH,
        )
        copy.start()
        sends.append(copy)
        return copy

    left_half = lax.broadcasted_iota(jnp.int32, (1, L), 1) < 64
    for g in range(NY):
        even = jnp.sum(ld_ref[pl.ds(2 * M * g, M, stride=2), :], axis=1, keepdims=True)
        odd = jnp.sum(ld_ref[pl.ds(2 * M * g + 1, M, stride=2), :], axis=1, keepdims=True)
        decay_own[g, 0:M, :] = jnp.where(left_half, even, odd)
        decay_own[g, M:8, :] = jnp.zeros((8 - M, L), F32)

    row = lax.broadcasted_iota(jnp.int32, (G, G), 0)
    col = lax.broadcasted_iota(jnp.int32, (G, G), 1)
    causal = row >= col
    lower = jnp.where(causal, 1.0, 0.0).astype(F32)
    log_decay = ld_ref[...]
    cum = lax.dot_general(
        log_decay, lower, (((1,), (1,)), ((), ())),
        precision=lax.Precision.HIGHEST, preferred_element_type=F32,
    )
    cum_t = lax.dot_general(
        lower, log_decay, (((1,), (1,)), ((), ())),
        precision=lax.Precision.HIGHEST, preferred_element_type=F32,
    )
    keys = kq_ref[:, :N]
    queries = kq_ref[:, N:]
    keys_t = keys.T

    pl.semaphore_wait(barrier, 1 + (NY - 1) + (NZ - 1) + (NX - 1))

    table_copies = [
        push(cls_ref, table.at[x], table_s.at[k], table_r.at[k], {"fsdp": lax.rem(x + k, NX)})
        for k in range(1, NX)
    ]
    own_rows = pltpu.make_async_copy(cls_ref, table.at[x], local_sem)
    own_rows.start()

    pair_decay = push(decay_own, decay_pair, pair_s.at[4], pair_r.at[4], {"seq": partner})
    pair_copies = []
    for g in range(NY):
        for m in range(M):
            j = g * M + m
            lanes = slice(j * L, (j + 1) * L)
            level = jnp.where(left_half, cum_t[:, 2 * j : 2 * j + 1], cum_t[:, 2 * j + 1 : 2 * j + 2])
            grow[j] = level
            weight = jnp.exp(level[G - 1 : G, :] - level)
            weighted = (v_ref[:, lanes].astype(F32) * weight).astype(BF16)
            state = jnp.dot(keys_t, weighted, preferred_element_type=F32).astype(BF16)
            for half in range(NC):
                for b in range(NZ):
                    first = half * 64 + b * 8
                    own_state[half, g, b, m * 8 : m * 8 + 8, :] = state[first : first + 8, :]
        pair_copies.append(
            push(own_state.at[other, g], pair_recv.at[g], pair_s.at[g], pair_r.at[g], {"seq": partner})
        )

    def inside(g):
        scores = lax.dot_general(
            queries, keys, (((1,), (1,)), ((), ())), preferred_element_type=F32
        )
        scores = jnp.where(causal, scores, 0.0)
        for m in range(M):
            j = g * M + m
            lanes = slice(j * L, (j + 1) * L)
            parts = []
            for h in (2 * j, 2 * j + 1):
                gap = jnp.minimum(cum_t[:, h : h + 1] - cum[h : h + 1, :], 0.0)
                parts.append((scores * jnp.exp(gap)).astype(BF16))
            value = v_ref[:, lanes]
            zero = jnp.zeros_like(value)
            stacked = jnp.concatenate(
                [jnp.where(left_half, value, zero), jnp.where(left_half, zero, value)], axis=0
            )
            diagonal = jnp.dot(
                jnp.concatenate(parts, axis=1), stacked, preferred_element_type=F32
            )
            direct = jnp.where(left_half, skip_ref[2 * j], skip_ref[2 * j + 1])
            local_out[j] = diagonal + direct * value.astype(F32)
            grow[j] = jnp.exp(grow[j])

    inside(0)

    pair_decay.wait_recv()
    for g in range(NY):
        mine, theirs = decay_own[g], decay_pair[g]
        decay_chip[g] = mine + theirs
        factor[0, g] = spread(jnp.where(c == 0, jnp.exp(theirs), 1.0))
        factor[1, g] = spread(jnp.where(c == 0, 1.0, jnp.exp(mine)))
        factor_chip[g] = spread(jnp.exp(jnp.where(c == 0, mine, theirs)))
    for copy in pair_copies:
        copy.wait_recv()

    plane_copies = []
    for k in (2, 1, 3, 0):
        g = ys[k]

        @pl.loop(0, NZ)
        def _(b, g=g, k=k):
            total = factor[0, g] * own_state[c, g, b].astype(F32) + factor[1, g] * pair_recv[g, b].astype(F32)
            if k == 0:
                plane_recv[y, b] = total.astype(BF16)
            else:
                pair_total[k, b] = total.astype(BF16)

        if k == 0:
            decay_plane[y] = decay_chip[y]
        else:
            plane_copies.append(
                push(decay_chip.at[g], decay_plane.at[y], plane_s.at[3 + k], plane_r.at[3 + k], {"seq": to_y[k]})
            )
            plane_copies.append(
                push(pair_total.at[k], plane_recv.at[y], plane_s.at[k], plane_r.at[k], {"seq": to_y[k]})
            )

    for g in range(1, NY):
        inside(g)
    for copy in plane_copies:
        copy.wait_recv()

    run = jnp.zeros((8, L), F32)
    for k in range(NY):
        factor[2, k] = spread(jnp.exp(decay_plane[k]))
        factor[3, k] = spread(jnp.exp(run))
        run = run + decay_plane[k]
    decay_sum[...] = run
    decay_axis[z] = run

    axis_copies = []
    for k in (4, 5, 3, 6, 2, 7, 1, 0):
        b = zs[k]
        total = jnp.zeros((ROWS, L), F32)
        for q in range(NY):
            plane_prefix[q, b] = total
            total = factor[2, q] * total + plane_recv[q, b].astype(F32)
        if k == 0:
            axis_recv[z] = total.astype(BF16)
        else:
            axis_send[k] = total.astype(BF16)
            axis_copies.append(
                push(decay_sum, decay_axis.at[z], axis_s.at[8 + k], axis_r.at[8 + k], {"seq": to_z[k]})
            )
            axis_copies.append(
                push(axis_send.at[k], axis_recv.at[z], axis_s.at[k], axis_r.at[k], {"seq": to_z[k]})
            )
    for copy in axis_copies:
        copy.wait_recv()

    total = jnp.zeros((ROWS, L), F32)
    for q in range(NZ):
        axis_prefix[q] = total.astype(BF16)
        if q < NZ - 1:
            total = spread(jnp.exp(decay_axis[q])) * total + axis_recv[q].astype(F32)
    back_copies = [
        push(axis_prefix.at[zs[k]], start_plane.at[z], axis_s.at[16 + k], axis_r.at[16 + k], {"seq": to_z[k]})
        for k in (4, 5, 3, 6, 2, 7, 1)
    ]
    start_plane[z] = axis_prefix[z]
    for copy in back_copies:
        copy.wait_recv()

    chip_copies = []
    for k in (2, 1, 3, 0):
        g = ys[k]

        @pl.loop(0, NZ)
        def _(b, g=g, k=k):
            start = factor[3, g] * start_plane[b].astype(F32) + plane_prefix[g, b]
            if k == 0:
                start_chip[y, b] = start.astype(BF16)
            else:
                start_send[k, b] = start.astype(BF16)

        if k:
            chip_copies.append(
                push(start_send.at[k], start_chip.at[y], plane_s.at[6 + k], plane_r.at[6 + k], {"seq": to_y[k]})
            )
    for copy in chip_copies:
        copy.wait_recv()

    half_copies = []
    for g in range(NY):

        @pl.loop(0, NZ)
        def _(b, g=g):
            first = start_chip[g, b].astype(F32)
            state = jnp.where(c == 0, own_state[c, g, b].astype(F32), pair_recv[g, b].astype(F32))
            second = factor_chip[g] * first + state
            carried[c, g, b] = jnp.where(c == 0, first, second).astype(BF16)
            carried_send[g, b] = jnp.where(c == 0, second, first).astype(BF16)

        half_copies.append(
            push(carried_send.at[g], carried.at[c, g], pair_s.at[5 + g], pair_r.at[5 + g], {"seq": partner})
        )

    pool_own[...] = jnp.zeros_like(pool_own)
    for g in range(NY):
        half_copies[g].wait_recv()
        for m in range(M):
            j = g * M + m
            start = jnp.concatenate(
                [
                    carried[half, g, b, m * 8 : m * 8 + 8, :]
                    for half in range(NC)
                    for b in range(NZ)
                ],
                axis=0,
            )
            full = local_out[j] + grow[j] * jnp.dot(queries, start, preferred_element_type=F32)
            mixed_ref[:, j * L : (j + 1) * L] = full.astype(BF16)
            pool_own[j : j + 1, :] = jnp.sum(full, axis=0, keepdims=True)

    pool_pair[c] = pool_own[...]
    copy = push(pool_own, pool_pair.at[c], pair_s.at[9], pair_r.at[9], {"seq": partner})
    copy.wait_recv()
    pool_pair_sum[...] = pool_pair[0] + pool_pair[1]
    pool_plane[y] = pool_pair_sum[...]
    copies = [
        push(pool_pair_sum, pool_plane.at[y], plane_s.at[9 + k], plane_r.at[9 + k], {"seq": to_y[k]})
        for k in (2, 1, 3)
    ]
    for copy in copies:
        copy.wait_recv()
    pool_plane_sum[...] = (pool_plane[0] + pool_plane[1]) + (pool_plane[2] + pool_plane[3])
    pool_axis[z] = pool_plane_sum[...]
    copies = [
        push(pool_plane_sum, pool_axis.at[z], axis_s.at[24 + k], axis_r.at[24 + k], {"seq": to_z[k]})
        for k in (4, 5, 3, 6, 2, 7, 1)
    ]
    for copy in copies:
        copy.wait_recv()
    pooled = pool_axis[0]
    for q in range(1, NZ):
        pooled = pooled + pool_axis[q]
    pooled = pooled / (G * NZ * NY * NC)
    square = jnp.sum(pooled * pooled, keepdims=True) / (TILES * L)
    normed = (pooled / jnp.sqrt(square + EPS)).astype(BF16)
    for copy in table_copies:
        copy.wait_recv()
    own_rows.wait()
    wide = jnp.concatenate(
        [jnp.broadcast_to(normed[j : j + 1, :], (16, L)) for j in range(TILES)], axis=1
    )
    classifier = table[...].reshape(TILES * L, L)
    logits = jnp.dot(wide, classifier, preferred_element_type=F32)
    logits_ref[...] = logits[0:1, :]

    for copy in sends:
        copy.wait_send()


def local(inputs, keys_queries, log_decay, skip, classifier):
    copies, positions, channels = inputs.shape
    heads = log_decay.shape[1]
    vm = pl.BlockSpec(memory_space=pltpu.VMEM)
    state = (NY, NZ, ROWS, L)
    scratch = [
        pltpu.VMEM((TILES, G, L), F32),
        pltpu.VMEM((TILES, G, L), F32),
        pltpu.VMEM((NC, *state), BF16),
        pltpu.VMEM(state, BF16),
        pltpu.VMEM(state, BF16),
        pltpu.VMEM(state, BF16),
        pltpu.VMEM(state, F32),
        pltpu.VMEM((NZ, ROWS, L), BF16),
        pltpu.VMEM((NZ, ROWS, L), BF16),
        pltpu.VMEM((NZ, ROWS, L), BF16),
        pltpu.VMEM((NZ, ROWS, L), BF16),
        pltpu.VMEM(state, BF16),
        pltpu.VMEM(state, BF16),
        pltpu.VMEM((NC, *state), BF16),
        pltpu.VMEM(state, BF16),
        pltpu.VMEM((NX, *classifier.shape), BF16),
        pltpu.VMEM((NY, 8, L), F32),
        pltpu.VMEM((NY, 8, L), F32),
        pltpu.VMEM((NY, 8, L), F32),
        pltpu.VMEM((NY, 8, L), F32),
        pltpu.VMEM((8, L), F32),
        pltpu.VMEM((NZ, 8, L), F32),
        pltpu.VMEM((4, NY, ROWS, L), F32),
        pltpu.VMEM((NY, ROWS, L), F32),
        pltpu.VMEM((32, L), F32),
        pltpu.VMEM((NC, 32, L), F32),
        pltpu.VMEM((32, L), F32),
        pltpu.VMEM((NY, 32, L), F32),
        pltpu.VMEM((32, L), F32),
        pltpu.VMEM((NZ, 32, L), F32),
        pltpu.SemaphoreType.DMA((10,)),
        pltpu.SemaphoreType.DMA((10,)),
        pltpu.SemaphoreType.DMA((13,)),
        pltpu.SemaphoreType.DMA((13,)),
        pltpu.SemaphoreType.DMA((32,)),
        pltpu.SemaphoreType.DMA((32,)),
        pltpu.SemaphoreType.DMA((4,)),
        pltpu.SemaphoreType.DMA((4,)),
        pltpu.SemaphoreType.DMA,
    ]
    mixed, logits = pl.pallas_call(
        kernel,
        out_shape=(
            jax.ShapeDtypeStruct((positions, channels), BF16),
            jax.ShapeDtypeStruct((1, classifier.shape[1]), F32),
        ),
        in_specs=[vm, vm, vm, pl.BlockSpec(memory_space=pltpu.SMEM), vm],
        out_specs=(vm, vm),
        scratch_shapes=scratch,
        compiler_params=pltpu.CompilerParams(
            collective_id=0, has_side_effects=True, vmem_limit_bytes=48 << 20
        ),
    )(
        inputs.reshape(positions, channels),
        keys_queries.reshape(positions, 2 * N),
        log_decay.reshape(heads, positions),
        skip,
        classifier,
    )
    return mixed.reshape(copies, positions, channels), logits


def solution(mesh):
    return jax.shard_map(
        local,
        mesh=mesh,
        in_specs=(
            P("fsdp", "seq", None),
            P("fsdp", "seq", None),
            P("fsdp", None, "seq"),
            P(),
            P("fsdp", None),
        ),
        out_specs=(P("fsdp", "seq", None), P("fsdp", None)),
        check_vma=False,
    )
```

```python
import jax
import jax.numpy as jnp
from jax import lax
from jax.experimental import pallas as pl
from jax.experimental.pallas import tpu as pltpu
from jax.sharding import PartitionSpec as P

MESH = pl.DeviceIdType.MESH
F32, BF16 = jnp.float32, jnp.bfloat16
HIGHEST = lax.Precision.HIGHEST

N = 128
G = 128
L = 128
NZ, NY, NC, NX = 8, 4, 2, 4
HEADS = 56
TILES = 28
M = TILES // NY
CHUNKS = ((0, 4), (4, 3))
NCH = len(CHUNKS)
EPS = 1e-06
FAR_Y = (2, 1, 3)
FAR_Z = (4, 5, 3, 6, 2, 7, 1)


def spread(x):
    return jnp.concatenate(
        [jnp.broadcast_to(x[m : m + 1, :], (8, L)) for m in range(M)], axis=0
    )


def kernel(
    v_hbm, kq_hbm, ld_hbm, skip_ref, cls_ref, mixed_ref, logits_ref,
    v_ref, kq_ref, ld_ref, out_ref, grow, local_out, table,
    decay_own, decay_pair, decay_chip, decay_plane, decay_sum, decay_axis,
    pair_factor, start_factor, plane_factor, plane_start, axis_factor,
    response, response_pair, pool_local, pool_own, pool_plane, pool_sum, pool_axis,
    *rest,
):
    buffers = [rest[i * 12 : (i + 1) * 12] for i in range(NCH)]
    (in_s, out_s, pair_s, pair_r, plane_s, plane_r, axis_s, axis_r,
     back_s, back_r, table_s, table_r, small_s, small_r) = rest[NCH * 12 :]
    me, x = lax.axis_index("seq"), lax.axis_index("fsdp")
    c = lax.rem(me, NC)
    y = lax.rem(me // NC, NY)
    z = me // (NC * NY)
    other = 1 - c
    ys = [lax.rem(y + k, NY) for k in range(NY)]
    zs = [lax.rem(z + k, NZ) for k in range(NZ)]

    def at(z_, y_, c_):
        return {"seq": (z_ * NY + y_) * NC + c_}

    to_pair = at(z, y, other)
    to_y = [at(z, ys[k], c) for k in range(NY)]
    to_y_other = [at(z, ys[k], other) for k in range(NY)]
    to_z = [at(zs[k], y, c) for k in range(NZ)]
    to_x = [{"fsdp": lax.rem(x + k, NX)} for k in range(NX)]

    barrier = pltpu.get_barrier_semaphore()
    partners = to_z[1:] + to_y[1:] + to_y_other[1:] + to_x[1:] + [to_pair]
    for who in partners:
        pl.semaphore_signal(barrier, inc=1, device_id=who, device_id_type=MESH)

    loads = [
        pltpu.make_async_copy(src, dst, in_s.at[i])
        for i, (src, dst) in enumerate(
            ((ld_hbm, ld_ref), (kq_hbm, kq_ref), (v_hbm, v_ref), (cls_ref, table.at[x]))
        )
    ]
    for load in loads:
        load.start()

    sends = []

    def push(src, dst, send, recv, who):
        copy = pltpu.make_async_remote_copy(
            src_ref=src, dst_ref=dst, send_sem=send, recv_sem=recv,
            device_id=who, device_id_type=MESH,
        )
        copy.start()
        sends.append(copy)
        return copy

    loads[0].wait()
    left_half = lax.broadcasted_iota(jnp.int32, (1, L), 1) < 64
    for g in range(NY):
        even = jnp.sum(ld_ref[pl.ds(2 * M * g, M, stride=2), :], axis=1, keepdims=True)
        odd = jnp.sum(ld_ref[pl.ds(2 * M * g + 1, M, stride=2), :], axis=1, keepdims=True)
        decay_own[g, 0:M, :] = jnp.where(left_half, even, odd)
        decay_own[g, M:8, :] = jnp.zeros((8 - M, L), F32)

    row = lax.broadcasted_iota(jnp.int32, (G, G), 0)
    col = lax.broadcasted_iota(jnp.int32, (G, G), 1)
    causal = row >= col
    lower = jnp.where(causal, 1.0, 0.0).astype(F32)
    log_decay = ld_ref[...]
    cum = lax.dot_general(
        log_decay, lower, (((1,), (1,)), ((), ())), precision=HIGHEST, preferred_element_type=F32
    )
    cum_t = lax.dot_general(
        lower, log_decay, (((1,), (1,)), ((), ())), precision=HIGHEST, preferred_element_type=F32
    )
    loads[1].wait()
    keys = kq_ref[:, :N]
    queries = kq_ref[:, N:]
    keys_t = keys.T
    loads[2].wait()

    def state_of(i):
        first, count = CHUNKS[i]
        state = buffers[i][0]
        for g in range(NY):
            for m in range(count):
                j = g * M + first + m
                lanes = slice(j * L, (j + 1) * L)
                level = jnp.where(
                    left_half, cum_t[:, 2 * j : 2 * j + 1], cum_t[:, 2 * j + 1 : 2 * j + 2]
                )
                grow[j] = level
                weight = jnp.exp(level[G - 1 : G, :] - level)
                weighted = (v_ref[:, lanes].astype(F32) * weight).astype(BF16)
                value = jnp.dot(keys_t, weighted, preferred_element_type=F32).astype(BF16)
                for half in range(NC):
                    to = jnp.where(c == half, c, 2)
                    for b in range(NZ):
                        at_row = half * 64 + b * 8
                        state[to, g, b, m * 8 : m * 8 + 8, :] = value[at_row : at_row + 8, :]

    def send_half(i):
        state = buffers[i][0]
        return push(state.at[2], state.at[c], pair_s.at[i], pair_r.at[i], to_pair)

    def inside(g):
        scores = lax.dot_general(
            queries, keys, (((1,), (1,)), ((), ())), preferred_element_type=F32
        )
        scores = jnp.where(causal, scores, 0.0)
        for m in range(M):
            j = g * M + m
            lanes = slice(j * L, (j + 1) * L)
            parts = []
            for h in (2 * j, 2 * j + 1):
                gap = jnp.minimum(cum_t[:, h : h + 1] - cum[h : h + 1, :], 0.0)
                parts.append((scores * jnp.exp(gap)).astype(BF16))
            value = v_ref[:, lanes]
            zero = jnp.zeros_like(value)
            stacked = jnp.concatenate(
                [jnp.where(left_half, value, zero), jnp.where(left_half, zero, value)], axis=0
            )
            diagonal = jnp.dot(
                jnp.concatenate(parts, axis=1), stacked, preferred_element_type=F32
            )
            direct = jnp.where(left_half, skip_ref[2 * j], skip_ref[2 * j + 1])
            result = diagonal + direct * value.astype(F32)
            local_out[j] = result
            pool_local[j : j + 1, :] = jnp.sum(result, axis=0, keepdims=True)
            grow[j] = jnp.exp(grow[j])

    pool_local[TILES:32, :] = jnp.zeros((32 - TILES, L), F32)
    state_of(0)
    pl.semaphore_wait(barrier, len(partners))
    pair_decay = push(decay_own, decay_pair, small_s.at[0], small_r.at[0], to_pair)
    pair_copies = [send_half(0)]
    for i in range(1, NCH):
        state_of(i)
        pair_copies.append(send_half(i))
    response[0] = lax.dot_general(
        jnp.exp(cum_t), queries.astype(F32), (((0,), (0,)), ((), ())),
        precision=HIGHEST, preferred_element_type=F32,
    )
    response[1] = jnp.broadcast_to(jnp.sum(log_decay, axis=1, keepdims=True), (HEADS, L))
    pair_response = push(response, response_pair, small_s.at[1], small_r.at[1], to_pair)
    table_copies = [
        push(cls_ref, table.at[x], table_s.at[k], table_r.at[k], to_x[k]) for k in range(1, NX)
    ]
    inside(0)

    pair_decay.wait_recv()
    for g in range(NY):
        mine, theirs = decay_own[g], decay_pair[g]
        decay_chip[g] = mine + theirs
        pair_factor[g] = spread(jnp.exp(jnp.where(c == 0, theirs, mine)))
        start_factor[g] = spread(jnp.exp(jnp.where(c == 0, mine, theirs)))
    plane_decays = [
        push(decay_chip.at[ys[k]], decay_plane.at[y], small_s.at[1 + k], small_r.at[1 + k], to_y[k])
        for k in FAR_Y
    ]
    decay_plane[y] = decay_chip[y]

    plane_copies = [[] for _ in CHUNKS]
    for i, (first, count) in enumerate(CHUNKS):
        state, pair_total, plane_recv = buffers[i][:3]
        rows = slice(first * 8, (first + count) * 8)
        pair_copies[i].wait_recv()
        for k in (*FAR_Y, 0):
            g = ys[k]

            @pl.loop(0, NZ)
            def _(b, g=g, k=k):
                total = pair_factor[g, rows, :] * state[0, g, b].astype(F32) + state[1, g, b].astype(F32)
                if k == 0:
                    plane_recv[y, b] = total.astype(BF16)
                else:
                    pair_total[k, b] = total.astype(BF16)

            if k:
                plane_copies[i].append(
                    push(pair_total.at[k], plane_recv.at[y], plane_s.at[i, k], plane_r.at[i, k], to_y[k])
                )

    inside(1)
    for copy in plane_decays:
        copy.wait_recv()
    run = jnp.zeros((8, L), F32)
    for k in range(NY):
        plane_factor[k] = spread(jnp.exp(decay_plane[k]))
        plane_start[k] = spread(jnp.exp(run))
        run = run + decay_plane[k]
    decay_sum[...] = run
    decay_axis[z] = run
    axis_decays = [
        push(decay_sum, decay_axis.at[z], small_s.at[4 + k], small_r.at[4 + k], to_z[k])
        for k in FAR_Z
    ]
    inside(2)

    axis_copies = [[] for _ in CHUNKS]
    for i, (first, count) in enumerate(CHUNKS):
        plane_recv, plane_prefix, axis_send, axis_recv = buffers[i][2:6]
        rows = slice(first * 8, (first + count) * 8)
        for copy in plane_copies[i]:
            copy.wait_recv()
        for k in (*FAR_Z, 0):
            b = zs[k]
            total = jnp.zeros((count * 8, L), F32)
            for q in range(NY):
                plane_prefix[q, b] = total
                total = plane_factor[q, rows, :] * total + plane_recv[q, b].astype(F32)
            if k == 0:
                axis_recv[z] = total.astype(BF16)
            else:
                axis_send[k] = total.astype(BF16)
                axis_copies[i].append(
                    push(axis_send.at[k], axis_recv.at[z], axis_s.at[i, k], axis_r.at[i, k], to_z[k])
                )
    inside(3)
    for copy in axis_decays:
        copy.wait_recv()
    for q in range(NZ):
        axis_factor[q] = spread(jnp.exp(decay_axis[q]))
    pair_response.wait_recv()
    resp_0 = jnp.where(c == 0, response[0], response_pair[0])
    resp_1 = jnp.where(c == 0, response_pair[0], response[0])
    resp_0 = resp_0 + jnp.exp(jnp.where(c == 0, response[1], response_pair[1])) * resp_1
    turned_0, turned_1 = pltpu.roll(resp_0, 64, 1), pltpu.roll(resp_1, 64, 1)
    both = jnp.where(
        c == 0, jnp.where(left_half, resp_0, turned_1), jnp.where(left_half, turned_0, resp_1)
    )
    both_high = both.astype(BF16)
    both_low = (both - both_high.astype(F32)).astype(BF16)
    half_queries = jnp.where(
        c == 0, queries.astype(F32), pltpu.roll(queries.astype(F32), 64, 1)
    ).astype(BF16)

    back_copies = [[] for _ in CHUNKS]
    for i, (first, count) in enumerate(CHUNKS):
        axis_recv, axis_prefix, start_plane = buffers[i][5:8]
        rows = slice(first * 8, (first + count) * 8)
        for copy in axis_copies[i]:
            copy.wait_recv()
        total = jnp.zeros((count * 8, L), F32)
        for q in range(NZ):
            axis_prefix[q] = total.astype(BF16)
            if q < NZ - 1:
                total = axis_factor[q, rows, :] * total + axis_recv[q].astype(F32)
        back_copies[i] = [
            push(axis_prefix.at[zs[k]], start_plane.at[z], back_s.at[i, k], back_r.at[i, k], to_z[k])
            for k in FAR_Z
        ]
        start_plane[z] = axis_prefix[z]

    chip_copies = [[] for _ in CHUNKS]
    for i, (first, count) in enumerate(CHUNKS):
        plane_prefix = buffers[i][3]
        start_plane, start_send, start_chip = buffers[i][7:10]
        rows = slice(first * 8, (first + count) * 8)
        for copy in back_copies[i]:
            copy.wait_recv()
        for k in (*FAR_Y, 0):
            g = ys[k]

            @pl.loop(0, NZ)
            def _(b, g=g, k=k):
                start = plane_start[g, rows, :] * start_plane[b].astype(F32) + plane_prefix[g, b]
                if k == 0:
                    start_chip[y, b] = start.astype(BF16)
                else:
                    start_send[k, b] = start.astype(BF16)

            if k:
                chip_copies[i].append(
                    push(start_send.at[k], start_chip.at[y], plane_s.at[i, 3 + k], plane_r.at[i, 3 + k], to_y[k])
                )

    half_copies = []
    for i, (first, count) in enumerate(CHUNKS):
        state = buffers[i][0]
        start_chip, carried, carried_recv = buffers[i][9:12]
        rows = slice(first * 8, (first + count) * 8)
        for copy in chip_copies[i]:
            copy.wait_recv()

        @pl.loop(0, NY)
        def _(g):
            @pl.loop(0, NZ)
            def _(b):
                before = start_chip[g, b].astype(F32)
                after = start_factor[g, rows, :] * before + state[0, g, b].astype(F32)
                carried[0, g, b] = start_chip[g, b]
                carried[1, g, b] = after.astype(BF16)

        half_copies.append(
            push(carried.at[other], carried_recv, pair_s.at[NCH + i], pair_r.at[NCH + i], to_pair)
        )
        for g in range(NY):
            for m in range(count):
                j = g * M + first + m
                tile = slice(m * 8, m * 8 + 8)
                start = jnp.concatenate(
                    [start_chip[g, b, tile, :] for b in range(NZ)]
                    + [state[0, g, b, tile, :] for b in range(NZ)],
                    axis=0,
                )
                added = jnp.dot(both_high, start, preferred_element_type=F32) + jnp.dot(
                    both_low, start, preferred_element_type=F32
                )
                pool_own[j : j + 1, :] = pool_local[j : j + 1, :] + jnp.where(
                    left_half, added[2 * j : 2 * j + 1, :], added[2 * j + 1 : 2 * j + 2, :]
                )

    pool_own[TILES:32, :] = pool_local[TILES:32, :]
    pool_plane[y * NC + c] = pool_own[...]
    mine = pool_plane.at[y * NC + c]
    pool_copies = (
        [push(pool_own, mine, small_s.at[11 + k], small_r.at[11 + k], to_y[k]) for k in FAR_Y]
        + [push(pool_own, mine, small_s.at[14 + k], small_r.at[14 + k], to_y_other[k]) for k in FAR_Y]
        + [push(pool_own, mine, small_s.at[18], small_r.at[18], to_pair)]
    )

    stores = []

    def final(i):
        first, count = CHUNKS[i]
        carried, carried_recv = buffers[i][10:12]
        half_copies[i].wait_recv()
        for g in range(NY):
            for m in range(count):
                j = g * M + first + m
                lanes = slice(j * L, (j + 1) * L)
                tile = slice(m * 8, m * 8 + 8)
                start = jnp.concatenate(
                    [carried[c, g, b, tile, :] for b in range(NZ)]
                    + [carried_recv[g, b, tile, :] for b in range(NZ)],
                    axis=0,
                )
                full = local_out[j] + grow[j] * jnp.dot(
                    half_queries, start, preferred_element_type=F32
                )
                out_ref[:, lanes] = full.astype(BF16)
            lanes = slice((g * M + first) * L, (g * M + first + count) * L)
            store = pltpu.make_async_copy(
                out_ref.at[:, lanes], mixed_ref.at[:, lanes], out_s.at[i * NY + g]
            )
            store.start()
            stores.append(store)

    def sum_plane():
        for copy in pool_copies:
            copy.wait_recv()
        total = pool_plane[0]
        for q in range(1, NY * NC):
            total = total + pool_plane[q]
        pool_sum[...] = total
        pool_axis[z] = total
        return [
            push(pool_sum, pool_axis.at[z], small_s.at[18 + k], small_r.at[18 + k], to_z[k])
            for k in FAR_Z
        ]

    if NCH == 1:
        last_copies = sum_plane()
        final(0)
    else:
        final(0)
        last_copies = sum_plane()
        for i in range(1, NCH):
            final(i)

    for copy in table_copies:
        copy.wait_recv()
    loads[3].wait()
    for copy in last_copies:
        copy.wait_recv()
    pooled = pool_axis[0]
    for q in range(1, NZ):
        pooled = pooled + pool_axis[q]
    pooled = pooled / (G * NZ * NY * NC)
    square = jnp.sum(pooled * pooled, keepdims=True) / (TILES * L)
    normed = (pooled / jnp.sqrt(square + EPS)).astype(BF16)
    wide = jnp.concatenate(
        [jnp.broadcast_to(normed[j : j + 1, :], (16, L)) for j in range(TILES)], axis=1
    )
    classifier = table[...].reshape(TILES * L, L)
    logits = jnp.dot(wide, classifier, preferred_element_type=F32)
    logits_ref[...] = logits[0:1, :]

    for store in stores:
        store.wait()
    for copy in sends:
        copy.wait_send()


def local(inputs, keys_queries, log_decay, skip, classifier):
    copies, positions, channels = inputs.shape
    heads = log_decay.shape[1]
    hbm = pl.BlockSpec(memory_space=pltpu.HBM)

    def chunk(count):
        slab = (NZ, count * 8, L)
        return [
            pltpu.VMEM((3, NY, *slab), BF16),
            pltpu.VMEM((NY, *slab), BF16),
            pltpu.VMEM((NY, *slab), BF16),
            pltpu.VMEM((NY, *slab), F32),
            pltpu.VMEM(slab, BF16),
            pltpu.VMEM(slab, BF16),
            pltpu.VMEM(slab, BF16),
            pltpu.VMEM(slab, BF16),
            pltpu.VMEM((NY, *slab), BF16),
            pltpu.VMEM((NY, *slab), BF16),
            pltpu.VMEM((NC, NY, *slab), BF16),
            pltpu.VMEM((NY, *slab), BF16),
        ]

    dma = pltpu.SemaphoreType.DMA
    scratch = [
        pltpu.VMEM((positions, channels), BF16),
        pltpu.VMEM((positions, 2 * N), BF16),
        pltpu.VMEM((heads, positions), F32),
        pltpu.VMEM((positions, channels), BF16),
        pltpu.VMEM((TILES, G, L), F32),
        pltpu.VMEM((TILES, G, L), F32),
        pltpu.VMEM((NX, *classifier.shape), BF16),
        pltpu.VMEM((NY, 8, L), F32),
        pltpu.VMEM((NY, 8, L), F32),
        pltpu.VMEM((NY, 8, L), F32),
        pltpu.VMEM((NY, 8, L), F32),
        pltpu.VMEM((8, L), F32),
        pltpu.VMEM((NZ, 8, L), F32),
        pltpu.VMEM((NY, M * 8, L), F32),
        pltpu.VMEM((NY, M * 8, L), F32),
        pltpu.VMEM((NY, M * 8, L), F32),
        pltpu.VMEM((NY, M * 8, L), F32),
        pltpu.VMEM((NZ, M * 8, L), F32),
        pltpu.VMEM((2, HEADS, L), F32),
        pltpu.VMEM((2, HEADS, L), F32),
        pltpu.VMEM((32, L), F32),
        pltpu.VMEM((32, L), F32),
        pltpu.VMEM((NY * NC, 32, L), F32),
        pltpu.VMEM((32, L), F32),
        pltpu.VMEM((NZ, 32, L), F32),
        *[ref for _, count in CHUNKS for ref in chunk(count)],
        dma((4,)), dma((NCH * NY,)),
        dma((2 * NCH,)), dma((2 * NCH,)), dma((NCH, 7)), dma((NCH, 7)),
        dma((NCH, NZ)), dma((NCH, NZ)), dma((NCH, NZ)), dma((NCH, NZ)),
        dma((NX,)), dma((NX,)), dma((26,)), dma((26,)),
    ]
    mixed, logits = pl.pallas_call(
        kernel,
        out_shape=(
            jax.ShapeDtypeStruct((positions, channels), BF16),
            jax.ShapeDtypeStruct((1, classifier.shape[1]), F32),
        ),
        in_specs=[hbm, hbm, hbm, pl.BlockSpec(memory_space=pltpu.SMEM), hbm],
        out_specs=(hbm, pl.BlockSpec(memory_space=pltpu.VMEM)),
        scratch_shapes=scratch,
        compiler_params=pltpu.CompilerParams(
            collective_id=0, has_side_effects=True, vmem_limit_bytes=60 << 20
        ),
    )(
        inputs.reshape(positions, channels),
        keys_queries.reshape(positions, 2 * N),
        log_decay.reshape(heads, positions),
        skip,
        classifier,
    )
    return mixed.reshape(copies, positions, channels), logits


def solution(mesh):
    return jax.shard_map(
        local,
        mesh=mesh,
        in_specs=(
            P("fsdp", "seq", None),
            P("fsdp", "seq", None),
            P("fsdp", None, "seq"),
            P(),
            P("fsdp", None),
        ),
        out_specs=(P("fsdp", "seq", None), P("fsdp", None)),
        check_vma=False,
    )
```

```python
import jax
import jax.numpy as jnp
from jax import lax
from jax.experimental import pallas as pl
from jax.experimental.pallas import tpu as pltpu
from jax.sharding import PartitionSpec as P

MESH = pl.DeviceIdType.MESH
F32, BF16 = jnp.float32, jnp.bfloat16
HIGHEST = lax.Precision.HIGHEST

N = 128
G = 128
L = 128
NZ, NY, NC, NX = 8, 4, 2, 4
HEADS = 56
TILES = 28
M = TILES // NY
CHUNKS = ((0, 4), (4, 3))
NCH = len(CHUNKS)
EPS = 1e-06
FAR_Y = (2, 1, 3)
FAR_Z = (4, 5, 3, 6, 2, 7, 1)


def spread(x):
    return jnp.concatenate(
        [jnp.broadcast_to(x[m : m + 1, :], (8, L)) for m in range(M)], axis=0
    )


def kernel(
    v_hbm, kq_hbm, ld_hbm, skip_ref, cls_ref, mixed_ref, logits_ref,
    v_ref, kq_ref, ld_ref, out_ref, grow, local_out, table,
    decay_own, decay_pair, decay_chip, decay_plane,
    pair_factor, start_factor, plane_factor, plane_start, axis_factor,
    response, response_pair, chip_response, plane_response, axis_note, axis_notes,
    pool_own, pool_parts, pool_send, pool_axis, pool_sum, pool_plane,
    *rest,
):
    buffers = [rest[i * 12 : (i + 1) * 12] for i in range(NCH)]
    (in_s, out_s, pair_s, pair_r, plane_s, plane_r, axis_s, axis_r,
     back_s, back_r, table_s, table_r, small_s, small_r) = rest[NCH * 12 :]
    me, x = lax.axis_index("seq"), lax.axis_index("fsdp")
    c = lax.rem(me, NC)
    y = lax.rem(me // NC, NY)
    z = me // (NC * NY)
    other = 1 - c
    ys = [lax.rem(y + k, NY) for k in range(NY)]
    zs = [lax.rem(z + k, NZ) for k in range(NZ)]

    def at(z_, y_, c_):
        return {"seq": (z_ * NY + y_) * NC + c_}

    to_pair = at(z, y, other)
    to_y = [at(z, ys[k], c) for k in range(NY)]
    to_y_other = [at(z, ys[k], other) for k in range(NY)]
    to_z = [at(zs[k], y, c) for k in range(NZ)]
    to_x = [{"fsdp": lax.rem(x + k, NX)} for k in range(NX)]

    barrier = pltpu.get_barrier_semaphore()
    partners = to_z[1:] + to_y[1:] + to_y_other[1:] + to_x[1:] + [to_pair]
    for who in partners:
        pl.semaphore_signal(barrier, inc=1, device_id=who, device_id_type=MESH)

    loads = [
        pltpu.make_async_copy(src, dst, in_s.at[i])
        for i, (src, dst) in enumerate(
            ((ld_hbm, ld_ref), (kq_hbm, kq_ref), (v_hbm, v_ref), (cls_ref, table.at[x]))
        )
    ]
    for load in loads:
        load.start()

    sends = []

    def push(src, dst, send, recv, who):
        copy = pltpu.make_async_remote_copy(
            src_ref=src, dst_ref=dst, send_sem=send, recv_sem=recv,
            device_id=who, device_id_type=MESH,
        )
        copy.start()
        sends.append(copy)
        return copy

    loads[0].wait()
    left_half = lax.broadcasted_iota(jnp.int32, (1, L), 1) < 64
    for g in range(NY):
        even = jnp.sum(ld_ref[pl.ds(2 * M * g, M, stride=2), :], axis=1, keepdims=True)
        odd = jnp.sum(ld_ref[pl.ds(2 * M * g + 1, M, stride=2), :], axis=1, keepdims=True)
        decay_own[g, 0:M, :] = jnp.where(left_half, even, odd)
        decay_own[g, M:8, :] = jnp.zeros((8 - M, L), F32)

    row = lax.broadcasted_iota(jnp.int32, (G, G), 0)
    col = lax.broadcasted_iota(jnp.int32, (G, G), 1)
    causal = row >= col
    lower = jnp.where(causal, 1.0, 0.0).astype(F32)
    log_decay = ld_ref[...]
    cum = lax.dot_general(
        log_decay, lower, (((1,), (1,)), ((), ())), precision=HIGHEST, preferred_element_type=F32
    )
    cum_t = lax.dot_general(
        lower, log_decay, (((1,), (1,)), ((), ())), precision=HIGHEST, preferred_element_type=F32
    )
    loads[1].wait()
    keys = kq_ref[:, :N]
    queries = kq_ref[:, N:]
    keys_t = keys.T
    loads[2].wait()

    def pool_rows(responses, parts, first, count):
        whole = jnp.concatenate(responses, axis=1)
        high = whole.astype(BF16)
        low = (whole - high.astype(F32)).astype(BF16)
        both = jnp.concatenate([high, low], axis=0)
        made = []
        for m in range(count):
            t = 2 * (first + m)
            added = jnp.dot(both, jnp.concatenate(parts(m), axis=0), preferred_element_type=F32)
            added = added[0 : 2 * M, :] + added[2 * M : 4 * M, :]
            made.append(jnp.where(left_half, added[t : t + 1, :], added[t + 1 : t + 2, :]))
        return jnp.concatenate(made, axis=0)

    def state_of(i):
        first, count = CHUNKS[i]
        state = buffers[i][0]
        for g in range(NY):
            for m in range(count):
                j = g * M + first + m
                lanes = slice(j * L, (j + 1) * L)
                level = jnp.where(
                    left_half, cum_t[:, 2 * j : 2 * j + 1], cum_t[:, 2 * j + 1 : 2 * j + 2]
                )
                grow[j] = level
                weight = jnp.exp(level[G - 1 : G, :] - level)
                weighted = (v_ref[:, lanes].astype(F32) * weight).astype(BF16)
                value = jnp.dot(keys_t, weighted, preferred_element_type=F32).astype(BF16)
                for half in range(NC):
                    to = jnp.where(c == half, c, 2)
                    for b in range(NZ):
                        at_row = half * 64 + b * 8
                        state[to, g, b, m * 8 : m * 8 + 8, :] = value[at_row : at_row + 8, :]

    def send_half(i):
        state = buffers[i][0]
        return push(state.at[2], state.at[c], pair_s.at[i], pair_r.at[i], to_pair)

    def inside(g):
        scores = lax.dot_general(
            queries, keys, (((1,), (1,)), ((), ())), preferred_element_type=F32
        )
        scores = jnp.where(causal, scores, 0.0)
        for m in range(M):
            j = g * M + m
            lanes = slice(j * L, (j + 1) * L)
            parts = []
            for h in (2 * j, 2 * j + 1):
                gap = jnp.minimum(cum_t[:, h : h + 1] - cum[h : h + 1, :], 0.0)
                parts.append((scores * jnp.exp(gap)).astype(BF16))
            value = v_ref[:, lanes]
            zero = jnp.zeros_like(value)
            stacked = jnp.concatenate(
                [jnp.where(left_half, value, zero), jnp.where(left_half, zero, value)], axis=0
            )
            diagonal = jnp.dot(
                jnp.concatenate(parts, axis=1), stacked, preferred_element_type=F32
            )
            direct = jnp.where(left_half, skip_ref[2 * j], skip_ref[2 * j + 1])
            result = diagonal + direct * value.astype(F32)
            local_out[j] = result
            pool_own[g, m : m + 1, :] = jnp.sum(result, axis=0, keepdims=True)
            grow[j] = jnp.exp(grow[j])

    for g in range(NY):
        pool_own[g, M:8, :] = jnp.zeros((8 - M, L), F32)
    state_of(0)
    pl.semaphore_wait(barrier, len(partners))
    pair_decay = push(decay_own, decay_pair, small_s.at[0], small_r.at[0], to_pair)
    pair_copies = [send_half(0)]
    for i in range(1, NCH):
        state_of(i)
        pair_copies.append(send_half(i))
    response[0] = lax.dot_general(
        jnp.exp(cum_t), queries.astype(F32), (((0,), (0,)), ((), ())),
        precision=HIGHEST, preferred_element_type=F32,
    )
    response[1] = jnp.broadcast_to(jnp.sum(log_decay, axis=1, keepdims=True), (HEADS, L))
    pair_response = push(response, response_pair, small_s.at[1], small_r.at[1], to_pair)
    table_copies = [
        push(cls_ref, table.at[x], table_s.at[k], table_r.at[k], to_x[k]) for k in range(1, NX)
    ]
    inside(0)

    pair_decay.wait_recv()
    for g in range(NY):
        mine, theirs = decay_own[g], decay_pair[g]
        decay_chip[g] = mine + theirs
        pair_factor[g] = spread(jnp.exp(jnp.where(c == 0, theirs, mine)))
        start_factor[g] = spread(jnp.exp(jnp.where(c == 0, mine, theirs)))
    plane_decays = [
        push(decay_chip.at[ys[k]], decay_plane.at[y], small_s.at[1 + k], small_r.at[1 + k], to_y[k])
        for k in FAR_Y
    ]
    decay_plane[y] = decay_chip[y]

    plane_copies = [[] for _ in CHUNKS]
    for i, (first, count) in enumerate(CHUNKS):
        state, pair_total, plane_recv = buffers[i][:3]
        rows = slice(first * 8, (first + count) * 8)
        pair_copies[i].wait_recv()
        for k in (*FAR_Y, 0):
            g = ys[k]

            @pl.loop(0, NZ)
            def _(b, g=g, k=k):
                total = pair_factor[g, rows, :] * state[0, g, b].astype(F32) + state[1, g, b].astype(F32)
                if k == 0:
                    plane_recv[y, b] = total.astype(BF16)
                else:
                    pair_total[k, b] = total.astype(BF16)

            if k:
                plane_copies[i].append(
                    push(pair_total.at[k], plane_recv.at[y], plane_s.at[i, k], plane_r.at[i, k], to_y[k])
                )

    pair_response.wait_recv()
    resp_0 = jnp.where(c == 0, response[0], response_pair[0])
    resp_1 = jnp.where(c == 0, response_pair[0], response[0])
    resp_0 = resp_0 + jnp.exp(jnp.where(c == 0, response[1], response_pair[1])) * resp_1
    chip_decay = response[1] + response_pair[1]
    for g in range(NY):
        heads = slice(2 * M * g, 2 * M * (g + 1))
        chip_response[g, 0, 0 : 2 * M, :] = resp_0[heads, :]
        chip_response[g, 1, 0 : 2 * M, :] = chip_decay[heads, :]
        chip_response[g, :, 2 * M : 16, :] = jnp.zeros((2, 16 - 2 * M, L), F32)
    plane_responses = [
        push(chip_response.at[ys[k]], plane_response.at[y], small_s.at[4 + k], small_r.at[4 + k], to_y[k])
        for k in FAR_Y
    ]
    plane_response[y] = chip_response[y]
    inside(1)
    for copy in (*plane_decays, *plane_responses):
        copy.wait_recv()
    run = jnp.zeros((8, L), F32)
    run_head = jnp.zeros((16, L), F32)
    summed = jnp.zeros((16, L), F32)
    for k in range(NY):
        plane_factor[k] = spread(jnp.exp(decay_plane[k]))
        plane_start[k] = spread(jnp.exp(run))
        run = run + decay_plane[k]
        summed = summed + jnp.exp(run_head) * plane_response[k, 0]
        run_head = run_head + plane_response[k, 1]
    axis_note[0:8, :] = run
    axis_note[8:24, :] = summed
    axis_notes[z, 0:8, :] = run
    axis_notes[z, 8:24, :] = summed
    note_copies = [
        push(axis_note, axis_notes.at[z], small_s.at[7 + k], small_r.at[7 + k], to_z[k])
        for k in FAR_Z
    ]
    inside(2)
    inside(3)
    mine_1 = jnp.where(c == 0, resp_1, pltpu.roll(resp_1, 64, 1))
    for i, (first, count) in enumerate(CHUNKS):
        state = buffers[i][0]
        for g in range(NY):
            group = pool_rows(
                [mine_1[2 * M * g : 2 * M * (g + 1), 0:64]],
                lambda m, g=g, state=state: [state[0, g, b, m * 8 : m * 8 + 8, :] for b in range(NZ)],
                first, count,
            )
            tiles = slice(first, first + count)
            pool_own[g, tiles, :] = pool_own[g, tiles, :] + group
    part_copies = [
        push(pool_own.at[ys[k]], pool_parts.at[y], small_s.at[14 + k], small_r.at[14 + k], to_y[k])
        for k in FAR_Y
    ]
    pool_parts[y] = pool_own[y]

    axis_copies = [[] for _ in CHUNKS]
    for i, (first, count) in enumerate(CHUNKS):
        plane_recv, plane_prefix, axis_send, axis_recv = buffers[i][2:6]
        rows = slice(first * 8, (first + count) * 8)
        for copy in plane_copies[i]:
            copy.wait_recv()
        for k in (*FAR_Z, 0):
            b = zs[k]
            total = jnp.zeros((count * 8, L), F32)
            for q in range(NY):
                plane_prefix[q, b] = total
                total = plane_factor[q, rows, :] * total + plane_recv[q, b].astype(F32)
            if k == 0:
                axis_recv[z] = total.astype(BF16)
            else:
                axis_send[k] = total.astype(BF16)
                axis_copies[i].append(
                    push(axis_send.at[k], axis_recv.at[z], axis_s.at[i, k], axis_r.at[i, k], to_z[k])
                )
    for copy in part_copies:
        copy.wait_recv()
    my_half = [
        jnp.where(c == 0, plane_response[q, 0], pltpu.roll(plane_response[q, 0], 64, 1))[0 : 2 * M, 0:64]
        for q in range(1, NY)
    ]
    pool_rest = (pool_parts[0] + pool_parts[1]) + (pool_parts[2] + pool_parts[3])
    pool_tiles = []
    for i, (first, count) in enumerate(CHUNKS):
        plane_prefix = buffers[i][3]
        pool_tiles.append(
            pool_rows(
                my_half,
                lambda m, plane_prefix=plane_prefix: [
                    plane_prefix[q, b, m * 8 : m * 8 + 8, :].astype(BF16)
                    for q in range(1, NY)
                    for b in range(NZ)
                ],
                first, count,
            )
        )
    for copy in note_copies:
        copy.wait_recv()
    lane = lax.broadcasted_iota(jnp.int32, (16, L), 1) // 8
    my_rows = jnp.zeros((16, L), F32)
    for q in range(NZ):
        axis_factor[q] = spread(jnp.exp(axis_notes[q, 0:8, :]))
        turned = pltpu.roll(axis_notes[q, 8:24, :], lax.rem(2 * L + 8 * q - 64 * c - 8 * z, L), 1)
        my_rows = my_rows + jnp.where(lane == q, turned, 0.0)
    half_queries = jnp.where(
        c == 0, queries.astype(F32), pltpu.roll(queries.astype(F32), 64, 1)
    ).astype(BF16)

    back_copies = [[] for _ in CHUNKS]
    for i, (first, count) in enumerate(CHUNKS):
        axis_recv, axis_prefix, start_plane = buffers[i][5:8]
        rows = slice(first * 8, (first + count) * 8)
        for copy in axis_copies[i]:
            copy.wait_recv()
        total = jnp.zeros((count * 8, L), F32)
        for q in range(NZ):
            axis_prefix[q] = total.astype(BF16)
            if q < NZ - 1:
                total = axis_factor[q, rows, :] * total + axis_recv[q].astype(F32)
        back_copies[i] = [
            push(axis_prefix.at[zs[k]], start_plane.at[z], back_s.at[i, k], back_r.at[i, k], to_z[k])
            for k in FAR_Z
        ]
        start_plane[z] = axis_prefix[z]
    for i, (first, count) in enumerate(CHUNKS):
        axis_prefix = buffers[i][6]
        pool_tiles[i] = pool_tiles[i] + pool_rows(
            [my_rows[0 : 2 * M, 0:64]],
            lambda m, axis_prefix=axis_prefix: [
                axis_prefix[q, m * 8 : m * 8 + 8, :] for q in range(NZ)
            ],
            first, count,
        )
    pool_send[...] = pool_rest + jnp.concatenate(
        [*pool_tiles, jnp.zeros((8 - M, L), F32)], axis=0
    )
    pool_axis[z] = pool_send[...]
    pool_copies = [
        push(pool_send, pool_axis.at[z], small_s.at[17 + k], small_r.at[17 + k], to_z[k])
        for k in FAR_Z
    ]

    chip_copies = [[] for _ in CHUNKS]
    for i, (first, count) in enumerate(CHUNKS):
        plane_prefix = buffers[i][3]
        start_plane, start_send, start_chip = buffers[i][7:10]
        rows = slice(first * 8, (first + count) * 8)
        for copy in back_copies[i]:
            copy.wait_recv()
        for k in (*FAR_Y, 0):
            g = ys[k]

            @pl.loop(0, NZ)
            def _(b, g=g, k=k):
                start = plane_start[g, rows, :] * start_plane[b].astype(F32) + plane_prefix[g, b]
                if k == 0:
                    start_chip[y, b] = start.astype(BF16)
                else:
                    start_send[k, b] = start.astype(BF16)

            if k:
                chip_copies[i].append(
                    push(start_send.at[k], start_chip.at[y], plane_s.at[i, 3 + k], plane_r.at[i, 3 + k], to_y[k])
                )

    for copy in pool_copies:
        copy.wait_recv()
    total = pool_axis[0]
    for q in range(1, NZ):
        total = total + pool_axis[q]
    pool_sum[...] = total
    mine = pool_plane.at[y * NC + c]
    pool_plane[y * NC + c] = total
    last_copies = (
        [push(pool_sum, mine, small_s.at[24 + k], small_r.at[24 + k], to_y[k]) for k in FAR_Y]
        + [push(pool_sum, mine, small_s.at[27 + k], small_r.at[27 + k], to_y_other[k]) for k in FAR_Y]
        + [push(pool_sum, mine, small_s.at[31], small_r.at[31], to_pair)]
    )

    half_copies = []
    for i, (first, count) in enumerate(CHUNKS):
        state = buffers[i][0]
        start_chip, carried, carried_recv = buffers[i][9:12]
        rows = slice(first * 8, (first + count) * 8)
        for copy in chip_copies[i]:
            copy.wait_recv()

        @pl.loop(0, NY)
        def _(g):
            @pl.loop(0, NZ)
            def _(b):
                before = start_chip[g, b].astype(F32)
                after = start_factor[g, rows, :] * before + state[0, g, b].astype(F32)
                carried[0, g, b] = start_chip[g, b]
                carried[1, g, b] = after.astype(BF16)

        half_copies.append(
            push(carried.at[other], carried_recv, pair_s.at[NCH + i], pair_r.at[NCH + i], to_pair)
        )

    for copy in table_copies:
        copy.wait_recv()
    loads[3].wait()
    for copy in last_copies:
        copy.wait_recv()
    pooled = [
        (pool_plane[NC * g] + pool_plane[NC * g + 1]) / (G * NZ * NY * NC) for g in range(NY)
    ]
    square = sum(jnp.sum(p * p, keepdims=True) for p in pooled) / (TILES * L)
    scale = 1.0 / jnp.sqrt(square + EPS)
    wide = jnp.concatenate(
        [
            jnp.broadcast_to((pooled[g] * scale)[m : m + 1, :], (16, L)).astype(BF16)
            for g in range(NY)
            for m in range(M)
        ],
        axis=1,
    )
    classifier = table[...].reshape(TILES * L, L)
    logits = jnp.dot(wide, classifier, preferred_element_type=F32)
    logits_ref[...] = logits[0:1, :]

    stores = []

    def final(i):
        first, count = CHUNKS[i]
        carried, carried_recv = buffers[i][10:12]
        half_copies[i].wait_recv()
        for g in range(NY):
            for m in range(count):
                j = g * M + first + m
                lanes = slice(j * L, (j + 1) * L)
                tile = slice(m * 8, m * 8 + 8)
                start = jnp.concatenate(
                    [carried[c, g, b, tile, :] for b in range(NZ)]
                    + [carried_recv[g, b, tile, :] for b in range(NZ)],
                    axis=0,
                )
                full = local_out[j] + grow[j] * jnp.dot(
                    half_queries, start, preferred_element_type=F32
                )
                out_ref[:, lanes] = full.astype(BF16)
            lanes = slice((g * M + first) * L, (g * M + first + count) * L)
            store = pltpu.make_async_copy(
                out_ref.at[:, lanes], mixed_ref.at[:, lanes], out_s.at[i * NY + g]
            )
            store.start()
            stores.append(store)

    for i in range(NCH):
        final(i)

    for store in stores:
        store.wait()
    for copy in sends:
        copy.wait_send()


def local(inputs, keys_queries, log_decay, skip, classifier):
    copies, positions, channels = inputs.shape
    heads = log_decay.shape[1]
    hbm = pl.BlockSpec(memory_space=pltpu.HBM)

    def chunk(count):
        slab = (NZ, count * 8, L)
        return [
            pltpu.VMEM((3, NY, *slab), BF16),
            pltpu.VMEM((NY, *slab), BF16),
            pltpu.VMEM((NY, *slab), BF16),
            pltpu.VMEM((NY, *slab), F32),
            pltpu.VMEM(slab, BF16),
            pltpu.VMEM(slab, BF16),
            pltpu.VMEM(slab, BF16),
            pltpu.VMEM(slab, BF16),
            pltpu.VMEM((NY, *slab), BF16),
            pltpu.VMEM((NY, *slab), BF16),
            pltpu.VMEM((NC, NY, *slab), BF16),
            pltpu.VMEM((NY, *slab), BF16),
        ]

    dma = pltpu.SemaphoreType.DMA
    scratch = [
        pltpu.VMEM((positions, channels), BF16),
        pltpu.VMEM((positions, 2 * N), BF16),
        pltpu.VMEM((heads, positions), F32),
        pltpu.VMEM((positions, channels), BF16),
        pltpu.VMEM((TILES, G, L), F32),
        pltpu.VMEM((TILES, G, L), F32),
        pltpu.VMEM((NX, *classifier.shape), BF16),
        pltpu.VMEM((NY, 8, L), F32),
        pltpu.VMEM((NY, 8, L), F32),
        pltpu.VMEM((NY, 8, L), F32),
        pltpu.VMEM((NY, 8, L), F32),
        pltpu.VMEM((NY, M * 8, L), F32),
        pltpu.VMEM((NY, M * 8, L), F32),
        pltpu.VMEM((NY, M * 8, L), F32),
        pltpu.VMEM((NY, M * 8, L), F32),
        pltpu.VMEM((NZ, M * 8, L), F32),
        pltpu.VMEM((2, HEADS, L), F32),
        pltpu.VMEM((2, HEADS, L), F32),
        pltpu.VMEM((NY, 2, 16, L), F32),
        pltpu.VMEM((NY, 2, 16, L), F32),
        pltpu.VMEM((24, L), F32),
        pltpu.VMEM((NZ, 24, L), F32),
        pltpu.VMEM((NY, 8, L), F32),
        pltpu.VMEM((NY, 8, L), F32),
        pltpu.VMEM((8, L), F32),
        pltpu.VMEM((NZ, 8, L), F32),
        pltpu.VMEM((8, L), F32),
        pltpu.VMEM((NY * NC, 8, L), F32),
        *[ref for _, count in CHUNKS for ref in chunk(count)],
        dma((4,)), dma((NCH * NY,)),
        dma((2 * NCH,)), dma((2 * NCH,)), dma((NCH, 7)), dma((NCH, 7)),
        dma((NCH, NZ)), dma((NCH, NZ)), dma((NCH, NZ)), dma((NCH, NZ)),
        dma((NX,)), dma((NX,)), dma((32,)), dma((32,)),
    ]
    mixed, logits = pl.pallas_call(
        kernel,
        out_shape=(
            jax.ShapeDtypeStruct((positions, channels), BF16),
            jax.ShapeDtypeStruct((1, classifier.shape[1]), F32),
        ),
        in_specs=[hbm, hbm, hbm, pl.BlockSpec(memory_space=pltpu.SMEM), hbm],
        out_specs=(hbm, pl.BlockSpec(memory_space=pltpu.VMEM)),
        scratch_shapes=scratch,
        compiler_params=pltpu.CompilerParams(
            collective_id=0, has_side_effects=True, vmem_limit_bytes=60 << 20
        ),
    )(
        inputs.reshape(positions, channels),
        keys_queries.reshape(positions, 2 * N),
        log_decay.reshape(heads, positions),
        skip,
        classifier,
    )
    return mixed.reshape(copies, positions, channels), logits


def solution(mesh):
    return jax.shard_map(
        local,
        mesh=mesh,
        in_specs=(
            P("fsdp", "seq", None),
            P("fsdp", "seq", None),
            P("fsdp", None, "seq"),
            P(),
            P("fsdp", None),
        ),
        out_specs=(P("fsdp", "seq", None), P("fsdp", None)),
        check_vma=False,
    )
```

```python
import jax
import jax.numpy as jnp
from jax import lax
from jax.experimental import pallas as pl
from jax.experimental.pallas import tpu as pltpu
from jax.sharding import PartitionSpec as P

MESH = pl.DeviceIdType.MESH
F32, BF16 = jnp.float32, jnp.bfloat16
HIGHEST = lax.Precision.HIGHEST

N = 128
G = 128
L = 128
NZ, NY, NC, NX = 8, 4, 2, 4
HEADS = 56
TILES = 28
M = TILES // NY
CHUNKS = ((0, 4), (4, 3))
NCH = len(CHUNKS)
EPS = 1e-06
PIECES = 8
FAR_Y = (2, 1, 3)
FAR_Z = (4, 5, 3, 6, 2, 7, 1)


def spread(x):
    return jnp.concatenate(
        [jnp.broadcast_to(x[m : m + 1, :], (8, L)) for m in range(M)], axis=0
    )


def kernel(
    v_hbm, kq_hbm, ld_hbm, skip_ref, cls_ref, mixed_ref, logits_ref,
    v_ref, kq_ref, ld_ref, out_ref, grow, local_out, table,
    decay_own, decay_pair, decay_chip, decay_plane,
    pair_factor, start_factor, plane_factor, plane_start,
    response, response_pair, chip_response, plane_response, axis_note, axis_notes,
    pool_own, pool_parts, pool_send, pool_axis, pool_sum, pool_plane,
    *rest,
):
    buffers = [rest[i * 12 : (i + 1) * 12] for i in range(NCH)]
    (in_s, out_s, pair_s, pair_r, plane_s, plane_r, axis_s, axis_r,
     back_s, back_r, note_s, note_r, table_s, table_r, small_s, small_r) = rest[NCH * 12 :]
    me, x = lax.axis_index("seq"), lax.axis_index("fsdp")
    c = lax.rem(me, NC)
    y = lax.rem(me // NC, NY)
    z = me // (NC * NY)
    other = 1 - c
    ys = [lax.rem(y + k, NY) for k in range(NY)]
    zs = [lax.rem(z + k, NZ) for k in range(NZ)]

    def at(z_, y_, c_):
        return {"seq": (z_ * NY + y_) * NC + c_}

    to_pair = at(z, y, other)
    to_y = [at(z, ys[k], c) for k in range(NY)]
    to_y_other = [at(z, ys[k], other) for k in range(NY)]
    to_z = [at(zs[k], y, c) for k in range(NZ)]
    to_x = [{"fsdp": lax.rem(x + k, NX)} for k in range(NX)]

    barrier = pltpu.get_barrier_semaphore()
    partners = to_z[1:] + to_y[1:] + to_y_other[1:] + to_x[1:] + [to_pair]
    for who in partners:
        pl.semaphore_signal(barrier, inc=1, device_id=who, device_id_type=MESH)

    loads = [
        pltpu.make_async_copy(src, dst, in_s.at[i])
        for i, (src, dst) in enumerate(
            ((ld_hbm, ld_ref), (kq_hbm, kq_ref), (v_hbm, v_ref), (cls_ref, table.at[x]))
        )
    ]
    for load in loads:
        load.start()

    sends = []

    def push(src, dst, send, recv, who):
        copy = pltpu.make_async_remote_copy(
            src_ref=src, dst_ref=dst, send_sem=send, recv_sem=recv,
            device_id=who, device_id_type=MESH,
        )
        copy.start()
        sends.append(copy)
        return copy

    loads[0].wait()
    left_half = lax.broadcasted_iota(jnp.int32, (1, L), 1) < 64
    for g in range(NY):
        even = jnp.sum(ld_ref[pl.ds(2 * M * g, M, stride=2), :], axis=1, keepdims=True)
        odd = jnp.sum(ld_ref[pl.ds(2 * M * g + 1, M, stride=2), :], axis=1, keepdims=True)
        decay_own[g, 0:M, :] = jnp.where(left_half, even, odd)
        decay_own[g, M:8, :] = jnp.zeros((8 - M, L), F32)

    row = lax.broadcasted_iota(jnp.int32, (G, G), 0)
    col = lax.broadcasted_iota(jnp.int32, (G, G), 1)
    causal = row >= col
    lower = jnp.where(causal, 1.0, 0.0).astype(F32)
    log_decay = ld_ref[...]
    cum_t = lax.dot_general(
        lower, log_decay, (((1,), (1,)), ((), ())), precision=HIGHEST, preferred_element_type=F32
    )
    loads[1].wait()
    keys = kq_ref[:, :N]
    queries = kq_ref[:, N:]
    keys_t = keys.T
    loads[2].wait()

    def pool_rows(responses, parts, first, count):
        whole = jnp.concatenate(responses, axis=1)
        high = whole.astype(BF16)
        low = (whole - high.astype(F32)).astype(BF16)
        both = jnp.concatenate([high, low], axis=0)
        made = []
        for m in range(count):
            t = 2 * (first + m)
            added = jnp.dot(both, jnp.concatenate(parts(m), axis=0), preferred_element_type=F32)
            added = added[0 : 2 * M, :] + added[2 * M : 4 * M, :]
            made.append(jnp.where(left_half, added[t : t + 1, :], added[t + 1 : t + 2, :]))
        return jnp.concatenate(made, axis=0)

    def state_of(i):
        first, count = CHUNKS[i]
        state = buffers[i][0]
        for g in range(NY):
            for m in range(count):
                j = g * M + first + m
                lanes = slice(j * L, (j + 1) * L)
                level = jnp.where(
                    left_half, cum_t[:, 2 * j : 2 * j + 1], cum_t[:, 2 * j + 1 : 2 * j + 2]
                )
                grow[j] = level
                weight = jnp.exp(level[G - 1 : G, :] - level)
                weighted = (v_ref[:, lanes].astype(F32) * weight).astype(BF16)
                value = jnp.dot(keys_t, weighted, preferred_element_type=F32).astype(BF16)
                for half in range(NC):
                    to = jnp.where(c == half, c, 2)
                    for b in range(NZ):
                        at_row = half * 64 + b * 8
                        state[to, g, b, m * 8 : m * 8 + 8, :] = value[at_row : at_row + 8, :]

    def send_half(i):
        state = buffers[i][0]
        return push(state.at[2], state.at[c], pair_s.at[i], pair_r.at[i], to_pair)

    def inside(g):
        scores = lax.dot_general(
            queries, keys, (((1,), (1,)), ((), ())), preferred_element_type=F32
        )
        scores = jnp.where(causal, scores, 0.0)
        for m in range(M):
            j = g * M + m
            lanes = slice(j * L, (j + 1) * L)
            parts = []
            for h in (2 * j, 2 * j + 1):
                gap = jnp.minimum(cum_t[:, h : h + 1] - cum[h : h + 1, :], 0.0)
                parts.append((scores * jnp.exp(gap)).astype(BF16))
            value = v_ref[:, lanes]
            zero = jnp.zeros_like(value)
            stacked = jnp.concatenate(
                [jnp.where(left_half, value, zero), jnp.where(left_half, zero, value)], axis=0
            )
            diagonal = jnp.dot(
                jnp.concatenate(parts, axis=1), stacked, preferred_element_type=F32
            )
            direct = jnp.where(left_half, skip_ref[2 * j], skip_ref[2 * j + 1])
            result = diagonal + direct * value.astype(F32)
            local_out[j] = result
            pool_own[g, m : m + 1, :] = jnp.sum(result, axis=0, keepdims=True)
            grow[j] = jnp.exp(grow[j])

    for g in range(NY):
        pool_own[g, M:8, :] = jnp.zeros((8 - M, L), F32)
    state_of(0)
    pl.semaphore_wait(barrier, len(partners))
    pair_decay = push(decay_own, decay_pair, small_s.at[0], small_r.at[0], to_pair)
    pair_copies = [send_half(0)]
    for i in range(1, NCH):
        state_of(i)
        pair_copies.append(send_half(i))
    response[0] = lax.dot_general(
        jnp.exp(cum_t), queries.astype(F32), (((0,), (0,)), ((), ())),
        precision=HIGHEST, preferred_element_type=F32,
    )
    response[1] = jnp.broadcast_to(jnp.sum(log_decay, axis=1, keepdims=True), (HEADS, L))
    pair_response = push(response, response_pair, small_s.at[1], small_r.at[1], to_pair)
    table_copies = [
        push(cls_ref, table.at[x], table_s.at[k], table_r.at[k], to_x[k]) for k in range(1, NX)
    ]
    cum = lax.dot_general(
        log_decay, lower, (((1,), (1,)), ((), ())), precision=HIGHEST, preferred_element_type=F32
    )
    inside(0)

    pair_decay.wait_recv()
    for g in range(NY):
        mine, theirs = decay_own[g], decay_pair[g]
        decay_chip[g] = mine + theirs
        pair_factor[g] = spread(jnp.exp(jnp.where(c == 0, theirs, mine)))
        start_factor[g] = spread(jnp.exp(jnp.where(c == 0, mine, theirs)))
    plane_decays = [
        push(decay_chip.at[ys[k]], decay_plane.at[y], small_s.at[1 + k], small_r.at[1 + k], to_y[k])
        for k in FAR_Y
    ]
    decay_plane[y] = decay_chip[y]

    plane_copies = [[] for _ in CHUNKS]
    for i, (first, count) in enumerate(CHUNKS):
        state, pair_total, plane_recv = buffers[i][:3]
        rows = slice(first * 8, (first + count) * 8)
        pair_copies[i].wait_recv()
        for k in (*FAR_Y, 0):
            g = ys[k]

            @pl.loop(0, NZ)
            def _(b, g=g, k=k):
                total = pair_factor[g, rows, :] * state[0, g, b].astype(F32) + state[1, g, b].astype(F32)
                if k == 0:
                    plane_recv[y, b] = total.astype(BF16)
                else:
                    pair_total[k, b] = total.astype(BF16)

            if k:
                plane_copies[i].append(
                    push(pair_total.at[k], plane_recv.at[y], plane_s.at[i, k], plane_r.at[i, k], to_y[k])
                )

    pair_response.wait_recv()
    resp_0 = jnp.where(c == 0, response[0], response_pair[0])
    resp_1 = jnp.where(c == 0, response_pair[0], response[0])
    resp_0 = resp_0 + jnp.exp(jnp.where(c == 0, response[1], response_pair[1])) * resp_1
    chip_decay = response[1] + response_pair[1]
    for g in range(NY):
        heads = slice(2 * M * g, 2 * M * (g + 1))
        chip_response[g, 0, 0 : 2 * M, :] = resp_0[heads, :]
        chip_response[g, 1, 0 : 2 * M, :] = chip_decay[heads, :]
        chip_response[g, :, 2 * M : 16, :] = jnp.zeros((2, 16 - 2 * M, L), F32)
    plane_responses = [
        push(chip_response.at[ys[k]], plane_response.at[y], small_s.at[4 + k], small_r.at[4 + k], to_y[k])
        for k in FAR_Y
    ]
    plane_response[y] = chip_response[y]
    inside(1)
    for copy in (*plane_decays, *plane_responses):
        copy.wait_recv()
    run = jnp.zeros((8, L), F32)
    run_head = jnp.zeros((16, L), F32)
    summed = jnp.zeros((16, L), F32)
    for k in range(NY):
        plane_factor[k] = spread(jnp.exp(decay_plane[k]))
        plane_start[k] = spread(jnp.exp(run))
        run = run + decay_plane[k]
        summed = summed + jnp.exp(run_head) * plane_response[k, 0]
        run_head = run_head + plane_response[k, 1]
    axis_note[0:8, :] = run
    axis_note[8:24, :] = summed
    axis_notes[z, 0:8, :] = run
    axis_notes[z, 8:24, :] = summed
    for k in FAR_Z:
        push(axis_note, axis_notes.at[z], note_s.at[k], note_r.at[z], to_z[k])
    inside(2)
    inside(3)
    mine_1 = jnp.where(c == 0, resp_1, pltpu.roll(resp_1, 64, 1))
    for i, (first, count) in enumerate(CHUNKS):
        state = buffers[i][0]
        for g in range(NY):
            group = pool_rows(
                [mine_1[2 * M * g : 2 * M * (g + 1), 0:64]],
                lambda m, g=g, state=state: [state[0, g, b, m * 8 : m * 8 + 8, :] for b in range(NZ)],
                first, count,
            )
            tiles = slice(first, first + count)
            pool_own[g, tiles, :] = pool_own[g, tiles, :] + group
    part_copies = [
        push(pool_own.at[ys[k]], pool_parts.at[y], small_s.at[14 + k], small_r.at[14 + k], to_y[k])
        for k in FAR_Y
    ]
    pool_parts[y] = pool_own[y]

    axis_copies = [[] for _ in CHUNKS]
    for i, (first, count) in enumerate(CHUNKS):
        plane_recv, plane_prefix, axis_send, axis_recv = buffers[i][2:6]
        rows = slice(first * 8, (first + count) * 8)
        for copy in plane_copies[i]:
            copy.wait_recv()
        for k in (*FAR_Z, 0):
            b = zs[k]
            total = jnp.zeros((count * 8, L), F32)
            for q in range(NY):
                plane_prefix[q, b] = total
                total = plane_factor[q, rows, :] * total + plane_recv[q, b].astype(F32)
            if k == 0:
                axis_recv[z] = total.astype(BF16)
            else:
                axis_send[k] = total.astype(BF16)
                axis_copies[i].append(
                    push(axis_send.at[k], axis_recv.at[z], axis_s.at[i, k], axis_r.at[i, z], to_z[k])
                )
    for copy in part_copies:
        copy.wait_recv()
    my_half = [
        jnp.where(c == 0, plane_response[q, 0], pltpu.roll(plane_response[q, 0], 64, 1))[0 : 2 * M, 0:64]
        for q in range(1, NY)
    ]
    pool_rest = (pool_parts[0] + pool_parts[1]) + (pool_parts[2] + pool_parts[3])
    pool_tiles = []
    for i, (first, count) in enumerate(CHUNKS):
        plane_prefix = buffers[i][3]
        pool_tiles.append(
            pool_rows(
                my_half,
                lambda m, plane_prefix=plane_prefix: [
                    plane_prefix[q, b, m * 8 : m * 8 + 8, :].astype(BF16)
                    for q in range(1, NY)
                    for b in range(NZ)
                ],
                first, count,
            )
        )
    half_queries = jnp.where(
        c == 0, queries.astype(F32), pltpu.roll(queries.astype(F32), 64, 1)
    ).astype(BF16)

    def from_z(q):
        note = pltpu.make_async_remote_copy(
            src_ref=axis_note, dst_ref=axis_notes.at[q], send_sem=note_s.at[0], recv_sem=note_r.at[q],
            device_id=at(q, y, c), device_id_type=MESH,
        )
        return [note] + [
            pltpu.make_async_remote_copy(
                src_ref=buffers[i][4].at[0], dst_ref=buffers[i][5].at[q],
                send_sem=axis_s.at[i, 0], recv_sem=axis_r.at[i, q],
                device_id=at(q, y, c), device_id_type=MESH,
            )
            for i in range(NCH)
        ]

    def back(q):
        return [
            pltpu.make_async_remote_copy(
                src_ref=buffers[i][6].at[q], dst_ref=buffers[i][7].at[z],
                send_sem=back_s.at[i, q], recv_sem=back_r.at[i, z],
                device_id=at(q, y, c), device_id_type=MESH,
            )
            for i in range(NCH)
        ]

    def from_back(q, i):
        return pltpu.make_async_remote_copy(
            src_ref=buffers[i][6].at[0], dst_ref=buffers[i][7].at[q],
            send_sem=back_s.at[i, 0], recv_sem=back_r.at[i, q],
            device_id=at(q, y, c), device_id_type=MESH,
        )

    totals = [jnp.zeros((count * 8, L), F32) for _, count in CHUNKS]
    for q in range(NZ):
        for i in range(NCH):
            buffers[i][6][q] = totals[i].astype(BF16)
        if q > 0:

            @pl.when(z != q)
            def _(q=q):
                for copy in back(q):
                    copy.start()

            @pl.when(z == q)
            def _(q=q):
                for i in range(NCH):
                    buffers[i][7][q] = buffers[i][6][q]

        @pl.when(z != q)
        def _(q=q):
            for copy in from_z(q):
                copy.wait_recv()

        if q < NZ - 1:
            factor = spread(jnp.exp(axis_notes[q, 0:8, :]))
            for i, (first, count) in enumerate(CHUNKS):
                rows = slice(first * 8, (first + count) * 8)
                totals[i] = factor[rows, :] * totals[i] + buffers[i][5][q].astype(F32)

    @pl.when(z == 0)
    def _():
        for i in range(NCH):
            buffers[i][7][...] = jnp.zeros_like(buffers[i][7])

    lane = lax.broadcasted_iota(jnp.int32, (16, L), 1) // 8
    my_rows = jnp.zeros((16, L), F32)
    for q in range(NZ):
        turned = pltpu.roll(axis_notes[q, 8:24, :], lax.rem(2 * L + 8 * q - 64 * c - 8 * z, L), 1)
        my_rows = my_rows + jnp.where(lane == q, turned, 0.0)
    for i, (first, count) in enumerate(CHUNKS):
        axis_prefix = buffers[i][6]
        pool_tiles[i] = pool_tiles[i] + pool_rows(
            [my_rows[0 : 2 * M, 0:64]],
            lambda m, axis_prefix=axis_prefix: [
                axis_prefix[q, m * 8 : m * 8 + 8, :] for q in range(NZ)
            ],
            first, count,
        )
    pool_send[...] = pool_rest + jnp.concatenate(
        [*pool_tiles, jnp.zeros((8 - M, L), F32)], axis=0
    )
    pool_axis[z] = pool_send[...]
    pool_copies = [
        push(pool_send, pool_axis.at[z], small_s.at[17 + k], small_r.at[17 + k], to_z[k])
        for k in FAR_Z
    ]

    earlier = list(sends)
    sends.clear()
    chip_copies = [[] for _ in CHUNKS]
    for i, (first, count) in enumerate(CHUNKS):
        plane_prefix = buffers[i][3]
        start_plane, start_send, start_chip = buffers[i][7:10]
        rows = slice(first * 8, (first + count) * 8)
        for q in range(NZ):

            @pl.when((z != q) & (z > 0))
            def _(q=q, i=i):
                from_back(q, i).wait_recv()

        for k in (*FAR_Y, 0):
            g = ys[k]

            @pl.loop(0, NZ)
            def _(b, g=g, k=k):
                start = plane_start[g, rows, :] * start_plane[b].astype(F32) + plane_prefix[g, b]
                if k == 0:
                    start_chip[y, b] = start.astype(BF16)
                else:
                    start_send[k, b] = start.astype(BF16)

            if k:
                chip_copies[i].append(
                    push(start_send.at[k], start_chip.at[y], plane_s.at[i, 3 + k], plane_r.at[i, 3 + k], to_y[k])
                )

    for copy in earlier:
        copy.wait_send()

    half_copies = []
    for i, (first, count) in enumerate(CHUNKS):
        state = buffers[i][0]
        start_chip, carried, carried_recv = buffers[i][9:12]
        rows = slice(first * 8, (first + count) * 8)
        for copy in chip_copies[i]:
            copy.wait_recv()

        @pl.loop(0, NY)
        def _(g):
            @pl.loop(0, NZ)
            def _(b):
                before = start_chip[g, b].astype(F32)
                after = start_factor[g, rows, :] * before + state[0, g, b].astype(F32)
                carried[0, g, b] = start_chip[g, b]
                carried[1, g, b] = after.astype(BF16)

        half_copies.append(
            push(carried.at[other], carried_recv, pair_s.at[NCH + i], pair_r.at[NCH + i], to_pair)
        )

    for copy in pool_copies:
        copy.wait_recv()
    total = pool_axis[0]
    for q in range(1, NZ):
        total = total + pool_axis[q]
    pool_sum[...] = total
    mine = pool_plane.at[y * NC + c]
    pool_plane[y * NC + c] = total
    last_copies = (
        [push(pool_sum, mine, small_s.at[24 + k], small_r.at[24 + k], to_y[k]) for k in FAR_Y]
        + [push(pool_sum, mine, small_s.at[27 + k], small_r.at[27 + k], to_y_other[k]) for k in FAR_Y]
        + [push(pool_sum, mine, small_s.at[31], small_r.at[31], to_pair)]
    )

    stores = []

    def final(i):
        first, count = CHUNKS[i]
        carried, carried_recv = buffers[i][10:12]
        half_copies[i].wait_recv()
        for g in range(NY):
            for m in range(count):
                j = g * M + first + m
                lanes = slice(j * L, (j + 1) * L)
                tile = slice(m * 8, m * 8 + 8)
                start = jnp.concatenate(
                    [carried[c, g, b, tile, :] for b in range(NZ)]
                    + [carried_recv[g, b, tile, :] for b in range(NZ)],
                    axis=0,
                )
                full = local_out[j] + grow[j] * jnp.dot(
                    half_queries, start, preferred_element_type=F32
                )
                out_ref[:, lanes] = full.astype(BF16)
            lanes = slice((g * M + first) * L, (g * M + first + count) * L)
            store = pltpu.make_async_copy(
                out_ref.at[:, lanes], mixed_ref.at[:, lanes], out_s.at[i * NY + g]
            )
            store.start()
            stores.append(store)

    for i in range(NCH):
        final(i)

    for copy in table_copies:
        copy.wait_recv()
    loads[3].wait()
    for copy in last_copies:
        copy.wait_recv()
    pooled = [
        (pool_plane[NC * g] + pool_plane[NC * g + 1]) / (G * NZ * NY * NC) for g in range(NY)
    ]
    square = sum(jnp.sum(p * p, keepdims=True) for p in pooled) / (TILES * L)
    scale = 1.0 / jnp.sqrt(square + EPS)
    wide = jnp.concatenate(
        [
            jnp.broadcast_to((pooled[g] * scale)[m : m + 1, :], (16, L)).astype(BF16)
            for g in range(NY)
            for m in range(M)
        ],
        axis=1,
    )
    classifier = table[...].reshape(TILES * L, L)
    logits = jnp.dot(wide, classifier, preferred_element_type=F32)
    logits_ref[...] = logits[0:1, :]

    for store in stores:
        store.wait()
    for q in range(1, NZ):

        @pl.when(z != q)
        def _(q=q):
            for copy in back(q):
                copy.wait_send()

    for copy in sends:
        copy.wait_send()


def hand_over(mixed_in, logits_in, mixed_out, logits_out, mixed, logits, in_sem, out_sem):
    pairs = [(logits_in, logits, logits_out)]
    for i in range(PIECES):
        rows = slice(i * (G // PIECES), (i + 1) * (G // PIECES))
        pairs.append((mixed_in.at[rows, :], mixed.at[rows, :], mixed_out.at[rows, :]))
    loads = [pltpu.make_async_copy(a, b, in_sem.at[i]) for i, (a, b, _) in enumerate(pairs)]
    stores = [pltpu.make_async_copy(b, c, out_sem.at[i]) for i, (_, b, c) in enumerate(pairs)]
    for load in loads:
        load.start()
    for load, store in zip(loads, stores):
        load.wait()
        store.start()
    for store in stores:
        store.wait()


def local(inputs, keys_queries, log_decay, skip, classifier):
    copies, positions, channels = inputs.shape
    heads = log_decay.shape[1]
    hbm = pl.BlockSpec(memory_space=pltpu.HBM)

    def chunk(count):
        slab = (NZ, count * 8, L)
        return [
            pltpu.VMEM((3, NY, *slab), BF16),
            pltpu.VMEM((NY, *slab), BF16),
            pltpu.VMEM((NY, *slab), BF16),
            pltpu.VMEM((NY, *slab), F32),
            pltpu.VMEM(slab, BF16),
            pltpu.VMEM(slab, BF16),
            pltpu.VMEM(slab, BF16),
            pltpu.VMEM(slab, BF16),
            pltpu.VMEM((NY, *slab), BF16),
            pltpu.VMEM((NY, *slab), BF16),
            pltpu.VMEM((NC, NY, *slab), BF16),
            pltpu.VMEM((NY, *slab), BF16),
        ]

    dma = pltpu.SemaphoreType.DMA
    scratch = [
        pltpu.VMEM((positions, channels), BF16),
        pltpu.VMEM((positions, 2 * N), BF16),
        pltpu.VMEM((heads, positions), F32),
        pltpu.VMEM((positions, channels), BF16),
        pltpu.VMEM((TILES, G, L), F32),
        pltpu.VMEM((TILES, G, L), F32),
        pltpu.VMEM((NX, *classifier.shape), BF16),
        pltpu.VMEM((NY, 8, L), F32),
        pltpu.VMEM((NY, 8, L), F32),
        pltpu.VMEM((NY, 8, L), F32),
        pltpu.VMEM((NY, 8, L), F32),
        pltpu.VMEM((NY, M * 8, L), F32),
        pltpu.VMEM((NY, M * 8, L), F32),
        pltpu.VMEM((NY, M * 8, L), F32),
        pltpu.VMEM((NY, M * 8, L), F32),
        pltpu.VMEM((2, HEADS, L), F32),
        pltpu.VMEM((2, HEADS, L), F32),
        pltpu.VMEM((NY, 2, 16, L), F32),
        pltpu.VMEM((NY, 2, 16, L), F32),
        pltpu.VMEM((24, L), F32),
        pltpu.VMEM((NZ, 24, L), F32),
        pltpu.VMEM((NY, 8, L), F32),
        pltpu.VMEM((NY, 8, L), F32),
        pltpu.VMEM((8, L), F32),
        pltpu.VMEM((NZ, 8, L), F32),
        pltpu.VMEM((8, L), F32),
        pltpu.VMEM((NY * NC, 8, L), F32),
        *[ref for _, count in CHUNKS for ref in chunk(count)],
        dma((4,)), dma((NCH * NY,)),
        dma((2 * NCH,)), dma((2 * NCH,)), dma((NCH, 7)), dma((NCH, 7)),
        dma((NCH, NZ)), dma((NCH, NZ)), dma((NCH, NZ)), dma((NCH, NZ)),
        dma((NZ,)), dma((NZ,)), dma((NX,)), dma((NX,)), dma((32,)), dma((32,)),
    ]
    mixed, logits = pl.pallas_call(
        kernel,
        out_shape=(
            jax.ShapeDtypeStruct((positions, channels), BF16),
            jax.ShapeDtypeStruct((1, classifier.shape[1]), F32),
        ),
        in_specs=[hbm, hbm, hbm, pl.BlockSpec(memory_space=pltpu.SMEM), hbm],
        out_specs=(hbm, pl.BlockSpec(memory_space=pltpu.VMEM)),
        scratch_shapes=scratch,
        compiler_params=pltpu.CompilerParams(
            collective_id=0, has_side_effects=True, vmem_limit_bytes=60 << 20
        ),
    )(
        inputs.reshape(positions, channels),
        keys_queries.reshape(positions, 2 * N),
        log_decay.reshape(heads, positions),
        skip,
        classifier,
    )
    mixed, logits = pl.pallas_call(
        hand_over,
        out_shape=(
            jax.ShapeDtypeStruct(mixed.shape, mixed.dtype),
            jax.ShapeDtypeStruct(logits.shape, logits.dtype),
        ),
        in_specs=[hbm, hbm],
        out_specs=(hbm, hbm),
        scratch_shapes=[
            pltpu.VMEM(mixed.shape, mixed.dtype),
            pltpu.VMEM(logits.shape, logits.dtype),
            dma((PIECES + 1,)),
            dma((PIECES + 1,)),
        ],
        compiler_params=pltpu.CompilerParams(vmem_limit_bytes=60 << 20),
    )(mixed, logits)
    return mixed.reshape(copies, positions, channels), logits


def solution(mesh):
    return jax.shard_map(
        local,
        mesh=mesh,
        in_specs=(
            P("fsdp", "seq", None),
            P("fsdp", "seq", None),
            P("fsdp", None, "seq"),
            P(),
            P("fsdp", None),
        ),
        out_specs=(P("fsdp", "seq", None), P("fsdp", None)),
        check_vma=False,
    )
```

```python
import jax
import jax.numpy as jnp
from jax import lax
from jax.experimental import pallas as pl
from jax.experimental.pallas import tpu as pltpu
from jax.sharding import PartitionSpec as P

MESH = pl.DeviceIdType.MESH
F32, BF16 = jnp.float32, jnp.bfloat16
HIGHEST = lax.Precision.HIGHEST

N = 128
G = 128
L = 128
NZ, NY, NC, NX = 8, 4, 2, 4
HEADS = 56
TILES = 28
M = TILES // NY
CHUNKS = ((0, 4), (4, 3))
NCH = len(CHUNKS)
EPS = 1e-06
PIECES = 8
FAR_Y = (2, 1, 3)
FAR_Z = (4, 5, 3, 6, 2, 7, 1)


def spread(x):
    return jnp.concatenate(
        [jnp.broadcast_to(x[m : m + 1, :], (8, L)) for m in range(M)], axis=0
    )


def kernel(
    v_hbm, kq_hbm, ld_hbm, skip_ref, cls_ref, mixed_ref, logits_ref,
    v_ref, kq_ref, ld_ref, out_ref, grow, local_out, table,
    decay_own, decay_pair, decay_chip, decay_plane,
    pair_factor, start_factor, plane_factor, plane_start,
    response, response_pair, chip_response, plane_response, axis_note, axis_notes,
    pool_own, pool_parts, pool_send, pool_axis, pool_sum, pool_plane,
    *rest,
):
    buffers = [rest[i * 12 : (i + 1) * 12] for i in range(NCH)]
    (in_s, out_s, pair_s, pair_r, plane_s, plane_r, axis_s, axis_r,
     back_s, back_r, note_s, note_r, table_s, table_r, small_s, small_r) = rest[NCH * 12 :]
    me, x = lax.axis_index("seq"), lax.axis_index("fsdp")
    c = lax.rem(me, NC)
    y = lax.rem(me // NC, NY)
    z = me // (NC * NY)
    other = 1 - c
    ys = [lax.rem(y + k, NY) for k in range(NY)]
    zs = [lax.rem(z + k, NZ) for k in range(NZ)]

    def at(z_, y_, c_):
        return {"seq": (z_ * NY + y_) * NC + c_}

    to_pair = at(z, y, other)
    to_y = [at(z, ys[k], c) for k in range(NY)]
    to_y_other = [at(z, ys[k], other) for k in range(NY)]
    to_z = [at(zs[k], y, c) for k in range(NZ)]
    to_x = [{"fsdp": lax.rem(x + k, NX)} for k in range(NX)]

    barrier = pltpu.get_barrier_semaphore()
    partners = to_z[1:] + to_y[1:] + to_y_other[1:] + to_x[1:] + [to_pair]
    for who in partners:
        pl.semaphore_signal(barrier, inc=1, device_id=who, device_id_type=MESH)

    loads = [
        pltpu.make_async_copy(src, dst, in_s.at[i])
        for i, (src, dst) in enumerate(
            ((ld_hbm, ld_ref), (kq_hbm, kq_ref), (v_hbm, v_ref), (cls_ref, table.at[x]))
        )
    ]
    for load in loads:
        load.start()

    sends = []

    def push(src, dst, send, recv, who):
        copy = pltpu.make_async_remote_copy(
            src_ref=src, dst_ref=dst, send_sem=send, recv_sem=recv,
            device_id=who, device_id_type=MESH,
        )
        copy.start()
        sends.append(copy)
        return copy

    loads[0].wait()
    left_half = lax.broadcasted_iota(jnp.int32, (1, L), 1) < 64
    for g in range(NY):
        even = jnp.sum(ld_ref[pl.ds(2 * M * g, M, stride=2), :], axis=1, keepdims=True)
        odd = jnp.sum(ld_ref[pl.ds(2 * M * g + 1, M, stride=2), :], axis=1, keepdims=True)
        decay_own[g, 0:M, :] = jnp.where(left_half, even, odd)
        decay_own[g, M:8, :] = jnp.zeros((8 - M, L), F32)

    row = lax.broadcasted_iota(jnp.int32, (G, G), 0)
    col = lax.broadcasted_iota(jnp.int32, (G, G), 1)
    causal = row >= col
    lower = jnp.where(causal, 1.0, 0.0).astype(F32)
    log_decay = ld_ref[...]
    cum_t = lax.dot_general(
        lower, log_decay, (((1,), (1,)), ((), ())), precision=HIGHEST, preferred_element_type=F32
    )
    loads[1].wait()
    keys = kq_ref[:, :N]
    queries = kq_ref[:, N:]
    keys_t = keys.T
    loads[2].wait()

    def pool_rows(responses, parts, first, count):
        whole = jnp.concatenate(responses, axis=1)
        high = whole.astype(BF16)
        low = (whole - high.astype(F32)).astype(BF16)
        both = jnp.concatenate([high, low], axis=0)
        made = []
        for m in range(count):
            t = 2 * (first + m)
            added = jnp.dot(both, jnp.concatenate(parts(m), axis=0), preferred_element_type=F32)
            added = added[0 : 2 * M, :] + added[2 * M : 4 * M, :]
            made.append(jnp.where(left_half, added[t : t + 1, :], added[t + 1 : t + 2, :]))
        return jnp.concatenate(made, axis=0)

    def state_of(i):
        first, count = CHUNKS[i]
        state = buffers[i][0]
        for g in range(NY):
            for m in range(count):
                j = g * M + first + m
                lanes = slice(j * L, (j + 1) * L)
                level = jnp.where(
                    left_half, cum_t[:, 2 * j : 2 * j + 1], cum_t[:, 2 * j + 1 : 2 * j + 2]
                )
                grow[j] = level
                weight = jnp.exp(level[G - 1 : G, :] - level)
                weighted = (v_ref[:, lanes].astype(F32) * weight).astype(BF16)
                value = jnp.dot(keys_t, weighted, preferred_element_type=F32).astype(BF16)
                for half in range(NC):
                    to = jnp.where(c == half, c, 2)
                    for b in range(NZ):
                        at_row = half * 64 + b * 8
                        state[to, g, b, m * 8 : m * 8 + 8, :] = value[at_row : at_row + 8, :]

    def send_half(i):
        state = buffers[i][0]
        return push(state.at[2], state.at[c], pair_s.at[i], pair_r.at[i], to_pair)

    def inside(g):
        scores = lax.dot_general(
            queries, keys, (((1,), (1,)), ((), ())), preferred_element_type=F32
        )
        scores = jnp.where(causal, scores, 0.0)
        for m in range(M):
            j = g * M + m
            lanes = slice(j * L, (j + 1) * L)
            parts = []
            for h in (2 * j, 2 * j + 1):
                gap = jnp.minimum(cum_t[:, h : h + 1] - cum[h : h + 1, :], 0.0)
                parts.append((scores * jnp.exp(gap)).astype(BF16))
            value = v_ref[:, lanes]
            zero = jnp.zeros_like(value)
            stacked = jnp.concatenate(
                [jnp.where(left_half, value, zero), jnp.where(left_half, zero, value)], axis=0
            )
            diagonal = jnp.dot(
                jnp.concatenate(parts, axis=1), stacked, preferred_element_type=F32
            )
            direct = jnp.where(left_half, skip_ref[2 * j], skip_ref[2 * j + 1])
            result = diagonal + direct * value.astype(F32)
            local_out[j] = result
            pool_own[g, m : m + 1, :] = jnp.sum(result, axis=0, keepdims=True)
            grow[j] = jnp.exp(grow[j])

    for g in range(NY):
        pool_own[g, M:8, :] = jnp.zeros((8 - M, L), F32)
    state_of(0)
    pl.semaphore_wait(barrier, len(partners))
    pair_decay = push(decay_own, decay_pair, small_s.at[0], small_r.at[0], to_pair)
    pair_copies = [send_half(0)]
    for i in range(1, NCH):
        state_of(i)
        pair_copies.append(send_half(i))
    response[0] = lax.dot_general(
        jnp.exp(cum_t), queries.astype(F32), (((0,), (0,)), ((), ())),
        precision=HIGHEST, preferred_element_type=F32,
    )
    response[1] = jnp.broadcast_to(jnp.sum(log_decay, axis=1, keepdims=True), (HEADS, L))
    pair_response = push(response, response_pair, small_s.at[1], small_r.at[1], to_pair)
    table_copies = [
        push(cls_ref, table.at[x], table_s.at[k], table_r.at[k], to_x[k]) for k in range(1, NX)
    ]
    cum = lax.dot_general(
        log_decay, lower, (((1,), (1,)), ((), ())), precision=HIGHEST, preferred_element_type=F32
    )
    inside(0)

    pair_decay.wait_recv()
    for g in range(NY):
        mine, theirs = decay_own[g], decay_pair[g]
        decay_chip[g] = mine + theirs
        pair_factor[g] = spread(jnp.exp(jnp.where(c == 0, theirs, mine)))
        start_factor[g] = spread(jnp.exp(jnp.where(c == 0, mine, theirs)))
    plane_decays = [
        push(decay_chip.at[ys[k]], decay_plane.at[y], small_s.at[1 + k], small_r.at[1 + k], to_y[k])
        for k in FAR_Y
    ]
    decay_plane[y] = decay_chip[y]

    plane_copies = [[] for _ in CHUNKS]
    for i, (first, count) in enumerate(CHUNKS):
        state, pair_total, plane_recv = buffers[i][:3]
        rows = slice(first * 8, (first + count) * 8)
        pair_copies[i].wait_recv()
        for k in (*FAR_Y, 0):
            g = ys[k]

            @pl.loop(0, NZ)
            def _(b, g=g, k=k):
                total = pair_factor[g, rows, :] * state[0, g, b].astype(F32) + state[1, g, b].astype(F32)
                if k == 0:
                    plane_recv[y, b] = total.astype(BF16)
                else:
                    pair_total[k, b] = total.astype(BF16)

            if k:
                plane_copies[i].append(
                    push(pair_total.at[k], plane_recv.at[y], plane_s.at[i, k], plane_r.at[i, k], to_y[k])
                )

    pair_response.wait_recv()
    resp_0 = jnp.where(c == 0, response[0], response_pair[0])
    resp_1 = jnp.where(c == 0, response_pair[0], response[0])
    resp_0 = resp_0 + jnp.exp(jnp.where(c == 0, response[1], response_pair[1])) * resp_1
    chip_decay = response[1] + response_pair[1]
    for g in range(NY):
        heads = slice(2 * M * g, 2 * M * (g + 1))
        chip_response[g, 0, 0 : 2 * M, :] = resp_0[heads, :]
        chip_response[g, 1, 0 : 2 * M, :] = chip_decay[heads, :]
        chip_response[g, :, 2 * M : 16, :] = jnp.zeros((2, 16 - 2 * M, L), F32)
    plane_responses = [
        push(chip_response.at[ys[k]], plane_response.at[y], small_s.at[4 + k], small_r.at[4 + k], to_y[k])
        for k in FAR_Y
    ]
    plane_response[y] = chip_response[y]
    inside(1)
    for copy in (*plane_decays, *plane_responses):
        copy.wait_recv()
    run = jnp.zeros((8, L), F32)
    run_head = jnp.zeros((16, L), F32)
    summed = jnp.zeros((16, L), F32)
    for k in range(NY):
        plane_factor[k] = spread(jnp.exp(decay_plane[k]))
        plane_start[k] = spread(jnp.exp(run))
        run = run + decay_plane[k]
        summed = summed + jnp.exp(run_head) * plane_response[k, 0]
        run_head = run_head + plane_response[k, 1]
    axis_note[0:8, :] = run
    axis_note[8:24, :] = summed
    axis_notes[z, 0:8, :] = run
    axis_notes[z, 8:24, :] = summed
    for k in FAR_Z:
        push(axis_note, axis_notes.at[z], note_s.at[k], note_r.at[z], to_z[k])
    inside(2)
    inside(3)
    mine_1 = jnp.where(c == 0, resp_1, pltpu.roll(resp_1, 64, 1))
    for i, (first, count) in enumerate(CHUNKS):
        state = buffers[i][0]
        for g in range(NY):
            group = pool_rows(
                [mine_1[2 * M * g : 2 * M * (g + 1), 0:64]],
                lambda m, g=g, state=state: [state[0, g, b, m * 8 : m * 8 + 8, :] for b in range(NZ)],
                first, count,
            )
            tiles = slice(first, first + count)
            pool_own[g, tiles, :] = pool_own[g, tiles, :] + group
    part_copies = [
        push(pool_own.at[ys[k]], pool_parts.at[y], small_s.at[14 + k], small_r.at[14 + k], to_y[k])
        for k in FAR_Y
    ]
    pool_parts[y] = pool_own[y]

    axis_copies = [[] for _ in CHUNKS]
    for i, (first, count) in enumerate(CHUNKS):
        plane_recv, plane_prefix, axis_send, axis_recv = buffers[i][2:6]
        rows = slice(first * 8, (first + count) * 8)
        for copy in plane_copies[i]:
            copy.wait_recv()
        for k in (*FAR_Z, 0):
            b = zs[k]
            total = jnp.zeros((count * 8, L), F32)
            for q in range(NY):
                plane_prefix[q, b] = total
                total = plane_factor[q, rows, :] * total + plane_recv[q, b].astype(F32)
            if k == 0:
                axis_recv[z] = total.astype(BF16)
            else:
                axis_send[k] = total.astype(BF16)
                axis_copies[i].append(
                    push(axis_send.at[k], axis_recv.at[z], axis_s.at[i, k], axis_r.at[i, z], to_z[k])
                )
    for copy in part_copies:
        copy.wait_recv()
    my_half = [
        jnp.where(c == 0, plane_response[q, 0], pltpu.roll(plane_response[q, 0], 64, 1))[0 : 2 * M, 0:64]
        for q in range(1, NY)
    ]
    pool_rest = (pool_parts[0] + pool_parts[1]) + (pool_parts[2] + pool_parts[3])
    pool_tiles = []
    for i, (first, count) in enumerate(CHUNKS):
        plane_prefix = buffers[i][3]
        pool_tiles.append(
            pool_rows(
                my_half,
                lambda m, plane_prefix=plane_prefix: [
                    plane_prefix[q, b, m * 8 : m * 8 + 8, :].astype(BF16)
                    for q in range(1, NY)
                    for b in range(NZ)
                ],
                first, count,
            )
        )
    half_queries = jnp.where(
        c == 0, queries.astype(F32), pltpu.roll(queries.astype(F32), 64, 1)
    ).astype(BF16)

    def from_z(q):
        note = pltpu.make_async_remote_copy(
            src_ref=axis_note, dst_ref=axis_notes.at[q], send_sem=note_s.at[0], recv_sem=note_r.at[q],
            device_id=at(q, y, c), device_id_type=MESH,
        )
        return [note] + [
            pltpu.make_async_remote_copy(
                src_ref=buffers[i][4].at[0], dst_ref=buffers[i][5].at[q],
                send_sem=axis_s.at[i, 0], recv_sem=axis_r.at[i, q],
                device_id=at(q, y, c), device_id_type=MESH,
            )
            for i in range(NCH)
        ]

    def back(q):
        return [
            pltpu.make_async_remote_copy(
                src_ref=buffers[i][6].at[q], dst_ref=buffers[i][7].at[z],
                send_sem=back_s.at[i, q], recv_sem=back_r.at[i, z],
                device_id=at(q, y, c), device_id_type=MESH,
            )
            for i in range(NCH)
        ]

    def from_back(q, i):
        return pltpu.make_async_remote_copy(
            src_ref=buffers[i][6].at[0], dst_ref=buffers[i][7].at[q],
            send_sem=back_s.at[i, 0], recv_sem=back_r.at[i, q],
            device_id=at(q, y, c), device_id_type=MESH,
        )

    totals = [jnp.zeros((count * 8, L), F32) for _, count in CHUNKS]
    for q in range(NZ):
        for i in range(NCH):
            buffers[i][6][q] = totals[i].astype(BF16)
        if q > 0:

            @pl.when(z != q)
            def _(q=q):
                for copy in back(q):
                    copy.start()

            @pl.when(z == q)
            def _(q=q):
                for i in range(NCH):
                    buffers[i][7][q] = buffers[i][6][q]

        @pl.when(z != q)
        def _(q=q):
            for copy in from_z(q):
                copy.wait_recv()

        if q < NZ - 1:
            factor = spread(jnp.exp(axis_notes[q, 0:8, :]))
            for i, (first, count) in enumerate(CHUNKS):
                rows = slice(first * 8, (first + count) * 8)
                totals[i] = factor[rows, :] * totals[i] + buffers[i][5][q].astype(F32)

    @pl.when(z == 0)
    def _():
        for i in range(NCH):
            buffers[i][7][...] = jnp.zeros_like(buffers[i][7])

    lane = lax.broadcasted_iota(jnp.int32, (16, L), 1) // 8
    my_rows = jnp.zeros((16, L), F32)
    for q in range(NZ):
        turned = pltpu.roll(axis_notes[q, 8:24, :], lax.rem(2 * L + 8 * q - 64 * c - 8 * z, L), 1)
        my_rows = my_rows + jnp.where(lane == q, turned, 0.0)
    for i, (first, count) in enumerate(CHUNKS):
        axis_prefix = buffers[i][6]
        pool_tiles[i] = pool_tiles[i] + pool_rows(
            [my_rows[0 : 2 * M, 0:64]],
            lambda m, axis_prefix=axis_prefix: [
                axis_prefix[q, m * 8 : m * 8 + 8, :] for q in range(NZ)
            ],
            first, count,
        )
    pool_send[...] = pool_rest + jnp.concatenate(
        [*pool_tiles, jnp.zeros((8 - M, L), F32)], axis=0
    )
    pool_axis[z] = pool_send[...]
    pool_copies = [
        push(pool_send, pool_axis.at[z], small_s.at[17 + k], small_r.at[17 + k], to_z[k])
        for k in FAR_Z
    ]

    earlier = list(sends)
    sends.clear()
    chip_copies = [[] for _ in CHUNKS]
    for i, (first, count) in enumerate(CHUNKS):
        plane_prefix = buffers[i][3]
        start_plane, start_send, start_chip = buffers[i][7:10]
        rows = slice(first * 8, (first + count) * 8)
        for q in range(NZ):

            @pl.when((z != q) & (z > 0))
            def _(q=q, i=i):
                from_back(q, i).wait_recv()

        for k in (*FAR_Y, 0):
            g = ys[k]

            @pl.loop(0, NZ)
            def _(b, g=g, k=k):
                start = plane_start[g, rows, :] * start_plane[b].astype(F32) + plane_prefix[g, b]
                if k == 0:
                    start_chip[y, b] = start.astype(BF16)
                else:
                    start_send[k, b] = start.astype(BF16)

            if k:
                chip_copies[i].append(
                    push(start_send.at[k], start_chip.at[y], plane_s.at[i, 3 + k], plane_r.at[i, 3 + k], to_y[k])
                )

    for copy in earlier:
        copy.wait_send()

    for copy in pool_copies:
        copy.wait_recv()
    total = pool_axis[0]
    for q in range(1, NZ):
        total = total + pool_axis[q]
    pool_sum[...] = total
    mine = pool_plane.at[y * NC + c]
    pool_plane[y * NC + c] = total
    last_copies = (
        [push(pool_sum, mine, small_s.at[24 + k], small_r.at[24 + k], to_y[k]) for k in FAR_Y]
        + [push(pool_sum, mine, small_s.at[27 + k], small_r.at[27 + k], to_y_other[k]) for k in FAR_Y]
        + [push(pool_sum, mine, small_s.at[31], small_r.at[31], to_pair)]
    )

    half_copies = []
    for i, (first, count) in enumerate(CHUNKS):
        state = buffers[i][0]
        start_chip, carried, carried_recv = buffers[i][9:12]
        rows = slice(first * 8, (first + count) * 8)
        for copy in chip_copies[i]:
            copy.wait_recv()

        @pl.loop(0, NY)
        def _(g):
            @pl.loop(0, NZ)
            def _(b):
                before = start_chip[g, b].astype(F32)
                after = start_factor[g, rows, :] * before + state[0, g, b].astype(F32)
                carried[0, g, b] = start_chip[g, b]
                carried[1, g, b] = after.astype(BF16)

        half_copies.append(
            push(carried.at[other], carried_recv, pair_s.at[NCH + i], pair_r.at[NCH + i], to_pair)
        )

    stores = []

    def final(i):
        first, count = CHUNKS[i]
        carried, carried_recv = buffers[i][10:12]
        half_copies[i].wait_recv()
        for g in range(NY):
            for m in range(count):
                j = g * M + first + m
                lanes = slice(j * L, (j + 1) * L)
                tile = slice(m * 8, m * 8 + 8)
                start = jnp.concatenate(
                    [carried[c, g, b, tile, :] for b in range(NZ)]
                    + [carried_recv[g, b, tile, :] for b in range(NZ)],
                    axis=0,
                )
                full = local_out[j] + grow[j] * jnp.dot(
                    half_queries, start, preferred_element_type=F32
                )
                out_ref[:, lanes] = full.astype(BF16)
            lanes = slice((g * M + first) * L, (g * M + first + count) * L)
            store = pltpu.make_async_copy(
                out_ref.at[:, lanes], mixed_ref.at[:, lanes], out_s.at[i * NY + g]
            )
            store.start()
            stores.append(store)

    for i in range(NCH):
        final(i)

    for copy in table_copies:
        copy.wait_recv()
    loads[3].wait()
    for copy in last_copies:
        copy.wait_recv()
    pooled = [
        (pool_plane[NC * g] + pool_plane[NC * g + 1]) / (G * NZ * NY * NC) for g in range(NY)
    ]
    square = sum(jnp.sum(p * p, keepdims=True) for p in pooled) / (TILES * L)
    scale = 1.0 / jnp.sqrt(square + EPS)
    wide = jnp.concatenate(
        [
            jnp.broadcast_to((pooled[g] * scale)[m : m + 1, :], (16, L)).astype(BF16)
            for g in range(NY)
            for m in range(M)
        ],
        axis=1,
    )
    classifier = table[...].reshape(TILES * L, L)
    logits = jnp.dot(wide, classifier, preferred_element_type=F32)
    logits_ref[...] = logits[0:1, :]

    for store in stores:
        store.wait()
    for q in range(1, NZ):

        @pl.when(z != q)
        def _(q=q):
            for copy in back(q):
                copy.wait_send()

    for copy in sends:
        copy.wait_send()


def hand_over(mixed_in, logits_in, mixed_out, logits_out, mixed, logits, in_sem, out_sem):
    pairs = [(logits_in, logits, logits_out)]
    for i in range(PIECES):
        rows = slice(i * (G // PIECES), (i + 1) * (G // PIECES))
        pairs.append((mixed_in.at[rows, :], mixed.at[rows, :], mixed_out.at[rows, :]))
    loads = [pltpu.make_async_copy(a, b, in_sem.at[i]) for i, (a, b, _) in enumerate(pairs)]
    stores = [pltpu.make_async_copy(b, c, out_sem.at[i]) for i, (_, b, c) in enumerate(pairs)]
    for load in loads:
        load.start()
    for load, store in zip(loads, stores):
        load.wait()
        store.start()
    for store in stores:
        store.wait()


def local(inputs, keys_queries, log_decay, skip, classifier):
    copies, positions, channels = inputs.shape
    heads = log_decay.shape[1]
    hbm = pl.BlockSpec(memory_space=pltpu.HBM)

    def chunk(count):
        slab = (NZ, count * 8, L)
        return [
            pltpu.VMEM((3, NY, *slab), BF16),
            pltpu.VMEM((NY, *slab), BF16),
            pltpu.VMEM((NY, *slab), BF16),
            pltpu.VMEM((NY, *slab), F32),
            pltpu.VMEM(slab, BF16),
            pltpu.VMEM(slab, BF16),
            pltpu.VMEM(slab, BF16),
            pltpu.VMEM(slab, BF16),
            pltpu.VMEM((NY, *slab), BF16),
            pltpu.VMEM((NY, *slab), BF16),
            pltpu.VMEM((NC, NY, *slab), BF16),
            pltpu.VMEM((NY, *slab), BF16),
        ]

    dma = pltpu.SemaphoreType.DMA
    scratch = [
        pltpu.VMEM((positions, channels), BF16),
        pltpu.VMEM((positions, 2 * N), BF16),
        pltpu.VMEM((heads, positions), F32),
        pltpu.VMEM((positions, channels), BF16),
        pltpu.VMEM((TILES, G, L), F32),
        pltpu.VMEM((TILES, G, L), F32),
        pltpu.VMEM((NX, *classifier.shape), BF16),
        pltpu.VMEM((NY, 8, L), F32),
        pltpu.VMEM((NY, 8, L), F32),
        pltpu.VMEM((NY, 8, L), F32),
        pltpu.VMEM((NY, 8, L), F32),
        pltpu.VMEM((NY, M * 8, L), F32),
        pltpu.VMEM((NY, M * 8, L), F32),
        pltpu.VMEM((NY, M * 8, L), F32),
        pltpu.VMEM((NY, M * 8, L), F32),
        pltpu.VMEM((2, HEADS, L), F32),
        pltpu.VMEM((2, HEADS, L), F32),
        pltpu.VMEM((NY, 2, 16, L), F32),
        pltpu.VMEM((NY, 2, 16, L), F32),
        pltpu.VMEM((24, L), F32),
        pltpu.VMEM((NZ, 24, L), F32),
        pltpu.VMEM((NY, 8, L), F32),
        pltpu.VMEM((NY, 8, L), F32),
        pltpu.VMEM((8, L), F32),
        pltpu.VMEM((NZ, 8, L), F32),
        pltpu.VMEM((8, L), F32),
        pltpu.VMEM((NY * NC, 8, L), F32),
        *[ref for _, count in CHUNKS for ref in chunk(count)],
        dma((4,)), dma((NCH * NY,)),
        dma((2 * NCH,)), dma((2 * NCH,)), dma((NCH, 7)), dma((NCH, 7)),
        dma((NCH, NZ)), dma((NCH, NZ)), dma((NCH, NZ)), dma((NCH, NZ)),
        dma((NZ,)), dma((NZ,)), dma((NX,)), dma((NX,)), dma((32,)), dma((32,)),
    ]
    mixed, logits = pl.pallas_call(
        kernel,
        out_shape=(
            jax.ShapeDtypeStruct((positions, channels), BF16),
            jax.ShapeDtypeStruct((1, classifier.shape[1]), F32),
        ),
        in_specs=[hbm, hbm, hbm, pl.BlockSpec(memory_space=pltpu.SMEM), hbm],
        out_specs=(hbm, pl.BlockSpec(memory_space=pltpu.VMEM)),
        scratch_shapes=scratch,
        compiler_params=pltpu.CompilerParams(
            collective_id=0, has_side_effects=True, vmem_limit_bytes=60 << 20
        ),
    )(
        inputs.reshape(positions, channels),
        keys_queries.reshape(positions, 2 * N),
        log_decay.reshape(heads, positions),
        skip,
        classifier,
    )
    mixed, logits = pl.pallas_call(
        hand_over,
        out_shape=(
            jax.ShapeDtypeStruct(mixed.shape, mixed.dtype),
            jax.ShapeDtypeStruct(logits.shape, logits.dtype),
        ),
        in_specs=[hbm, hbm],
        out_specs=(hbm, hbm),
        scratch_shapes=[
            pltpu.VMEM(mixed.shape, mixed.dtype),
            pltpu.VMEM(logits.shape, logits.dtype),
            dma((PIECES + 1,)),
            dma((PIECES + 1,)),
        ],
        compiler_params=pltpu.CompilerParams(vmem_limit_bytes=60 << 20),
    )(mixed, logits)
    return mixed.reshape(copies, positions, channels), logits


def solution(mesh):
    return jax.shard_map(
        local,
        mesh=mesh,
        in_specs=(
            P("fsdp", "seq", None),
            P("fsdp", "seq", None),
            P("fsdp", None, "seq"),
            P(),
            P("fsdp", None),
        ),
        out_specs=(P("fsdp", "seq", None), P("fsdp", None)),
        check_vma=False,
    )
```

```python
import jax
import jax.numpy as jnp
from jax import lax
from jax.experimental import pallas as pl
from jax.experimental.pallas import tpu as pltpu
from jax.sharding import PartitionSpec as P

MESH = pl.DeviceIdType.MESH
F32, BF16 = jnp.float32, jnp.bfloat16
HIGHEST = lax.Precision.HIGHEST

N = 128
G = 128
L = 128
NZ, NY, NC, NX = 8, 4, 2, 4
HEADS = 56
TILES = 28
M = TILES // NY
CHUNKS = ((0, 4), (4, 3))
NCH = len(CHUNKS)
EPS = 1e-06
PIECES = 8
FAR_Y = (2, 1, 3)
FAR_Z = (4, 5, 3, 6, 2, 7, 1)


def spread(x):
    return jnp.concatenate(
        [jnp.broadcast_to(x[m : m + 1, :], (8, L)) for m in range(M)], axis=0
    )


def kernel(
    v_hbm, kq_hbm, ld_hbm, skip_ref, cls_ref, mixed_ref, logits_ref,
    v_ref, kq_ref, ld_ref, out_ref, grow, local_out, table,
    decay_own, decay_pair, decay_chip, decay_plane,
    pair_factor, start_factor, plane_factor, plane_start,
    response, response_pair, chip_response, plane_response, axis_note, axis_notes,
    pool_own, pool_parts, pool_send, pool_axis, pool_sum, pool_plane,
    *rest,
):
    buffers = [rest[i * 12 : (i + 1) * 12] for i in range(NCH)]
    (in_s, out_s, pair_s, pair_r, plane_s, plane_r, axis_s, axis_r,
     back_s, back_r, note_s, note_r, table_s, table_r, small_s, small_r) = rest[NCH * 12 :]
    me, x = lax.axis_index("seq"), lax.axis_index("fsdp")
    c = lax.rem(me, NC)
    y = lax.rem(me // NC, NY)
    z = me // (NC * NY)
    other = 1 - c
    ys = [lax.rem(y + k, NY) for k in range(NY)]
    zs = [lax.rem(z + k, NZ) for k in range(NZ)]

    def at(z_, y_, c_):
        return {"seq": (z_ * NY + y_) * NC + c_}

    to_pair = at(z, y, other)
    to_y = [at(z, ys[k], c) for k in range(NY)]
    to_y_other = [at(z, ys[k], other) for k in range(NY)]
    to_z = [at(zs[k], y, c) for k in range(NZ)]
    to_x = [{"fsdp": lax.rem(x + k, NX)} for k in range(NX)]

    barrier = pltpu.get_barrier_semaphore()
    partners = to_z[1:] + to_y[1:] + to_y_other[1:] + to_x[1:] + [to_pair]
    for who in partners:
        pl.semaphore_signal(barrier, inc=1, device_id=who, device_id_type=MESH)

    loads = [
        pltpu.make_async_copy(src, dst, in_s.at[i])
        for i, (src, dst) in enumerate(
            ((ld_hbm, ld_ref), (kq_hbm, kq_ref), (v_hbm, v_ref), (cls_ref, table.at[x]))
        )
    ]
    for load in loads:
        load.start()

    sends = []

    def push(src, dst, send, recv, who):
        copy = pltpu.make_async_remote_copy(
            src_ref=src, dst_ref=dst, send_sem=send, recv_sem=recv,
            device_id=who, device_id_type=MESH,
        )
        copy.start()
        sends.append(copy)
        return copy

    loads[0].wait()
    left_half = lax.broadcasted_iota(jnp.int32, (1, L), 1) < 64
    for g in range(NY):
        even = jnp.sum(ld_ref[pl.ds(2 * M * g, M, stride=2), :], axis=1, keepdims=True)
        odd = jnp.sum(ld_ref[pl.ds(2 * M * g + 1, M, stride=2), :], axis=1, keepdims=True)
        decay_own[g, 0:M, :] = jnp.where(left_half, even, odd)
        decay_own[g, M:8, :] = jnp.zeros((8 - M, L), F32)

    row = lax.broadcasted_iota(jnp.int32, (G, G), 0)
    col = lax.broadcasted_iota(jnp.int32, (G, G), 1)
    causal = row >= col
    lower = jnp.where(causal, 1.0, 0.0).astype(F32)
    log_decay = ld_ref[...]
    cum_t = lax.dot_general(
        lower, log_decay, (((1,), (1,)), ((), ())), precision=HIGHEST, preferred_element_type=F32
    )
    loads[1].wait()
    keys = kq_ref[:, :N]
    queries = kq_ref[:, N:]
    keys_t = keys.T
    loads[2].wait()

    def pool_rows(responses, parts, first, count):
        whole = jnp.concatenate(responses, axis=1)
        high = whole.astype(BF16)
        low = (whole - high.astype(F32)).astype(BF16)
        both = jnp.concatenate([high, low], axis=0)
        made = []
        for m in range(count):
            t = 2 * (first + m)
            added = jnp.dot(both, jnp.concatenate(parts(m), axis=0), preferred_element_type=F32)
            added = added[0 : 2 * M, :] + added[2 * M : 4 * M, :]
            made.append(jnp.where(left_half, added[t : t + 1, :], added[t + 1 : t + 2, :]))
        return jnp.concatenate(made, axis=0)

    def state_of(i):
        first, count = CHUNKS[i]
        state = buffers[i][0]
        for g in range(NY):
            for m in range(count):
                j = g * M + first + m
                lanes = slice(j * L, (j + 1) * L)
                level = jnp.where(
                    left_half, cum_t[:, 2 * j : 2 * j + 1], cum_t[:, 2 * j + 1 : 2 * j + 2]
                )
                grow[j] = level
                weight = jnp.exp(level[G - 1 : G, :] - level)
                weighted = (v_ref[:, lanes].astype(F32) * weight).astype(BF16)
                value = jnp.dot(keys_t, weighted, preferred_element_type=F32).astype(BF16)
                for half in range(NC):
                    to = jnp.where(c == half, c, 2)
                    for b in range(NZ):
                        at_row = half * 64 + b * 8
                        state[to, g, b, m * 8 : m * 8 + 8, :] = value[at_row : at_row + 8, :]

    def send_half(i):
        state = buffers[i][0]
        return push(state.at[2], state.at[c], pair_s.at[i], pair_r.at[i], to_pair)

    def inside(g):
        scores = lax.dot_general(
            queries, keys, (((1,), (1,)), ((), ())), preferred_element_type=F32
        )
        scores = jnp.where(causal, scores, 0.0)
        for m in range(M):
            j = g * M + m
            lanes = slice(j * L, (j + 1) * L)
            parts = []
            for h in (2 * j, 2 * j + 1):
                gap = jnp.minimum(cum_t[:, h : h + 1] - cum[h : h + 1, :], 0.0)
                parts.append((scores * jnp.exp(gap)).astype(BF16))
            value = v_ref[:, lanes]
            zero = jnp.zeros_like(value)
            stacked = jnp.concatenate(
                [jnp.where(left_half, value, zero), jnp.where(left_half, zero, value)], axis=0
            )
            diagonal = jnp.dot(
                jnp.concatenate(parts, axis=1), stacked, preferred_element_type=F32
            )
            direct = jnp.where(left_half, skip_ref[2 * j], skip_ref[2 * j + 1])
            result = diagonal + direct * value.astype(F32)
            local_out[j] = result
            pool_own[g, m : m + 1, :] = jnp.sum(result, axis=0, keepdims=True)
            grow[j] = jnp.exp(grow[j])

    for g in range(NY):
        pool_own[g, M:8, :] = jnp.zeros((8 - M, L), F32)
    state_of(0)
    pl.semaphore_wait(barrier, len(partners))
    pair_decay = push(decay_own, decay_pair, small_s.at[0], small_r.at[0], to_pair)
    pair_copies = [send_half(0)]
    for i in range(1, NCH):
        state_of(i)
        pair_copies.append(send_half(i))
    response[0] = lax.dot_general(
        jnp.exp(cum_t), queries.astype(F32), (((0,), (0,)), ((), ())),
        precision=HIGHEST, preferred_element_type=F32,
    )
    response[1] = jnp.broadcast_to(jnp.sum(log_decay, axis=1, keepdims=True), (HEADS, L))
    pair_response = push(response, response_pair, small_s.at[1], small_r.at[1], to_pair)
    table_copies = [
        push(cls_ref, table.at[x], table_s.at[k], table_r.at[k], to_x[k]) for k in range(1, NX)
    ]
    cum = lax.dot_general(
        log_decay, lower, (((1,), (1,)), ((), ())), precision=HIGHEST, preferred_element_type=F32
    )
    inside(0)

    pair_decay.wait_recv()
    for g in range(NY):
        mine, theirs = decay_own[g], decay_pair[g]
        decay_chip[g] = mine + theirs
        pair_factor[g] = spread(jnp.exp(jnp.where(c == 0, theirs, mine)))
        start_factor[g] = spread(jnp.exp(jnp.where(c == 0, mine, theirs)))
    plane_decays = [
        push(decay_chip.at[ys[k]], decay_plane.at[y], small_s.at[1 + k], small_r.at[1 + k], to_y[k])
        for k in FAR_Y
    ]
    decay_plane[y] = decay_chip[y]

    plane_copies = [[] for _ in CHUNKS]
    for i, (first, count) in enumerate(CHUNKS):
        state, pair_total, plane_recv = buffers[i][:3]
        rows = slice(first * 8, (first + count) * 8)
        pair_copies[i].wait_recv()
        for k in (*FAR_Y, 0):
            g = ys[k]

            @pl.loop(0, NZ)
            def _(b, g=g, k=k):
                total = pair_factor[g, rows, :] * state[0, g, b].astype(F32) + state[1, g, b].astype(F32)
                if k == 0:
                    plane_recv[y, b] = total.astype(BF16)
                else:
                    pair_total[k, b] = total.astype(BF16)

            if k:
                plane_copies[i].append(
                    push(pair_total.at[k], plane_recv.at[y], plane_s.at[i, k], plane_r.at[i, k], to_y[k])
                )

    pair_response.wait_recv()
    resp_0 = jnp.where(c == 0, response[0], response_pair[0])
    resp_1 = jnp.where(c == 0, response_pair[0], response[0])
    resp_0 = resp_0 + jnp.exp(jnp.where(c == 0, response[1], response_pair[1])) * resp_1
    chip_decay = response[1] + response_pair[1]
    for g in range(NY):
        heads = slice(2 * M * g, 2 * M * (g + 1))
        chip_response[g, 0, 0 : 2 * M, :] = resp_0[heads, :]
        chip_response[g, 1, 0 : 2 * M, :] = chip_decay[heads, :]
        chip_response[g, :, 2 * M : 16, :] = jnp.zeros((2, 16 - 2 * M, L), F32)
    plane_responses = [
        push(chip_response.at[ys[k]], plane_response.at[y], small_s.at[4 + k], small_r.at[4 + k], to_y[k])
        for k in FAR_Y
    ]
    plane_response[y] = chip_response[y]
    inside(1)
    for copy in (*plane_decays, *plane_responses):
        copy.wait_recv()
    run = jnp.zeros((8, L), F32)
    run_head = jnp.zeros((16, L), F32)
    summed = jnp.zeros((16, L), F32)
    for k in range(NY):
        plane_factor[k] = spread(jnp.exp(decay_plane[k]))
        plane_start[k] = spread(jnp.exp(run))
        run = run + decay_plane[k]
        summed = summed + jnp.exp(run_head) * plane_response[k, 0]
        run_head = run_head + plane_response[k, 1]
    axis_note[0:8, :] = run
    axis_note[8:24, :] = summed
    axis_notes[z, 0:8, :] = run
    axis_notes[z, 8:24, :] = summed
    for k in FAR_Z:
        push(axis_note, axis_notes.at[z], note_s.at[k], note_r.at[z], to_z[k])
    inside(2)
    inside(3)
    mine_1 = jnp.where(c == 0, resp_1, pltpu.roll(resp_1, 64, 1))
    for i, (first, count) in enumerate(CHUNKS):
        state = buffers[i][0]
        for g in range(NY):
            group = pool_rows(
                [mine_1[2 * M * g : 2 * M * (g + 1), 0:64]],
                lambda m, g=g, state=state: [state[0, g, b, m * 8 : m * 8 + 8, :] for b in range(NZ)],
                first, count,
            )
            tiles = slice(first, first + count)
            pool_own[g, tiles, :] = pool_own[g, tiles, :] + group
    part_copies = [
        push(pool_own.at[ys[k]], pool_parts.at[y], small_s.at[14 + k], small_r.at[14 + k], to_y[k])
        for k in FAR_Y
    ]
    pool_parts[y] = pool_own[y]

    axis_copies = [[] for _ in CHUNKS]
    for i, (first, count) in enumerate(CHUNKS):
        plane_recv, plane_prefix, axis_send, axis_recv = buffers[i][2:6]
        rows = slice(first * 8, (first + count) * 8)
        for copy in plane_copies[i]:
            copy.wait_recv()
        for k in (*FAR_Z, 0):
            b = zs[k]
            total = jnp.zeros((count * 8, L), F32)
            for q in range(NY):
                plane_prefix[q, b] = total
                total = plane_factor[q, rows, :] * total + plane_recv[q, b].astype(F32)
            if k == 0:
                axis_recv[z] = total.astype(BF16)
            else:
                axis_send[k] = total.astype(BF16)
                axis_copies[i].append(
                    push(axis_send.at[k], axis_recv.at[z], axis_s.at[i, k], axis_r.at[i, z], to_z[k])
                )
    half_queries = jnp.where(
        c == 0, queries.astype(F32), pltpu.roll(queries.astype(F32), 64, 1)
    ).astype(BF16)

    def from_z(q):
        note = pltpu.make_async_remote_copy(
            src_ref=axis_note, dst_ref=axis_notes.at[q], send_sem=note_s.at[0], recv_sem=note_r.at[q],
            device_id=at(q, y, c), device_id_type=MESH,
        )
        return [note] + [
            pltpu.make_async_remote_copy(
                src_ref=buffers[i][4].at[0], dst_ref=buffers[i][5].at[q],
                send_sem=axis_s.at[i, 0], recv_sem=axis_r.at[i, q],
                device_id=at(q, y, c), device_id_type=MESH,
            )
            for i in range(NCH)
        ]

    def back(q):
        return [
            pltpu.make_async_remote_copy(
                src_ref=buffers[i][6].at[q], dst_ref=buffers[i][7].at[z],
                send_sem=back_s.at[i, q], recv_sem=back_r.at[i, z],
                device_id=at(q, y, c), device_id_type=MESH,
            )
            for i in range(NCH)
        ]

    def from_back(q, i):
        return pltpu.make_async_remote_copy(
            src_ref=buffers[i][6].at[0], dst_ref=buffers[i][7].at[q],
            send_sem=back_s.at[i, 0], recv_sem=back_r.at[i, q],
            device_id=at(q, y, c), device_id_type=MESH,
        )

    totals = [jnp.zeros((count * 8, L), F32) for _, count in CHUNKS]
    for q in range(NZ):
        for i in range(NCH):
            buffers[i][6][q] = totals[i].astype(BF16)
        if q > 0:

            @pl.when(z != q)
            def _(q=q):
                for copy in back(q):
                    copy.start()

            @pl.when(z == q)
            def _(q=q):
                for i in range(NCH):
                    buffers[i][7][q] = buffers[i][6][q]

        @pl.when(z != q)
        def _(q=q):
            for copy in from_z(q):
                copy.wait_recv()

        if q < NZ - 1:
            factor = spread(jnp.exp(axis_notes[q, 0:8, :]))
            for i, (first, count) in enumerate(CHUNKS):
                rows = slice(first * 8, (first + count) * 8)
                totals[i] = factor[rows, :] * totals[i] + buffers[i][5][q].astype(F32)

    @pl.when(z == 0)
    def _():
        for i in range(NCH):
            buffers[i][7][...] = jnp.zeros_like(buffers[i][7])

    for copy in part_copies:
        copy.wait_recv()
    my_half = [
        jnp.where(c == 0, plane_response[q, 0], pltpu.roll(plane_response[q, 0], 64, 1))[0 : 2 * M, 0:64]
        for q in range(1, NY)
    ]
    pool_rest = (pool_parts[0] + pool_parts[1]) + (pool_parts[2] + pool_parts[3])
    pool_tiles = []
    for i, (first, count) in enumerate(CHUNKS):
        plane_prefix = buffers[i][3]
        pool_tiles.append(
            pool_rows(
                my_half,
                lambda m, plane_prefix=plane_prefix: [
                    plane_prefix[q, b, m * 8 : m * 8 + 8, :].astype(BF16)
                    for q in range(1, NY)
                    for b in range(NZ)
                ],
                first, count,
            )
        )
    lane = lax.broadcasted_iota(jnp.int32, (16, L), 1) // 8
    my_rows = jnp.zeros((16, L), F32)
    for q in range(NZ):
        turned = pltpu.roll(axis_notes[q, 8:24, :], lax.rem(2 * L + 8 * q - 64 * c - 8 * z, L), 1)
        my_rows = my_rows + jnp.where(lane == q, turned, 0.0)
    for i, (first, count) in enumerate(CHUNKS):
        axis_prefix = buffers[i][6]
        pool_tiles[i] = pool_tiles[i] + pool_rows(
            [my_rows[0 : 2 * M, 0:64]],
            lambda m, axis_prefix=axis_prefix: [
                axis_prefix[q, m * 8 : m * 8 + 8, :] for q in range(NZ)
            ],
            first, count,
        )
    pool_send[...] = pool_rest + jnp.concatenate(
        [*pool_tiles, jnp.zeros((8 - M, L), F32)], axis=0
    )
    pool_axis[z] = pool_send[...]
    pool_copies = [
        push(pool_send, pool_axis.at[z], small_s.at[17 + k], small_r.at[17 + k], to_z[k])
        for k in FAR_Z
    ]

    earlier = list(sends)
    sends.clear()
    chip_copies = [[] for _ in CHUNKS]
    for i, (first, count) in enumerate(CHUNKS):
        plane_prefix = buffers[i][3]
        start_plane, start_send, start_chip = buffers[i][7:10]
        rows = slice(first * 8, (first + count) * 8)
        for q in range(NZ):

            @pl.when((z != q) & (z > 0))
            def _(q=q, i=i):
                from_back(q, i).wait_recv()

        for k in (*FAR_Y, 0):
            g = ys[k]

            @pl.loop(0, NZ)
            def _(b, g=g, k=k):
                start = plane_start[g, rows, :] * start_plane[b].astype(F32) + plane_prefix[g, b]
                if k == 0:
                    start_chip[y, b] = start.astype(BF16)
                else:
                    start_send[k, b] = start.astype(BF16)

            if k:
                chip_copies[i].append(
                    push(start_send.at[k], start_chip.at[y], plane_s.at[i, 3 + k], plane_r.at[i, 3 + k], to_y[k])
                )

    for copy in earlier:
        copy.wait_send()

    for copy in pool_copies:
        copy.wait_recv()
    total = pool_axis[0]
    for q in range(1, NZ):
        total = total + pool_axis[q]
    pool_sum[...] = total
    mine = pool_plane.at[y * NC + c]
    pool_plane[y * NC + c] = total
    last_copies = (
        [push(pool_sum, mine, small_s.at[24 + k], small_r.at[24 + k], to_y[k]) for k in FAR_Y]
        + [push(pool_sum, mine, small_s.at[27 + k], small_r.at[27 + k], to_y_other[k]) for k in FAR_Y]
        + [push(pool_sum, mine, small_s.at[31], small_r.at[31], to_pair)]
    )

    half_copies = []
    for i, (first, count) in enumerate(CHUNKS):
        state = buffers[i][0]
        start_chip, carried, carried_recv = buffers[i][9:12]
        rows = slice(first * 8, (first + count) * 8)
        for copy in chip_copies[i]:
            copy.wait_recv()

        @pl.loop(0, NY)
        def _(g):
            @pl.loop(0, NZ)
            def _(b):
                before = start_chip[g, b].astype(F32)
                after = start_factor[g, rows, :] * before + state[0, g, b].astype(F32)
                carried[0, g, b] = start_chip[g, b]
                carried[1, g, b] = after.astype(BF16)

        half_copies.append(
            push(carried.at[other], carried_recv, pair_s.at[NCH + i], pair_r.at[NCH + i], to_pair)
        )

    stores = []

    def final(i):
        first, count = CHUNKS[i]
        carried, carried_recv = buffers[i][10:12]
        half_copies[i].wait_recv()
        for g in range(NY):
            for m in range(count):
                j = g * M + first + m
                lanes = slice(j * L, (j + 1) * L)
                tile = slice(m * 8, m * 8 + 8)
                start = jnp.concatenate(
                    [carried[c, g, b, tile, :] for b in range(NZ)]
                    + [carried_recv[g, b, tile, :] for b in range(NZ)],
                    axis=0,
                )
                full = local_out[j] + grow[j] * jnp.dot(
                    half_queries, start, preferred_element_type=F32
                )
                out_ref[:, lanes] = full.astype(BF16)
            lanes = slice((g * M + first) * L, (g * M + first + count) * L)
            store = pltpu.make_async_copy(
                out_ref.at[:, lanes], mixed_ref.at[:, lanes], out_s.at[i * NY + g]
            )
            store.start()
            stores.append(store)

    for i in range(NCH):
        final(i)

    for copy in table_copies:
        copy.wait_recv()
    loads[3].wait()
    for copy in last_copies:
        copy.wait_recv()
    pooled = [
        (pool_plane[NC * g] + pool_plane[NC * g + 1]) / (G * NZ * NY * NC) for g in range(NY)
    ]
    square = sum(jnp.sum(p * p, keepdims=True) for p in pooled) / (TILES * L)
    scale = 1.0 / jnp.sqrt(square + EPS)
    wide = jnp.concatenate(
        [
            jnp.broadcast_to((pooled[g] * scale)[m : m + 1, :], (16, L)).astype(BF16)
            for g in range(NY)
            for m in range(M)
        ],
        axis=1,
    )
    classifier = table[...].reshape(TILES * L, L)
    logits = jnp.dot(wide, classifier, preferred_element_type=F32)
    logits_ref[...] = logits[0:1, :]

    for store in stores:
        store.wait()
    for q in range(1, NZ):

        @pl.when(z != q)
        def _(q=q):
            for copy in back(q):
                copy.wait_send()

    for copy in sends:
        copy.wait_send()


def hand_over(mixed_in, logits_in, mixed_out, logits_out, mixed, logits, in_sem, out_sem):
    pairs = [(logits_in, logits, logits_out)]
    for i in range(PIECES):
        rows = slice(i * (G // PIECES), (i + 1) * (G // PIECES))
        pairs.append((mixed_in.at[rows, :], mixed.at[rows, :], mixed_out.at[rows, :]))
    loads = [pltpu.make_async_copy(a, b, in_sem.at[i]) for i, (a, b, _) in enumerate(pairs)]
    stores = [pltpu.make_async_copy(b, c, out_sem.at[i]) for i, (_, b, c) in enumerate(pairs)]
    for load in loads:
        load.start()
    for load, store in zip(loads, stores):
        load.wait()
        store.start()
    for store in stores:
        store.wait()


def local(inputs, keys_queries, log_decay, skip, classifier):
    copies, positions, channels = inputs.shape
    heads = log_decay.shape[1]
    hbm = pl.BlockSpec(memory_space=pltpu.HBM)

    def chunk(count):
        slab = (NZ, count * 8, L)
        return [
            pltpu.VMEM((3, NY, *slab), BF16),
            pltpu.VMEM((NY, *slab), BF16),
            pltpu.VMEM((NY, *slab), BF16),
            pltpu.VMEM((NY, *slab), F32),
            pltpu.VMEM(slab, BF16),
            pltpu.VMEM(slab, BF16),
            pltpu.VMEM(slab, BF16),
            pltpu.VMEM(slab, BF16),
            pltpu.VMEM((NY, *slab), BF16),
            pltpu.VMEM((NY, *slab), BF16),
            pltpu.VMEM((NC, NY, *slab), BF16),
            pltpu.VMEM((NY, *slab), BF16),
        ]

    dma = pltpu.SemaphoreType.DMA
    scratch = [
        pltpu.VMEM((positions, channels), BF16),
        pltpu.VMEM((positions, 2 * N), BF16),
        pltpu.VMEM((heads, positions), F32),
        pltpu.VMEM((positions, channels), BF16),
        pltpu.VMEM((TILES, G, L), F32),
        pltpu.VMEM((TILES, G, L), F32),
        pltpu.VMEM((NX, *classifier.shape), BF16),
        pltpu.VMEM((NY, 8, L), F32),
        pltpu.VMEM((NY, 8, L), F32),
        pltpu.VMEM((NY, 8, L), F32),
        pltpu.VMEM((NY, 8, L), F32),
        pltpu.VMEM((NY, M * 8, L), F32),
        pltpu.VMEM((NY, M * 8, L), F32),
        pltpu.VMEM((NY, M * 8, L), F32),
        pltpu.VMEM((NY, M * 8, L), F32),
        pltpu.VMEM((2, HEADS, L), F32),
        pltpu.VMEM((2, HEADS, L), F32),
        pltpu.VMEM((NY, 2, 16, L), F32),
        pltpu.VMEM((NY, 2, 16, L), F32),
        pltpu.VMEM((24, L), F32),
        pltpu.VMEM((NZ, 24, L), F32),
        pltpu.VMEM((NY, 8, L), F32),
        pltpu.VMEM((NY, 8, L), F32),
        pltpu.VMEM((8, L), F32),
        pltpu.VMEM((NZ, 8, L), F32),
        pltpu.VMEM((8, L), F32),
        pltpu.VMEM((NY * NC, 8, L), F32),
        *[ref for _, count in CHUNKS for ref in chunk(count)],
        dma((4,)), dma((NCH * NY,)),
        dma((2 * NCH,)), dma((2 * NCH,)), dma((NCH, 7)), dma((NCH, 7)),
        dma((NCH, NZ)), dma((NCH, NZ)), dma((NCH, NZ)), dma((NCH, NZ)),
        dma((NZ,)), dma((NZ,)), dma((NX,)), dma((NX,)), dma((32,)), dma((32,)),
    ]
    mixed, logits = pl.pallas_call(
        kernel,
        out_shape=(
            jax.ShapeDtypeStruct((positions, channels), BF16),
            jax.ShapeDtypeStruct((1, classifier.shape[1]), F32),
        ),
        in_specs=[hbm, hbm, hbm, pl.BlockSpec(memory_space=pltpu.SMEM), hbm],
        out_specs=(hbm, pl.BlockSpec(memory_space=pltpu.VMEM)),
        scratch_shapes=scratch,
        compiler_params=pltpu.CompilerParams(
            collective_id=0, has_side_effects=True, vmem_limit_bytes=60 << 20
        ),
    )(
        inputs.reshape(positions, channels),
        keys_queries.reshape(positions, 2 * N),
        log_decay.reshape(heads, positions),
        skip,
        classifier,
    )
    mixed, logits = pl.pallas_call(
        hand_over,
        out_shape=(
            jax.ShapeDtypeStruct(mixed.shape, mixed.dtype),
            jax.ShapeDtypeStruct(logits.shape, logits.dtype),
        ),
        in_specs=[hbm, hbm],
        out_specs=(hbm, hbm),
        scratch_shapes=[
            pltpu.VMEM(mixed.shape, mixed.dtype),
            pltpu.VMEM(logits.shape, logits.dtype),
            dma((PIECES + 1,)),
            dma((PIECES + 1,)),
        ],
        compiler_params=pltpu.CompilerParams(vmem_limit_bytes=60 << 20),
    )(mixed, logits)
    return mixed.reshape(copies, positions, channels), logits


def solution(mesh):
    return jax.shard_map(
        local,
        mesh=mesh,
        in_specs=(
            P("fsdp", "seq", None),
            P("fsdp", "seq", None),
            P("fsdp", None, "seq"),
            P(),
            P("fsdp", None),
        ),
        out_specs=(P("fsdp", "seq", None), P("fsdp", None)),
        check_vma=False,
    )
```

```python
import jax
import jax.numpy as jnp
from jax import lax
from jax.experimental import pallas as pl
from jax.experimental.pallas import tpu as pltpu
from jax.sharding import PartitionSpec as P

MESH = pl.DeviceIdType.MESH
F32, BF16 = jnp.float32, jnp.bfloat16
HIGHEST = lax.Precision.HIGHEST

N = 128
G = 128
L = 128
NZ, NY, NC, NX = 8, 4, 2, 4
HEADS = 56
TILES = 28
M = TILES // NY
CHUNKS = ((0, 4), (4, 3))
NCH = len(CHUNKS)
EPS = 1e-06
PIECES = 8
FAR_Y = (2, 1, 3)
FAR_Z = (4, 5, 3, 6, 2, 7, 1)


def spread(x):
    return jnp.concatenate(
        [jnp.broadcast_to(x[m : m + 1, :], (8, L)) for m in range(M)], axis=0
    )


def kernel(
    v_hbm, kq_hbm, ld_hbm, skip_ref, cls_ref, mixed_ref, logits_ref,
    v_ref, kq_ref, ld_ref, out_ref, grow, local_out, table,
    decay_own, decay_pair, decay_chip, decay_plane,
    pair_factor, start_factor, plane_factor, plane_start,
    response, response_pair, chip_response, plane_response, axis_note, axis_notes,
    pool_own, pool_parts, pool_send, pool_axis, pool_sum, pool_plane,
    *rest,
):
    buffers = [rest[i * 12 : (i + 1) * 12] for i in range(NCH)]
    (in_s, out_s, pair_s, pair_r, plane_s, plane_r, axis_s, axis_r,
     back_s, back_r, note_s, note_r, table_s, table_r, small_s, small_r) = rest[NCH * 12 :]
    me, x = lax.axis_index("seq"), lax.axis_index("fsdp")
    c = lax.rem(me, NC)
    y = lax.rem(me // NC, NY)
    z = me // (NC * NY)
    other = 1 - c
    ys = [lax.rem(y + k, NY) for k in range(NY)]
    zs = [lax.rem(z + k, NZ) for k in range(NZ)]

    def at(z_, y_, c_):
        return {"seq": (z_ * NY + y_) * NC + c_}

    to_pair = at(z, y, other)
    to_y = [at(z, ys[k], c) for k in range(NY)]
    to_y_other = [at(z, ys[k], other) for k in range(NY)]
    to_z = [at(zs[k], y, c) for k in range(NZ)]
    to_x = [{"fsdp": lax.rem(x + k, NX)} for k in range(NX)]

    barrier = pltpu.get_barrier_semaphore()
    partners = to_z[1:] + to_y[1:] + to_y_other[1:] + to_x[1:] + [to_pair]
    for who in partners:
        pl.semaphore_signal(barrier, inc=1, device_id=who, device_id_type=MESH)

    loads = [
        pltpu.make_async_copy(src, dst, in_s.at[i])
        for i, (src, dst) in enumerate(
            ((ld_hbm, ld_ref), (kq_hbm, kq_ref), (cls_ref, table.at[x]))
        )
    ]
    value_loads = []
    for i, (first, count) in enumerate(CHUNKS):
        for g in range(NY):
            lanes = slice((g * M + first) * L, (g * M + first + count) * L)
            value_loads.append(
                pltpu.make_async_copy(
                    v_hbm.at[:, lanes], v_ref.at[:, lanes], in_s.at[3 + i * NY + g]
                )
            )
    for load in (*loads[:2], *value_loads, loads[2]):
        load.start()

    sends = []

    def push(src, dst, send, recv, who):
        copy = pltpu.make_async_remote_copy(
            src_ref=src, dst_ref=dst, send_sem=send, recv_sem=recv,
            device_id=who, device_id_type=MESH,
        )
        copy.start()
        sends.append(copy)
        return copy

    loads[0].wait()
    left_half = lax.broadcasted_iota(jnp.int32, (1, L), 1) < 64
    for g in range(NY):
        even = jnp.sum(ld_ref[pl.ds(2 * M * g, M, stride=2), :], axis=1, keepdims=True)
        odd = jnp.sum(ld_ref[pl.ds(2 * M * g + 1, M, stride=2), :], axis=1, keepdims=True)
        decay_own[g, 0:M, :] = jnp.where(left_half, even, odd)
        decay_own[g, M:8, :] = jnp.zeros((8 - M, L), F32)

    row = lax.broadcasted_iota(jnp.int32, (G, G), 0)
    col = lax.broadcasted_iota(jnp.int32, (G, G), 1)
    causal = row >= col
    log_decay = ld_ref[...]
    high = log_decay.astype(BF16)
    middle = (log_decay - high.astype(F32)).astype(BF16)
    low = (log_decay - high.astype(F32) - middle.astype(F32)).astype(BF16)
    decay_parts = jnp.concatenate([high, middle, low], axis=1)
    lower = jnp.where(causal, 1.0, 0.0).astype(BF16)
    lower = jnp.concatenate([lower] * 3, axis=1)
    cum_t = lax.dot_general(
        lower, decay_parts, (((1,), (1,)), ((), ())), preferred_element_type=F32
    )
    loads[1].wait()
    keys = kq_ref[:, :N]
    queries = kq_ref[:, N:]
    keys_t = keys.T

    def pool_rows(responses, parts, first, count):
        whole = jnp.concatenate(responses, axis=1)
        high = whole.astype(BF16)
        low = (whole - high.astype(F32)).astype(BF16)
        both = jnp.concatenate([high, low], axis=0)
        made = []
        for m in range(count):
            t = 2 * (first + m)
            added = jnp.dot(both, jnp.concatenate(parts(m), axis=0), preferred_element_type=F32)
            added = added[0 : 2 * M, :] + added[2 * M : 4 * M, :]
            made.append(jnp.where(left_half, added[t : t + 1, :], added[t + 1 : t + 2, :]))
        return jnp.concatenate(made, axis=0)

    def state_of(i):
        first, count = CHUNKS[i]
        state = buffers[i][0]
        for g in range(NY):
            value_loads[i * NY + g].wait()
            for m in range(count):
                j = g * M + first + m
                lanes = slice(j * L, (j + 1) * L)
                level = jnp.where(
                    left_half, cum_t[:, 2 * j : 2 * j + 1], cum_t[:, 2 * j + 1 : 2 * j + 2]
                )
                grow[j] = level
                weight = jnp.exp(level[G - 1 : G, :] - level)
                weighted = (v_ref[:, lanes].astype(F32) * weight).astype(BF16)
                value = jnp.dot(keys_t, weighted, preferred_element_type=F32).astype(BF16)
                for half in range(NC):
                    to = jnp.where(c == half, c, 2)
                    for b in range(NZ):
                        at_row = half * 64 + b * 8
                        state[to, g, b, m * 8 : m * 8 + 8, :] = value[at_row : at_row + 8, :]

    def send_half(i):
        state = buffers[i][0]
        return push(state.at[2], state.at[c], pair_s.at[i], pair_r.at[i], to_pair)

    def inside(g):
        scores = lax.dot_general(
            queries, keys, (((1,), (1,)), ((), ())), preferred_element_type=F32
        )
        scores = jnp.where(causal, scores, 0.0)
        for m in range(M):
            j = g * M + m
            lanes = slice(j * L, (j + 1) * L)
            parts = []
            for h in (2 * j, 2 * j + 1):
                gap = jnp.minimum(cum_t[:, h : h + 1] - cum[h : h + 1, :], 0.0)
                parts.append((scores * jnp.exp(gap)).astype(BF16))
            value = v_ref[:, lanes]
            zero = jnp.zeros_like(value)
            stacked = jnp.concatenate(
                [jnp.where(left_half, value, zero), jnp.where(left_half, zero, value)], axis=0
            )
            diagonal = jnp.dot(
                jnp.concatenate(parts, axis=1), stacked, preferred_element_type=F32
            )
            direct = jnp.where(left_half, skip_ref[2 * j], skip_ref[2 * j + 1])
            result = diagonal + direct * value.astype(F32)
            local_out[j] = result
            pool_own[g, m : m + 1, :] = jnp.sum(result, axis=0, keepdims=True)
            grow[j] = jnp.exp(grow[j])

    for g in range(NY):
        pool_own[g, M:8, :] = jnp.zeros((8 - M, L), F32)
    state_of(0)
    pl.semaphore_wait(barrier, len(partners))
    pair_decay = push(decay_own, decay_pair, small_s.at[0], small_r.at[0], to_pair)
    pair_copies = [send_half(0)]
    for i in range(1, NCH):
        state_of(i)
        pair_copies.append(send_half(i))
    response[0] = lax.dot_general(
        jnp.exp(cum_t), queries.astype(F32), (((0,), (0,)), ((), ())),
        precision=HIGHEST, preferred_element_type=F32,
    )
    response[1] = jnp.broadcast_to(jnp.sum(log_decay, axis=1, keepdims=True), (HEADS, L))
    pair_response = push(response, response_pair, small_s.at[1], small_r.at[1], to_pair)
    table_copies = [
        push(cls_ref, table.at[x], table_s.at[k], table_r.at[k], to_x[k]) for k in range(1, NX)
    ]
    cum = lax.dot_general(
        decay_parts, lower, (((1,), (1,)), ((), ())), preferred_element_type=F32
    )
    inside(0)

    pair_decay.wait_recv()
    for g in range(NY):
        mine, theirs = decay_own[g], decay_pair[g]
        decay_chip[g] = mine + theirs
        pair_factor[g] = spread(jnp.exp(jnp.where(c == 0, theirs, mine)))
        start_factor[g] = spread(jnp.exp(jnp.where(c == 0, mine, theirs)))
    plane_decays = [
        push(decay_chip.at[ys[k]], decay_plane.at[y], small_s.at[1 + k], small_r.at[1 + k], to_y[k])
        for k in FAR_Y
    ]
    decay_plane[y] = decay_chip[y]

    plane_copies = [[] for _ in CHUNKS]
    for i, (first, count) in enumerate(CHUNKS):
        state, pair_total, plane_recv = buffers[i][:3]
        rows = slice(first * 8, (first + count) * 8)
        pair_copies[i].wait_recv()
        for k in (*FAR_Y, 0):
            g = ys[k]

            @pl.loop(0, NZ, unroll=True)
            def _(b, g=g, k=k):
                total = pair_factor[g, rows, :] * state[0, g, b].astype(F32) + state[1, g, b].astype(F32)
                if k == 0:
                    plane_recv[y, b] = total.astype(BF16)
                else:
                    pair_total[k, b] = total.astype(BF16)

            if k:
                plane_copies[i].append(
                    push(pair_total.at[k], plane_recv.at[y], plane_s.at[i, k], plane_r.at[i, k], to_y[k])
                )

    pair_response.wait_recv()
    resp_0 = jnp.where(c == 0, response[0], response_pair[0])
    resp_1 = jnp.where(c == 0, response_pair[0], response[0])
    resp_0 = resp_0 + jnp.exp(jnp.where(c == 0, response[1], response_pair[1])) * resp_1
    chip_decay = response[1] + response_pair[1]
    for g in range(NY):
        heads = slice(2 * M * g, 2 * M * (g + 1))
        chip_response[g, 0, 0 : 2 * M, :] = resp_0[heads, :]
        chip_response[g, 1, 0 : 2 * M, :] = chip_decay[heads, :]
        chip_response[g, :, 2 * M : 16, :] = jnp.zeros((2, 16 - 2 * M, L), F32)
    plane_responses = [
        push(chip_response.at[ys[k]], plane_response.at[y], small_s.at[4 + k], small_r.at[4 + k], to_y[k])
        for k in FAR_Y
    ]
    plane_response[y] = chip_response[y]
    inside(1)
    for copy in (*plane_decays, *plane_responses):
        copy.wait_recv()
    run = jnp.zeros((8, L), F32)
    run_head = jnp.zeros((16, L), F32)
    summed = jnp.zeros((16, L), F32)
    for k in range(NY):
        plane_factor[k] = spread(jnp.exp(decay_plane[k]))
        plane_start[k] = spread(jnp.exp(run))
        run = run + decay_plane[k]
        summed = summed + jnp.exp(run_head) * plane_response[k, 0]
        run_head = run_head + plane_response[k, 1]
    axis_note[0:8, :] = run
    axis_note[8:24, :] = summed
    axis_notes[z, 0:8, :] = run
    axis_notes[z, 8:24, :] = summed
    for k in FAR_Z:
        push(axis_note, axis_notes.at[z], note_s.at[k], note_r.at[z], to_z[k])
    inside(2)
    inside(3)
    mine_1 = jnp.where(c == 0, resp_1, pltpu.roll(resp_1, 64, 1))
    for i, (first, count) in enumerate(CHUNKS):
        state = buffers[i][0]
        for g in range(NY):
            group = pool_rows(
                [mine_1[2 * M * g : 2 * M * (g + 1), 0:64]],
                lambda m, g=g, state=state: [state[0, g, b, m * 8 : m * 8 + 8, :] for b in range(NZ)],
                first, count,
            )
            tiles = slice(first, first + count)
            pool_own[g, tiles, :] = pool_own[g, tiles, :] + group
    part_copies = [
        push(pool_own.at[ys[k]], pool_parts.at[y], small_s.at[14 + k], small_r.at[14 + k], to_y[k])
        for k in FAR_Y
    ]
    pool_parts[y] = pool_own[y]

    axis_copies = [[] for _ in CHUNKS]
    for i, (first, count) in enumerate(CHUNKS):
        plane_recv, plane_prefix, axis_send, axis_recv = buffers[i][2:6]
        rows = slice(first * 8, (first + count) * 8)
        for copy in plane_copies[i]:
            copy.wait_recv()
        for k in (*FAR_Z, 0):
            b = zs[k]
            total = jnp.zeros((count * 8, L), F32)
            for q in range(NY):
                plane_prefix[q, b] = total
                total = plane_factor[q, rows, :] * total + plane_recv[q, b].astype(F32)
            if k == 0:
                axis_recv[z] = total.astype(BF16)
            else:
                axis_send[k] = total.astype(BF16)
                axis_copies[i].append(
                    push(axis_send.at[k], axis_recv.at[z], axis_s.at[i, k], axis_r.at[i, z], to_z[k])
                )
    half_queries = jnp.where(
        c == 0, queries.astype(F32), pltpu.roll(queries.astype(F32), 64, 1)
    ).astype(BF16)

    def from_z(q):
        note = pltpu.make_async_remote_copy(
            src_ref=axis_note, dst_ref=axis_notes.at[q], send_sem=note_s.at[0], recv_sem=note_r.at[q],
            device_id=at(q, y, c), device_id_type=MESH,
        )
        return [note] + [
            pltpu.make_async_remote_copy(
                src_ref=buffers[i][4].at[0], dst_ref=buffers[i][5].at[q],
                send_sem=axis_s.at[i, 0], recv_sem=axis_r.at[i, q],
                device_id=at(q, y, c), device_id_type=MESH,
            )
            for i in range(NCH)
        ]

    def back(q):
        return [
            pltpu.make_async_remote_copy(
                src_ref=buffers[i][6].at[q], dst_ref=buffers[i][7].at[z],
                send_sem=back_s.at[i, q], recv_sem=back_r.at[i, z],
                device_id=at(q, y, c), device_id_type=MESH,
            )
            for i in range(NCH)
        ]

    def from_back(q, i):
        return pltpu.make_async_remote_copy(
            src_ref=buffers[i][6].at[0], dst_ref=buffers[i][7].at[q],
            send_sem=back_s.at[i, 0], recv_sem=back_r.at[i, q],
            device_id=at(q, y, c), device_id_type=MESH,
        )

    totals = [jnp.zeros((count * 8, L), F32) for _, count in CHUNKS]
    for q in range(NZ):
        for i in range(NCH):
            buffers[i][6][q] = totals[i].astype(BF16)
        if q > 0:

            @pl.when(z != q)
            def _(q=q):
                for copy in back(q):
                    copy.start()

            @pl.when(z == q)
            def _(q=q):
                for i in range(NCH):
                    buffers[i][7][q] = buffers[i][6][q]

        @pl.when(z != q)
        def _(q=q):
            for copy in from_z(q):
                copy.wait_recv()

        if q < NZ - 1:
            factor = spread(jnp.exp(axis_notes[q, 0:8, :]))
            for i, (first, count) in enumerate(CHUNKS):
                rows = slice(first * 8, (first + count) * 8)
                totals[i] = factor[rows, :] * totals[i] + buffers[i][5][q].astype(F32)

    @pl.when(z == 0)
    def _():
        for i in range(NCH):
            buffers[i][7][...] = jnp.zeros_like(buffers[i][7])

    for copy in part_copies:
        copy.wait_recv()
    my_half = [
        jnp.where(c == 0, plane_response[q, 0], pltpu.roll(plane_response[q, 0], 64, 1))[0 : 2 * M, 0:64]
        for q in range(1, NY)
    ]
    pool_rest = (pool_parts[0] + pool_parts[1]) + (pool_parts[2] + pool_parts[3])
    pool_tiles = []
    for i, (first, count) in enumerate(CHUNKS):
        plane_prefix = buffers[i][3]
        pool_tiles.append(
            pool_rows(
                my_half,
                lambda m, plane_prefix=plane_prefix: [
                    plane_prefix[q, b, m * 8 : m * 8 + 8, :].astype(BF16)
                    for q in range(1, NY)
                    for b in range(NZ)
                ],
                first, count,
            )
        )
    lane = lax.broadcasted_iota(jnp.int32, (16, L), 1) // 8
    my_rows = jnp.zeros((16, L), F32)
    for q in range(NZ):
        turned = pltpu.roll(axis_notes[q, 8:24, :], lax.rem(2 * L + 8 * q - 64 * c - 8 * z, L), 1)
        my_rows = my_rows + jnp.where(lane == q, turned, 0.0)
    for i, (first, count) in enumerate(CHUNKS):
        axis_prefix = buffers[i][6]
        pool_tiles[i] = pool_tiles[i] + pool_rows(
            [my_rows[0 : 2 * M, 0:64]],
            lambda m, axis_prefix=axis_prefix: [
                axis_prefix[q, m * 8 : m * 8 + 8, :] for q in range(NZ)
            ],
            first, count,
        )
    pool_send[...] = pool_rest + jnp.concatenate(
        [*pool_tiles, jnp.zeros((8 - M, L), F32)], axis=0
    )
    pool_axis[z] = pool_send[...]
    pool_copies = [
        push(pool_send, pool_axis.at[z], small_s.at[17 + k], small_r.at[17 + k], to_z[k])
        for k in FAR_Z
    ]

    earlier = list(sends)
    sends.clear()
    chip_copies = [[] for _ in CHUNKS]
    for i, (first, count) in enumerate(CHUNKS):
        plane_prefix = buffers[i][3]
        start_plane, start_send, start_chip = buffers[i][7:10]
        rows = slice(first * 8, (first + count) * 8)
        for q in range(NZ):

            @pl.when((z != q) & (z > 0))
            def _(q=q, i=i):
                from_back(q, i).wait_recv()

        for k in (*FAR_Y, 0):
            g = ys[k]

            @pl.loop(0, NZ, unroll=True)
            def _(b, g=g, k=k):
                start = plane_start[g, rows, :] * start_plane[b].astype(F32) + plane_prefix[g, b]
                if k == 0:
                    start_chip[y, b] = start.astype(BF16)
                else:
                    start_send[k, b] = start.astype(BF16)

            if k:
                chip_copies[i].append(
                    push(start_send.at[k], start_chip.at[y], plane_s.at[i, 3 + k], plane_r.at[i, 3 + k], to_y[k])
                )

    for copy in earlier:
        copy.wait_send()

    for copy in pool_copies:
        copy.wait_recv()
    total = pool_axis[0]
    for q in range(1, NZ):
        total = total + pool_axis[q]
    pool_sum[...] = total
    mine = pool_plane.at[y * NC + c]
    pool_plane[y * NC + c] = total
    last_copies = (
        [push(pool_sum, mine, small_s.at[24 + k], small_r.at[24 + k], to_y[k]) for k in FAR_Y]
        + [push(pool_sum, mine, small_s.at[27 + k], small_r.at[27 + k], to_y_other[k]) for k in FAR_Y]
        + [push(pool_sum, mine, small_s.at[31], small_r.at[31], to_pair)]
    )

    half_copies = []
    for i, (first, count) in enumerate(CHUNKS):
        state = buffers[i][0]
        start_chip, carried, carried_recv = buffers[i][9:12]
        rows = slice(first * 8, (first + count) * 8)
        for copy in chip_copies[i]:
            copy.wait_recv()

        @pl.loop(0, NY)
        def _(g):
            @pl.loop(0, NZ, unroll=True)
            def _(b):
                before = start_chip[g, b].astype(F32)
                after = start_factor[g, rows, :] * before + state[0, g, b].astype(F32)
                carried[0, g, b] = start_chip[g, b]
                carried[1, g, b] = after.astype(BF16)

        half_copies.append(
            push(carried.at[other], carried_recv, pair_s.at[NCH + i], pair_r.at[NCH + i], to_pair)
        )

    stores = []

    def final(i):
        first, count = CHUNKS[i]
        carried, carried_recv = buffers[i][10:12]
        half_copies[i].wait_recv()
        for g in range(NY):
            for m in range(count):
                j = g * M + first + m
                lanes = slice(j * L, (j + 1) * L)
                tile = slice(m * 8, m * 8 + 8)
                start = jnp.concatenate(
                    [carried[c, g, b, tile, :] for b in range(NZ)]
                    + [carried_recv[g, b, tile, :] for b in range(NZ)],
                    axis=0,
                )
                full = local_out[j] + grow[j] * jnp.dot(
                    half_queries, start, preferred_element_type=F32
                )
                out_ref[:, lanes] = full.astype(BF16)
            lanes = slice((g * M + first) * L, (g * M + first + count) * L)
            store = pltpu.make_async_copy(
                out_ref.at[:, lanes], mixed_ref.at[:, lanes], out_s.at[i * NY + g]
            )
            store.start()
            stores.append(store)

    for i in range(NCH):
        final(i)

    for copy in table_copies:
        copy.wait_recv()
    loads[2].wait()
    for copy in last_copies:
        copy.wait_recv()
    pooled = [
        (pool_plane[NC * g] + pool_plane[NC * g + 1]) / (G * NZ * NY * NC) for g in range(NY)
    ]
    square = sum(jnp.sum(p * p, keepdims=True) for p in pooled) / (TILES * L)
    scale = 1.0 / jnp.sqrt(square + EPS)
    wide = jnp.concatenate(
        [
            jnp.broadcast_to((pooled[g] * scale)[m : m + 1, :], (16, L)).astype(BF16)
            for g in range(NY)
            for m in range(M)
        ],
        axis=1,
    )
    classifier = table[...].reshape(TILES * L, L)
    logits = jnp.dot(wide, classifier, preferred_element_type=F32)
    logits_ref[...] = logits[0:1, :]

    for store in stores:
        store.wait()
    for q in range(1, NZ):

        @pl.when(z != q)
        def _(q=q):
            for copy in back(q):
                copy.wait_send()

    for copy in sends:
        copy.wait_send()


def hand_over(mixed_in, logits_in, mixed_out, logits_out, mixed, logits, in_sem, out_sem):
    pairs = [(logits_in, logits, logits_out)]
    for i in range(PIECES):
        rows = slice(i * (G // PIECES), (i + 1) * (G // PIECES))
        pairs.append((mixed_in.at[rows, :], mixed.at[rows, :], mixed_out.at[rows, :]))
    loads = [pltpu.make_async_copy(a, b, in_sem.at[i]) for i, (a, b, _) in enumerate(pairs)]
    stores = [pltpu.make_async_copy(b, c, out_sem.at[i]) for i, (_, b, c) in enumerate(pairs)]
    for load in loads:
        load.start()
    for load, store in zip(loads, stores):
        load.wait()
        store.start()
    for store in stores:
        store.wait()


def local(inputs, keys_queries, log_decay, skip, classifier):
    copies, positions, channels = inputs.shape
    heads = log_decay.shape[1]
    hbm = pl.BlockSpec(memory_space=pltpu.HBM)

    def chunk(count):
        slab = (NZ, count * 8, L)
        return [
            pltpu.VMEM((3, NY, *slab), BF16),
            pltpu.VMEM((NY, *slab), BF16),
            pltpu.VMEM((NY, *slab), BF16),
            pltpu.VMEM((NY, *slab), F32),
            pltpu.VMEM(slab, BF16),
            pltpu.VMEM(slab, BF16),
            pltpu.VMEM(slab, BF16),
            pltpu.VMEM(slab, BF16),
            pltpu.VMEM((NY, *slab), BF16),
            pltpu.VMEM((NY, *slab), BF16),
            pltpu.VMEM((NC, NY, *slab), BF16),
            pltpu.VMEM((NY, *slab), BF16),
        ]

    dma = pltpu.SemaphoreType.DMA
    scratch = [
        pltpu.VMEM((positions, channels), BF16),
        pltpu.VMEM((positions, 2 * N), BF16),
        pltpu.VMEM((heads, positions), F32),
        pltpu.VMEM((positions, channels), BF16),
        pltpu.VMEM((TILES, G, L), F32),
        pltpu.VMEM((TILES, G, L), F32),
        pltpu.VMEM((NX, *classifier.shape), BF16),
        pltpu.VMEM((NY, 8, L), F32),
        pltpu.VMEM((NY, 8, L), F32),
        pltpu.VMEM((NY, 8, L), F32),
        pltpu.VMEM((NY, 8, L), F32),
        pltpu.VMEM((NY, M * 8, L), F32),
        pltpu.VMEM((NY, M * 8, L), F32),
        pltpu.VMEM((NY, M * 8, L), F32),
        pltpu.VMEM((NY, M * 8, L), F32),
        pltpu.VMEM((2, HEADS, L), F32),
        pltpu.VMEM((2, HEADS, L), F32),
        pltpu.VMEM((NY, 2, 16, L), F32),
        pltpu.VMEM((NY, 2, 16, L), F32),
        pltpu.VMEM((24, L), F32),
        pltpu.VMEM((NZ, 24, L), F32),
        pltpu.VMEM((NY, 8, L), F32),
        pltpu.VMEM((NY, 8, L), F32),
        pltpu.VMEM((8, L), F32),
        pltpu.VMEM((NZ, 8, L), F32),
        pltpu.VMEM((8, L), F32),
        pltpu.VMEM((NY * NC, 8, L), F32),
        *[ref for _, count in CHUNKS for ref in chunk(count)],
        dma((3 + NCH * NY,)), dma((NCH * NY,)),
        dma((2 * NCH,)), dma((2 * NCH,)), dma((NCH, 7)), dma((NCH, 7)),
        dma((NCH, NZ)), dma((NCH, NZ)), dma((NCH, NZ)), dma((NCH, NZ)),
        dma((NZ,)), dma((NZ,)), dma((NX,)), dma((NX,)), dma((32,)), dma((32,)),
    ]
    mixed, logits = pl.pallas_call(
        kernel,
        out_shape=(
            jax.ShapeDtypeStruct((positions, channels), BF16),
            jax.ShapeDtypeStruct((1, classifier.shape[1]), F32),
        ),
        in_specs=[hbm, hbm, hbm, pl.BlockSpec(memory_space=pltpu.SMEM), hbm],
        out_specs=(hbm, pl.BlockSpec(memory_space=pltpu.VMEM)),
        scratch_shapes=scratch,
        compiler_params=pltpu.CompilerParams(
            collective_id=0, has_side_effects=True, vmem_limit_bytes=60 << 20
        ),
    )(
        inputs.reshape(positions, channels),
        keys_queries.reshape(positions, 2 * N),
        log_decay.reshape(heads, positions),
        skip,
        classifier,
    )
    mixed, logits = pl.pallas_call(
        hand_over,
        out_shape=(
            jax.ShapeDtypeStruct(mixed.shape, mixed.dtype),
            jax.ShapeDtypeStruct(logits.shape, logits.dtype),
        ),
        in_specs=[hbm, hbm],
        out_specs=(hbm, hbm),
        scratch_shapes=[
            pltpu.VMEM(mixed.shape, mixed.dtype),
            pltpu.VMEM(logits.shape, logits.dtype),
            dma((PIECES + 1,)),
            dma((PIECES + 1,)),
        ],
        compiler_params=pltpu.CompilerParams(vmem_limit_bytes=60 << 20),
    )(mixed, logits)
    return mixed.reshape(copies, positions, channels), logits


def solution(mesh):
    return jax.shard_map(
        local,
        mesh=mesh,
        in_specs=(
            P("fsdp", "seq", None),
            P("fsdp", "seq", None),
            P("fsdp", None, "seq"),
            P(),
            P("fsdp", None),
        ),
        out_specs=(P("fsdp", "seq", None), P("fsdp", None)),
        check_vma=False,
    )
```

```python
import jax
import jax.numpy as jnp
from jax import lax
from jax.experimental import pallas as pl
from jax.experimental.pallas import tpu as pltpu
from jax.sharding import PartitionSpec as P

MESH = pl.DeviceIdType.MESH
F32, BF16 = jnp.float32, jnp.bfloat16
HIGHEST = lax.Precision.HIGHEST

N = 128
G = 128
L = 128
NZ, NY, NC, NX = 8, 4, 2, 4
HEADS = 56
TILES = 28
M = TILES // NY
CHUNKS = ((0, 4), (4, 3))
NCH = len(CHUNKS)
EPS = 1e-06
PIECES = 8
EARLY = NZ // 2
FAR_Y = (2, 1, 3)
FAR_Z = (4, 5, 3, 6, 2, 7, 1)


def spread(x):
    return jnp.concatenate(
        [jnp.broadcast_to(x[m : m + 1, :], (8, L)) for m in range(M)], axis=0
    )


def kernel(
    v_hbm, kq_hbm, ld_hbm, skip_ref, cls_ref, mixed_ref, logits_ref,
    v_ref, kq_ref, ld_ref, out_ref, grow, local_out, table,
    decay_own, decay_pair, decay_chip, decay_plane,
    pair_factor, start_factor, plane_factor, plane_start,
    response, response_pair, chip_response, plane_response, axis_note, axis_notes,
    pool_own, pool_parts, pool_send, pool_axis, pool_sum, pool_plane,
    *rest,
):
    buffers = [rest[i * 12 : (i + 1) * 12] for i in range(NCH)]
    (in_s, out_s, pair_s, pair_r, plane_s, plane_r, axis_s, axis_r,
     back_s, back_r, note_s, note_r, table_s, table_r, small_s, small_r) = rest[NCH * 12 :]
    me, x = lax.axis_index("seq"), lax.axis_index("fsdp")
    c = lax.rem(me, NC)
    y = lax.rem(me // NC, NY)
    z = me // (NC * NY)
    other = 1 - c
    ys = [lax.rem(y + k, NY) for k in range(NY)]
    zs = [lax.rem(z + k, NZ) for k in range(NZ)]

    def at(z_, y_, c_):
        return {"seq": (z_ * NY + y_) * NC + c_}

    to_pair = at(z, y, other)
    to_y = [at(z, ys[k], c) for k in range(NY)]
    to_y_other = [at(z, ys[k], other) for k in range(NY)]
    to_z = [at(zs[k], y, c) for k in range(NZ)]
    to_x = [{"fsdp": lax.rem(x + k, NX)} for k in range(NX)]

    barrier = pltpu.get_barrier_semaphore()
    partners = to_y[1:] + to_y_other[1:] + to_x[1:] + [to_pair]
    for who in partners:
        pl.semaphore_signal(barrier, inc=1, device_id=who, device_id_type=MESH)
    early = z < EARLY

    def greet_along_z(alike):
        for q in range(NZ):
            kind = early if q < EARLY else z >= EARLY
            chosen = kind & (z != q) if alike else jnp.logical_not(kind)

            @pl.when(chosen)
            def _(q=q):
                pl.semaphore_signal(
                    barrier, inc=1, device_id=at(q, y, c), device_id_type=MESH
                )

    greet_along_z(True)

    loads = [
        pltpu.make_async_copy(src, dst, in_s.at[i])
        for i, (src, dst) in enumerate(
            ((ld_hbm, ld_ref), (kq_hbm, kq_ref), (cls_ref, table.at[x]))
        )
    ]
    value_loads = []
    for i, (first, count) in enumerate(CHUNKS):
        for g in range(NY):
            lanes = slice((g * M + first) * L, (g * M + first + count) * L)
            value_loads.append(
                pltpu.make_async_copy(
                    v_hbm.at[:, lanes], v_ref.at[:, lanes], in_s.at[3 + i * NY + g]
                )
            )
    for load in (*loads[:2], *value_loads, loads[2]):
        load.start()

    sends = []

    def push(src, dst, send, recv, who):
        copy = pltpu.make_async_remote_copy(
            src_ref=src, dst_ref=dst, send_sem=send, recv_sem=recv,
            device_id=who, device_id_type=MESH,
        )
        copy.start()
        sends.append(copy)
        return copy

    loads[0].wait()
    left_half = lax.broadcasted_iota(jnp.int32, (1, L), 1) < 64
    for g in range(NY):
        even = jnp.sum(ld_ref[pl.ds(2 * M * g, M, stride=2), :], axis=1, keepdims=True)
        odd = jnp.sum(ld_ref[pl.ds(2 * M * g + 1, M, stride=2), :], axis=1, keepdims=True)
        decay_own[g, 0:M, :] = jnp.where(left_half, even, odd)
        decay_own[g, M:8, :] = jnp.zeros((8 - M, L), F32)

    row = lax.broadcasted_iota(jnp.int32, (G, G), 0)
    col = lax.broadcasted_iota(jnp.int32, (G, G), 1)
    causal = row >= col
    log_decay = ld_ref[...]
    high = log_decay.astype(BF16)
    middle = (log_decay - high.astype(F32)).astype(BF16)
    low = (log_decay - high.astype(F32) - middle.astype(F32)).astype(BF16)
    decay_parts = jnp.concatenate([high, middle, low], axis=1)
    lower = jnp.where(causal, 1.0, 0.0).astype(BF16)
    lower = jnp.concatenate([lower] * 3, axis=1)
    cum_t = lax.dot_general(
        lower, decay_parts, (((1,), (1,)), ((), ())), preferred_element_type=F32
    )
    loads[1].wait()
    keys = kq_ref[:, :N]
    queries = kq_ref[:, N:]
    keys_t = keys.T

    def pool_rows(responses, parts, first, count):
        whole = jnp.concatenate(responses, axis=1)
        high = whole.astype(BF16)
        low = (whole - high.astype(F32)).astype(BF16)
        both = jnp.concatenate([high, low], axis=0)
        made = []
        for m in range(count):
            t = 2 * (first + m)
            added = jnp.dot(both, jnp.concatenate(parts(m), axis=0), preferred_element_type=F32)
            added = added[0 : 2 * M, :] + added[2 * M : 4 * M, :]
            made.append(jnp.where(left_half, added[t : t + 1, :], added[t + 1 : t + 2, :]))
        return jnp.concatenate(made, axis=0)

    def state_of(i):
        first, count = CHUNKS[i]
        state = buffers[i][0]
        for g in range(NY):
            value_loads[i * NY + g].wait()
            for m in range(count):
                j = g * M + first + m
                lanes = slice(j * L, (j + 1) * L)
                level = jnp.where(
                    left_half, cum_t[:, 2 * j : 2 * j + 1], cum_t[:, 2 * j + 1 : 2 * j + 2]
                )
                grow[j] = level
                weight = jnp.exp(level[G - 1 : G, :] - level)
                weighted = (v_ref[:, lanes].astype(F32) * weight).astype(BF16)
                value = jnp.dot(keys_t, weighted, preferred_element_type=F32).astype(BF16)
                for half in range(NC):
                    to = jnp.where(c == half, c, 2)
                    for b in range(NZ):
                        at_row = half * 64 + b * 8
                        state[to, g, b, m * 8 : m * 8 + 8, :] = value[at_row : at_row + 8, :]

    def send_half(i):
        state = buffers[i][0]
        return push(state.at[2], state.at[c], pair_s.at[i], pair_r.at[i], to_pair)

    def inside(g):
        scores = lax.dot_general(
            queries, keys, (((1,), (1,)), ((), ())), preferred_element_type=F32
        )
        scores = jnp.where(causal, scores, 0.0)
        for m in range(M):
            j = g * M + m
            lanes = slice(j * L, (j + 1) * L)
            parts = []
            for h in (2 * j, 2 * j + 1):
                gap = jnp.minimum(cum_t[:, h : h + 1] - cum[h : h + 1, :], 0.0)
                parts.append((scores * jnp.exp(gap)).astype(BF16))
            value = v_ref[:, lanes]
            zero = jnp.zeros_like(value)
            stacked = jnp.concatenate(
                [jnp.where(left_half, value, zero), jnp.where(left_half, zero, value)], axis=0
            )
            diagonal = jnp.dot(
                jnp.concatenate(parts, axis=1), stacked, preferred_element_type=F32
            )
            direct = jnp.where(left_half, skip_ref[2 * j], skip_ref[2 * j + 1])
            result = diagonal + direct * value.astype(F32)
            local_out[j] = result
            pool_own[g, m : m + 1, :] = jnp.sum(result, axis=0, keepdims=True)
            grow[j] = jnp.exp(grow[j])

    for g in range(NY):
        pool_own[g, M:8, :] = jnp.zeros((8 - M, L), F32)
    state_of(0)
    met = len(partners) + EARLY - 1
    pl.semaphore_wait(barrier, jnp.where(early, met, met + EARLY))
    greet_along_z(False)
    pair_decay = push(decay_own, decay_pair, small_s.at[0], small_r.at[0], to_pair)
    pair_copies = [send_half(0)]
    for i in range(1, NCH):
        state_of(i)
        pair_copies.append(send_half(i))
    response[0] = lax.dot_general(
        jnp.exp(cum_t), queries.astype(F32), (((0,), (0,)), ((), ())),
        precision=HIGHEST, preferred_element_type=F32,
    )
    response[1] = jnp.broadcast_to(jnp.sum(log_decay, axis=1, keepdims=True), (HEADS, L))
    pair_response = push(response, response_pair, small_s.at[1], small_r.at[1], to_pair)
    cum = lax.dot_general(
        decay_parts, lower, (((1,), (1,)), ((), ())), preferred_element_type=F32
    )
    inside(0)

    pair_decay.wait_recv()
    for g in range(NY):
        mine, theirs = decay_own[g], decay_pair[g]
        decay_chip[g] = mine + theirs
        pair_factor[g] = spread(jnp.exp(jnp.where(c == 0, theirs, mine)))
        start_factor[g] = spread(jnp.exp(jnp.where(c == 0, mine, theirs)))
    plane_decays = [
        push(decay_chip.at[ys[k]], decay_plane.at[y], small_s.at[1 + k], small_r.at[1 + k], to_y[k])
        for k in FAR_Y
    ]
    decay_plane[y] = decay_chip[y]

    plane_copies = [[] for _ in CHUNKS]
    for i, (first, count) in enumerate(CHUNKS):
        state, pair_total, plane_recv = buffers[i][:3]
        rows = slice(first * 8, (first + count) * 8)
        pair_copies[i].wait_recv()
        for k in (*FAR_Y, 0):
            g = ys[k]

            @pl.loop(0, NZ, unroll=True)
            def _(b, g=g, k=k):
                total = pair_factor[g, rows, :] * state[0, g, b].astype(F32) + state[1, g, b].astype(F32)
                if k == 0:
                    plane_recv[y, b] = total.astype(BF16)
                else:
                    pair_total[k, b] = total.astype(BF16)

            if k:
                plane_copies[i].append(
                    push(pair_total.at[k], plane_recv.at[y], plane_s.at[i, k], plane_r.at[i, k], to_y[k])
                )

    pair_response.wait_recv()
    resp_0 = jnp.where(c == 0, response[0], response_pair[0])
    resp_1 = jnp.where(c == 0, response_pair[0], response[0])
    resp_0 = resp_0 + jnp.exp(jnp.where(c == 0, response[1], response_pair[1])) * resp_1
    chip_decay = response[1] + response_pair[1]
    for g in range(NY):
        heads = slice(2 * M * g, 2 * M * (g + 1))
        chip_response[g, 0, 0 : 2 * M, :] = resp_0[heads, :]
        chip_response[g, 1, 0 : 2 * M, :] = chip_decay[heads, :]
        chip_response[g, :, 2 * M : 16, :] = jnp.zeros((2, 16 - 2 * M, L), F32)
    plane_responses = [
        push(chip_response.at[ys[k]], plane_response.at[y], small_s.at[4 + k], small_r.at[4 + k], to_y[k])
        for k in FAR_Y
    ]
    plane_response[y] = chip_response[y]
    inside(1)
    for copy in (*plane_decays, *plane_responses):
        copy.wait_recv()
    run = jnp.zeros((8, L), F32)
    run_head = jnp.zeros((16, L), F32)
    summed = jnp.zeros((16, L), F32)
    for k in range(NY):
        plane_factor[k] = spread(jnp.exp(decay_plane[k]))
        plane_start[k] = spread(jnp.exp(run))
        run = run + decay_plane[k]
        summed = summed + jnp.exp(run_head) * plane_response[k, 0]
        run_head = run_head + plane_response[k, 1]
    axis_note[0:8, :] = run
    axis_note[8:24, :] = summed
    axis_notes[z, 0:8, :] = run
    axis_notes[z, 8:24, :] = summed

    @pl.when(early)
    def _():
        pl.semaphore_wait(barrier, NZ - EARLY)

    for k in FAR_Z:
        push(axis_note, axis_notes.at[z], note_s.at[k], note_r.at[z], to_z[k])
    table_copies = [
        push(cls_ref, table.at[x], table_s.at[k], table_r.at[k], to_x[k]) for k in range(1, NX)
    ]
    inside(2)
    inside(3)
    mine_1 = jnp.where(c == 0, resp_1, pltpu.roll(resp_1, 64, 1))
    for i, (first, count) in enumerate(CHUNKS):
        state = buffers[i][0]
        for g in range(NY):
            group = pool_rows(
                [mine_1[2 * M * g : 2 * M * (g + 1), 0:64]],
                lambda m, g=g, state=state: [state[0, g, b, m * 8 : m * 8 + 8, :] for b in range(NZ)],
                first, count,
            )
            tiles = slice(first, first + count)
            pool_own[g, tiles, :] = pool_own[g, tiles, :] + group
    part_copies = [
        push(pool_own.at[ys[k]], pool_parts.at[y], small_s.at[14 + k], small_r.at[14 + k], to_y[k])
        for k in FAR_Y
    ]
    pool_parts[y] = pool_own[y]

    axis_copies = [[] for _ in CHUNKS]
    for i, (first, count) in enumerate(CHUNKS):
        plane_recv, plane_prefix, axis_send, axis_recv = buffers[i][2:6]
        rows = slice(first * 8, (first + count) * 8)
        for copy in plane_copies[i]:
            copy.wait_recv()
        for k in (*FAR_Z, 0):
            b = zs[k]
            total = jnp.zeros((count * 8, L), F32)
            for q in range(NY):
                plane_prefix[q, b] = total
                total = plane_factor[q, rows, :] * total + plane_recv[q, b].astype(F32)
            if k == 0:
                axis_recv[z] = total.astype(BF16)
            else:
                axis_send[k] = total.astype(BF16)
                axis_copies[i].append(
                    push(axis_send.at[k], axis_recv.at[z], axis_s.at[i, k], axis_r.at[i, z], to_z[k])
                )
    half_queries = jnp.where(
        c == 0, queries.astype(F32), pltpu.roll(queries.astype(F32), 64, 1)
    ).astype(BF16)

    def from_z(q):
        note = pltpu.make_async_remote_copy(
            src_ref=axis_note, dst_ref=axis_notes.at[q], send_sem=note_s.at[0], recv_sem=note_r.at[q],
            device_id=at(q, y, c), device_id_type=MESH,
        )
        return [note] + [
            pltpu.make_async_remote_copy(
                src_ref=buffers[i][4].at[0], dst_ref=buffers[i][5].at[q],
                send_sem=axis_s.at[i, 0], recv_sem=axis_r.at[i, q],
                device_id=at(q, y, c), device_id_type=MESH,
            )
            for i in range(NCH)
        ]

    def back(q):
        return [
            pltpu.make_async_remote_copy(
                src_ref=buffers[i][6].at[q], dst_ref=buffers[i][7].at[z],
                send_sem=back_s.at[i, q], recv_sem=back_r.at[i, z],
                device_id=at(q, y, c), device_id_type=MESH,
            )
            for i in range(NCH)
        ]

    def from_back(q, i):
        return pltpu.make_async_remote_copy(
            src_ref=buffers[i][6].at[0], dst_ref=buffers[i][7].at[q],
            send_sem=back_s.at[i, 0], recv_sem=back_r.at[i, q],
            device_id=at(q, y, c), device_id_type=MESH,
        )

    totals = [jnp.zeros((count * 8, L), F32) for _, count in CHUNKS]
    for q in range(NZ):
        for i in range(NCH):
            buffers[i][6][q] = totals[i].astype(BF16)
        if q > 0:

            @pl.when(z != q)
            def _(q=q):
                for copy in back(q):
                    copy.start()

            @pl.when(z == q)
            def _(q=q):
                for i in range(NCH):
                    buffers[i][7][q] = buffers[i][6][q]

        if q == EARLY:
            for copy in part_copies:
                copy.wait_recv()
            my_half = [
                jnp.where(c == 0, plane_response[q, 0], pltpu.roll(plane_response[q, 0], 64, 1))[0 : 2 * M, 0:64]
                for q in range(1, NY)
            ]
            pool_rest = (pool_parts[0] + pool_parts[1]) + (pool_parts[2] + pool_parts[3])
            pool_tiles = []
            for i, (first, count) in enumerate(CHUNKS):
                plane_prefix = buffers[i][3]
                pool_tiles.append(
                    pool_rows(
                        my_half,
                        lambda m, plane_prefix=plane_prefix: [
                            plane_prefix[q, b, m * 8 : m * 8 + 8, :].astype(BF16)
                            for q in range(1, NY)
                            for b in range(NZ)
                        ],
                        first, count,
                    )
                )

        @pl.when(z != q)
        def _(q=q):
            for copy in from_z(q):
                copy.wait_recv()

        if q < NZ - 1:
            factor = spread(jnp.exp(axis_notes[q, 0:8, :]))
            for i, (first, count) in enumerate(CHUNKS):
                rows = slice(first * 8, (first + count) * 8)
                totals[i] = factor[rows, :] * totals[i] + buffers[i][5][q].astype(F32)

    @pl.when(z == 0)
    def _():
        for i in range(NCH):
            buffers[i][7][...] = jnp.zeros_like(buffers[i][7])

    lane = lax.broadcasted_iota(jnp.int32, (16, L), 1) // 8
    my_rows = jnp.zeros((16, L), F32)
    for q in range(NZ):
        turned = pltpu.roll(axis_notes[q, 8:24, :], lax.rem(2 * L + 8 * q - 64 * c - 8 * z, L), 1)
        my_rows = my_rows + jnp.where(lane == q, turned, 0.0)
    for i, (first, count) in enumerate(CHUNKS):
        axis_prefix = buffers[i][6]
        pool_tiles[i] = pool_tiles[i] + pool_rows(
            [my_rows[0 : 2 * M, 0:64]],
            lambda m, axis_prefix=axis_prefix: [
                axis_prefix[q, m * 8 : m * 8 + 8, :] for q in range(NZ)
            ],
            first, count,
        )
    pool_send[...] = pool_rest + jnp.concatenate(
        [*pool_tiles, jnp.zeros((8 - M, L), F32)], axis=0
    )
    pool_axis[z] = pool_send[...]
    pool_copies = [
        push(pool_send, pool_axis.at[z], small_s.at[17 + k], small_r.at[17 + k], to_z[k])
        for k in FAR_Z
    ]

    earlier = list(sends)
    sends.clear()
    chip_copies = [[] for _ in CHUNKS]
    for i, (first, count) in enumerate(CHUNKS):
        plane_prefix = buffers[i][3]
        start_plane, start_send, start_chip = buffers[i][7:10]
        rows = slice(first * 8, (first + count) * 8)
        for q in range(NZ):

            @pl.when((z != q) & (z > 0))
            def _(q=q, i=i):
                from_back(q, i).wait_recv()

        for k in (*FAR_Y, 0):
            g = ys[k]

            @pl.loop(0, NZ, unroll=True)
            def _(b, g=g, k=k):
                start = plane_start[g, rows, :] * start_plane[b].astype(F32) + plane_prefix[g, b]
                if k == 0:
                    start_chip[y, b] = start.astype(BF16)
                else:
                    start_send[k, b] = start.astype(BF16)

            if k:
                chip_copies[i].append(
                    push(start_send.at[k], start_chip.at[y], plane_s.at[i, 3 + k], plane_r.at[i, 3 + k], to_y[k])
                )

    for copy in earlier:
        copy.wait_send()

    for copy in pool_copies:
        copy.wait_recv()
    total = pool_axis[0]
    for q in range(1, NZ):
        total = total + pool_axis[q]
    pool_sum[...] = total
    mine = pool_plane.at[y * NC + c]
    pool_plane[y * NC + c] = total
    last_copies = (
        [push(pool_sum, mine, small_s.at[24 + k], small_r.at[24 + k], to_y[k]) for k in FAR_Y]
        + [push(pool_sum, mine, small_s.at[27 + k], small_r.at[27 + k], to_y_other[k]) for k in FAR_Y]
        + [push(pool_sum, mine, small_s.at[31], small_r.at[31], to_pair)]
    )

    half_copies = []
    for i, (first, count) in enumerate(CHUNKS):
        state = buffers[i][0]
        start_chip, carried, carried_recv = buffers[i][9:12]
        rows = slice(first * 8, (first + count) * 8)
        for copy in chip_copies[i]:
            copy.wait_recv()

        @pl.loop(0, NY)
        def _(g):
            @pl.loop(0, NZ, unroll=True)
            def _(b):
                before = start_chip[g, b].astype(F32)
                after = start_factor[g, rows, :] * before + state[0, g, b].astype(F32)
                carried[0, g, b] = start_chip[g, b]
                carried[1, g, b] = after.astype(BF16)

        half_copies.append(
            push(carried.at[other], carried_recv, pair_s.at[NCH + i], pair_r.at[NCH + i], to_pair)
        )

    stores = []

    def final(i):
        first, count = CHUNKS[i]
        carried, carried_recv = buffers[i][10:12]
        half_copies[i].wait_recv()
        for g in range(NY):
            for m in range(count):
                j = g * M + first + m
                lanes = slice(j * L, (j + 1) * L)
                tile = slice(m * 8, m * 8 + 8)
                start = jnp.concatenate(
                    [carried[c, g, b, tile, :] for b in range(NZ)]
                    + [carried_recv[g, b, tile, :] for b in range(NZ)],
                    axis=0,
                )
                full = local_out[j] + grow[j] * jnp.dot(
                    half_queries, start, preferred_element_type=F32
                )
                out_ref[:, lanes] = full.astype(BF16)
            lanes = slice((g * M + first) * L, (g * M + first + count) * L)
            store = pltpu.make_async_copy(
                out_ref.at[:, lanes], mixed_ref.at[:, lanes], out_s.at[i * NY + g]
            )
            store.start()
            stores.append(store)

    for i in range(NCH):
        final(i)

    for copy in table_copies:
        copy.wait_recv()
    loads[2].wait()
    for copy in last_copies:
        copy.wait_recv()
    pooled = [
        (pool_plane[NC * g] + pool_plane[NC * g + 1]) / (G * NZ * NY * NC) for g in range(NY)
    ]
    square = sum(jnp.sum(p * p, keepdims=True) for p in pooled) / (TILES * L)
    scale = 1.0 / jnp.sqrt(square + EPS)
    wide = jnp.concatenate(
        [
            jnp.broadcast_to((pooled[g] * scale)[m : m + 1, :], (16, L)).astype(BF16)
            for g in range(NY)
            for m in range(M)
        ],
        axis=1,
    )
    classifier = table[...].reshape(TILES * L, L)
    logits = jnp.dot(wide, classifier, preferred_element_type=F32)
    logits_ref[...] = logits[0:1, :]

    for store in stores:
        store.wait()
    for q in range(1, NZ):

        @pl.when(z != q)
        def _(q=q):
            for copy in back(q):
                copy.wait_send()

    for copy in sends:
        copy.wait_send()


def hand_over(mixed_in, logits_in, mixed_out, logits_out, mixed, logits, in_sem, out_sem):
    pairs = [(logits_in, logits, logits_out)]
    for i in range(PIECES):
        rows = slice(i * (G // PIECES), (i + 1) * (G // PIECES))
        pairs.append((mixed_in.at[rows, :], mixed.at[rows, :], mixed_out.at[rows, :]))
    loads = [pltpu.make_async_copy(a, b, in_sem.at[i]) for i, (a, b, _) in enumerate(pairs)]
    stores = [pltpu.make_async_copy(b, c, out_sem.at[i]) for i, (_, b, c) in enumerate(pairs)]
    for load in loads:
        load.start()
    for load, store in zip(loads, stores):
        load.wait()
        store.start()
    for store in stores:
        store.wait()


def local(inputs, keys_queries, log_decay, skip, classifier):
    copies, positions, channels = inputs.shape
    heads = log_decay.shape[1]
    hbm = pl.BlockSpec(memory_space=pltpu.HBM)

    def chunk(count):
        slab = (NZ, count * 8, L)
        return [
            pltpu.VMEM((3, NY, *slab), BF16),
            pltpu.VMEM((NY, *slab), BF16),
            pltpu.VMEM((NY, *slab), BF16),
            pltpu.VMEM((NY, *slab), F32),
            pltpu.VMEM(slab, BF16),
            pltpu.VMEM(slab, BF16),
            pltpu.VMEM(slab, BF16),
            pltpu.VMEM(slab, BF16),
            pltpu.VMEM((NY, *slab), BF16),
            pltpu.VMEM((NY, *slab), BF16),
            pltpu.VMEM((NC, NY, *slab), BF16),
            pltpu.VMEM((NY, *slab), BF16),
        ]

    dma = pltpu.SemaphoreType.DMA
    scratch = [
        pltpu.VMEM((positions, channels), BF16),
        pltpu.VMEM((positions, 2 * N), BF16),
        pltpu.VMEM((heads, positions), F32),
        pltpu.VMEM((positions, channels), BF16),
        pltpu.VMEM((TILES, G, L), F32),
        pltpu.VMEM((TILES, G, L), F32),
        pltpu.VMEM((NX, *classifier.shape), BF16),
        pltpu.VMEM((NY, 8, L), F32),
        pltpu.VMEM((NY, 8, L), F32),
        pltpu.VMEM((NY, 8, L), F32),
        pltpu.VMEM((NY, 8, L), F32),
        pltpu.VMEM((NY, M * 8, L), F32),
        pltpu.VMEM((NY, M * 8, L), F32),
        pltpu.VMEM((NY, M * 8, L), F32),
        pltpu.VMEM((NY, M * 8, L), F32),
        pltpu.VMEM((2, HEADS, L), F32),
        pltpu.VMEM((2, HEADS, L), F32),
        pltpu.VMEM((NY, 2, 16, L), F32),
        pltpu.VMEM((NY, 2, 16, L), F32),
        pltpu.VMEM((24, L), F32),
        pltpu.VMEM((NZ, 24, L), F32),
        pltpu.VMEM((NY, 8, L), F32),
        pltpu.VMEM((NY, 8, L), F32),
        pltpu.VMEM((8, L), F32),
        pltpu.VMEM((NZ, 8, L), F32),
        pltpu.VMEM((8, L), F32),
        pltpu.VMEM((NY * NC, 8, L), F32),
        *[ref for _, count in CHUNKS for ref in chunk(count)],
        dma((3 + NCH * NY,)), dma((NCH * NY,)),
        dma((2 * NCH,)), dma((2 * NCH,)), dma((NCH, 7)), dma((NCH, 7)),
        dma((NCH, NZ)), dma((NCH, NZ)), dma((NCH, NZ)), dma((NCH, NZ)),
        dma((NZ,)), dma((NZ,)), dma((NX,)), dma((NX,)), dma((32,)), dma((32,)),
    ]
    mixed, logits = pl.pallas_call(
        kernel,
        out_shape=(
            jax.ShapeDtypeStruct((positions, channels), BF16),
            jax.ShapeDtypeStruct((1, classifier.shape[1]), F32),
        ),
        in_specs=[hbm, hbm, hbm, pl.BlockSpec(memory_space=pltpu.SMEM), hbm],
        out_specs=(hbm, pl.BlockSpec(memory_space=pltpu.VMEM)),
        scratch_shapes=scratch,
        compiler_params=pltpu.CompilerParams(
            collective_id=0, has_side_effects=True, vmem_limit_bytes=60 << 20
        ),
    )(
        inputs.reshape(positions, channels),
        keys_queries.reshape(positions, 2 * N),
        log_decay.reshape(heads, positions),
        skip,
        classifier,
    )
    mixed, logits = pl.pallas_call(
        hand_over,
        out_shape=(
            jax.ShapeDtypeStruct(mixed.shape, mixed.dtype),
            jax.ShapeDtypeStruct(logits.shape, logits.dtype),
        ),
        in_specs=[hbm, hbm],
        out_specs=(hbm, hbm),
        scratch_shapes=[
            pltpu.VMEM(mixed.shape, mixed.dtype),
            pltpu.VMEM(logits.shape, logits.dtype),
            dma((PIECES + 1,)),
            dma((PIECES + 1,)),
        ],
        compiler_params=pltpu.CompilerParams(vmem_limit_bytes=60 << 20),
    )(mixed, logits)
    return mixed.reshape(copies, positions, channels), logits


def solution(mesh):
    return jax.shard_map(
        local,
        mesh=mesh,
        in_specs=(
            P("fsdp", "seq", None),
            P("fsdp", "seq", None),
            P("fsdp", None, "seq"),
            P(),
            P("fsdp", None),
        ),
        out_specs=(P("fsdp", "seq", None), P("fsdp", None)),
        check_vma=False,
    )
```

```python
import jax
import jax.numpy as jnp
from jax import lax
from jax.experimental import pallas as pl
from jax.experimental.pallas import tpu as pltpu
from jax.sharding import PartitionSpec as P

MESH = pl.DeviceIdType.MESH
F32, BF16 = jnp.float32, jnp.bfloat16
HIGHEST = lax.Precision.HIGHEST

N = 128
G = 128
L = 128
NZ, NY, NC, NX = 8, 4, 2, 4
HEADS = 56
TILES = 28
M = TILES // NY
CHUNKS = ((0, 4), (4, 3))
NCH = len(CHUNKS)
EPS = 1e-06
PIECES = 8
EARLY = 3
FAR_Y = (2, 1, 3)
FAR_Z = (4, 5, 3, 6, 2, 7, 1)


def spread(x):
    return jnp.concatenate(
        [jnp.broadcast_to(x[m : m + 1, :], (8, L)) for m in range(M)], axis=0
    )


def kernel(
    v_hbm, kq_hbm, ld_hbm, skip_ref, cls_ref, mixed_ref, logits_ref,
    v_ref, kq_ref, ld_ref, out_ref, grow, local_out, table,
    decay_own, decay_pair, decay_chip, decay_plane,
    pair_factor, start_factor, plane_factor, plane_start,
    response, response_pair, chip_response, plane_response, axis_note, axis_notes,
    pool_own, pool_parts, pool_send, pool_axis, pool_sum, pool_plane,
    *rest,
):
    buffers = [rest[i * 12 : (i + 1) * 12] for i in range(NCH)]
    (in_s, out_s, pair_s, pair_r, plane_s, plane_r, axis_s, axis_r,
     back_s, back_r, note_s, note_r, table_s, table_r, small_s, small_r) = rest[NCH * 12 :]
    me, x = lax.axis_index("seq"), lax.axis_index("fsdp")
    c = lax.rem(me, NC)
    y = lax.rem(me // NC, NY)
    z = me // (NC * NY)
    other = 1 - c
    ys = [lax.rem(y + k, NY) for k in range(NY)]
    zs = [lax.rem(z + k, NZ) for k in range(NZ)]

    def at(z_, y_, c_):
        return {"seq": (z_ * NY + y_) * NC + c_}

    to_pair = at(z, y, other)
    to_y = [at(z, ys[k], c) for k in range(NY)]
    to_y_other = [at(z, ys[k], other) for k in range(NY)]
    to_z = [at(zs[k], y, c) for k in range(NZ)]
    to_x = [{"fsdp": lax.rem(x + k, NX)} for k in range(NX)]

    barrier = pltpu.get_barrier_semaphore()
    partners = to_y[1:] + to_y_other[1:] + to_x[1:] + [to_pair]
    for who in partners:
        pl.semaphore_signal(barrier, inc=1, device_id=who, device_id_type=MESH)
    early = z < EARLY

    def greet_along_z(alike):
        for q in range(NZ):
            kind = early if q < EARLY else z >= EARLY
            chosen = kind & (z != q) if alike else jnp.logical_not(kind)

            @pl.when(chosen)
            def _(q=q):
                pl.semaphore_signal(
                    barrier, inc=1, device_id=at(q, y, c), device_id_type=MESH
                )

    greet_along_z(True)

    loads = [
        pltpu.make_async_copy(src, dst, in_s.at[i])
        for i, (src, dst) in enumerate(
            ((ld_hbm, ld_ref), (kq_hbm, kq_ref), (cls_ref, table.at[x]))
        )
    ]
    value_loads = []
    for i, (first, count) in enumerate(CHUNKS):
        for g in range(NY):
            lanes = slice((g * M + first) * L, (g * M + first + count) * L)
            value_loads.append(
                pltpu.make_async_copy(
                    v_hbm.at[:, lanes], v_ref.at[:, lanes], in_s.at[3 + i * NY + g]
                )
            )
    for load in (*loads[:2], *value_loads, loads[2]):
        load.start()

    sends = []

    def push(src, dst, send, recv, who):
        copy = pltpu.make_async_remote_copy(
            src_ref=src, dst_ref=dst, send_sem=send, recv_sem=recv,
            device_id=who, device_id_type=MESH,
        )
        copy.start()
        sends.append(copy)
        return copy

    loads[0].wait()
    left_half = lax.broadcasted_iota(jnp.int32, (1, L), 1) < 64
    for g in range(NY):
        even = jnp.sum(ld_ref[pl.ds(2 * M * g, M, stride=2), :], axis=1, keepdims=True)
        odd = jnp.sum(ld_ref[pl.ds(2 * M * g + 1, M, stride=2), :], axis=1, keepdims=True)
        decay_own[g, 0:M, :] = jnp.where(left_half, even, odd)
        decay_own[g, M:8, :] = jnp.zeros((8 - M, L), F32)

    row = lax.broadcasted_iota(jnp.int32, (G, G), 0)
    col = lax.broadcasted_iota(jnp.int32, (G, G), 1)
    causal = row >= col
    log_decay = ld_ref[...]
    high = log_decay.astype(BF16)
    middle = (log_decay - high.astype(F32)).astype(BF16)
    low = (log_decay - high.astype(F32) - middle.astype(F32)).astype(BF16)
    decay_parts = jnp.concatenate([high, middle, low], axis=1)
    lower = jnp.where(causal, 1.0, 0.0).astype(BF16)
    lower = jnp.concatenate([lower] * 3, axis=1)
    cum_t = lax.dot_general(
        lower, decay_parts, (((1,), (1,)), ((), ())), preferred_element_type=F32
    )
    loads[1].wait()
    keys = kq_ref[:, :N]
    queries = kq_ref[:, N:]
    keys_t = keys.T

    def pool_rows(responses, parts, first, count):
        whole = jnp.concatenate(responses, axis=1)
        high = whole.astype(BF16)
        low = (whole - high.astype(F32)).astype(BF16)
        both = jnp.concatenate([high, low], axis=0)
        made = []
        for m in range(count):
            t = 2 * (first + m)
            added = jnp.dot(both, jnp.concatenate(parts(m), axis=0), preferred_element_type=F32)
            added = added[0 : 2 * M, :] + added[2 * M : 4 * M, :]
            made.append(jnp.where(left_half, added[t : t + 1, :], added[t + 1 : t + 2, :]))
        return jnp.concatenate(made, axis=0)

    def state_of(i):
        first, count = CHUNKS[i]
        state = buffers[i][0]
        for g in range(NY):
            value_loads[i * NY + g].wait()
            for m in range(count):
                j = g * M + first + m
                lanes = slice(j * L, (j + 1) * L)
                level = jnp.where(
                    left_half, cum_t[:, 2 * j : 2 * j + 1], cum_t[:, 2 * j + 1 : 2 * j + 2]
                )
                grow[j] = level
                weight = jnp.exp(level[G - 1 : G, :] - level)
                weighted = (v_ref[:, lanes].astype(F32) * weight).astype(BF16)
                value = jnp.dot(keys_t, weighted, preferred_element_type=F32).astype(BF16)
                for half in range(NC):
                    to = jnp.where(c == half, c, 2)
                    for b in range(NZ):
                        at_row = half * 64 + b * 8
                        state[to, g, b, m * 8 : m * 8 + 8, :] = value[at_row : at_row + 8, :]

    def send_half(i):
        state = buffers[i][0]
        return push(state.at[2], state.at[c], pair_s.at[i], pair_r.at[i], to_pair)

    def inside(g):
        scores = lax.dot_general(
            queries, keys, (((1,), (1,)), ((), ())), preferred_element_type=F32
        )
        scores = jnp.where(causal, scores, 0.0)
        for m in range(M):
            j = g * M + m
            lanes = slice(j * L, (j + 1) * L)
            parts = []
            for h in (2 * j, 2 * j + 1):
                gap = jnp.minimum(cum_t[:, h : h + 1] - cum[h : h + 1, :], 0.0)
                parts.append((scores * jnp.exp(gap)).astype(BF16))
            value = v_ref[:, lanes]
            zero = jnp.zeros_like(value)
            stacked = jnp.concatenate(
                [jnp.where(left_half, value, zero), jnp.where(left_half, zero, value)], axis=0
            )
            diagonal = jnp.dot(
                jnp.concatenate(parts, axis=1), stacked, preferred_element_type=F32
            )
            direct = jnp.where(left_half, skip_ref[2 * j], skip_ref[2 * j + 1])
            result = diagonal + direct * value.astype(F32)
            local_out[j] = result
            pool_own[g, m : m + 1, :] = jnp.sum(result, axis=0, keepdims=True)
            grow[j] = jnp.exp(grow[j])

    for g in range(NY):
        pool_own[g, M:8, :] = jnp.zeros((8 - M, L), F32)
    state_of(0)
    met = len(partners)
    pl.semaphore_wait(barrier, jnp.where(early, met + EARLY - 1, met + NZ - 1))
    greet_along_z(False)
    pair_decay = push(decay_own, decay_pair, small_s.at[0], small_r.at[0], to_pair)
    pair_copies = [send_half(0)]
    for i in range(1, NCH):
        state_of(i)
        pair_copies.append(send_half(i))
    response[0] = lax.dot_general(
        jnp.exp(cum_t), queries.astype(F32), (((0,), (0,)), ((), ())),
        precision=HIGHEST, preferred_element_type=F32,
    )
    response[1] = jnp.broadcast_to(jnp.sum(log_decay, axis=1, keepdims=True), (HEADS, L))
    pair_response = push(response, response_pair, small_s.at[1], small_r.at[1], to_pair)
    cum = lax.dot_general(
        decay_parts, lower, (((1,), (1,)), ((), ())), preferred_element_type=F32
    )
    inside(0)

    pair_decay.wait_recv()
    for g in range(NY):
        mine, theirs = decay_own[g], decay_pair[g]
        decay_chip[g] = mine + theirs
        pair_factor[g] = spread(jnp.exp(jnp.where(c == 0, theirs, mine)))
        start_factor[g] = spread(jnp.exp(jnp.where(c == 0, mine, theirs)))
    plane_decays = [
        push(decay_chip.at[ys[k]], decay_plane.at[y], small_s.at[1 + k], small_r.at[1 + k], to_y[k])
        for k in FAR_Y
    ]
    decay_plane[y] = decay_chip[y]

    plane_copies = [[] for _ in CHUNKS]
    for i, (first, count) in enumerate(CHUNKS):
        state, pair_total, plane_recv = buffers[i][:3]
        rows = slice(first * 8, (first + count) * 8)
        pair_copies[i].wait_recv()
        for k in (*FAR_Y, 0):
            g = ys[k]

            @pl.loop(0, NZ, unroll=True)
            def _(b, g=g, k=k):
                total = pair_factor[g, rows, :] * state[0, g, b].astype(F32) + state[1, g, b].astype(F32)
                if k == 0:
                    plane_recv[y, b] = total.astype(BF16)
                else:
                    pair_total[k, b] = total.astype(BF16)

            if k:
                plane_copies[i].append(
                    push(pair_total.at[k], plane_recv.at[y], plane_s.at[i, k], plane_r.at[i, k], to_y[k])
                )

    pair_response.wait_recv()
    resp_0 = jnp.where(c == 0, response[0], response_pair[0])
    resp_1 = jnp.where(c == 0, response_pair[0], response[0])
    resp_0 = resp_0 + jnp.exp(jnp.where(c == 0, response[1], response_pair[1])) * resp_1
    chip_decay = response[1] + response_pair[1]
    for g in range(NY):
        heads = slice(2 * M * g, 2 * M * (g + 1))
        chip_response[g, 0, 0 : 2 * M, :] = resp_0[heads, :]
        chip_response[g, 1, 0 : 2 * M, :] = chip_decay[heads, :]
        chip_response[g, :, 2 * M : 16, :] = jnp.zeros((2, 16 - 2 * M, L), F32)
    plane_responses = [
        push(chip_response.at[ys[k]], plane_response.at[y], small_s.at[4 + k], small_r.at[4 + k], to_y[k])
        for k in FAR_Y
    ]
    plane_response[y] = chip_response[y]
    inside(1)
    for copy in (*plane_decays, *plane_responses):
        copy.wait_recv()
    run = jnp.zeros((8, L), F32)
    run_head = jnp.zeros((16, L), F32)
    summed = jnp.zeros((16, L), F32)
    for k in range(NY):
        plane_factor[k] = spread(jnp.exp(decay_plane[k]))
        plane_start[k] = spread(jnp.exp(run))
        run = run + decay_plane[k]
        summed = summed + jnp.exp(run_head) * plane_response[k, 0]
        run_head = run_head + plane_response[k, 1]
    axis_note[0:8, :] = run
    axis_note[8:24, :] = summed
    axis_notes[z, 0:8, :] = run
    axis_notes[z, 8:24, :] = summed

    @pl.when(early)
    def _():
        pl.semaphore_wait(barrier, NZ - EARLY)

    for k in FAR_Z:
        push(axis_note, axis_notes.at[z], note_s.at[k], note_r.at[z], to_z[k])
    table_copies = [
        push(cls_ref, table.at[x], table_s.at[k], table_r.at[k], to_x[k]) for k in range(1, NX)
    ]
    inside(2)
    inside(3)
    mine_1 = jnp.where(c == 0, resp_1, pltpu.roll(resp_1, 64, 1))
    for i, (first, count) in enumerate(CHUNKS):
        state = buffers[i][0]
        for g in range(NY):
            group = pool_rows(
                [mine_1[2 * M * g : 2 * M * (g + 1), 0:64]],
                lambda m, g=g, state=state: [state[0, g, b, m * 8 : m * 8 + 8, :] for b in range(NZ)],
                first, count,
            )
            tiles = slice(first, first + count)
            pool_own[g, tiles, :] = pool_own[g, tiles, :] + group
    part_copies = [
        push(pool_own.at[ys[k]], pool_parts.at[y], small_s.at[14 + k], small_r.at[14 + k], to_y[k])
        for k in FAR_Y
    ]
    pool_parts[y] = pool_own[y]

    axis_copies = [[] for _ in CHUNKS]
    for i, (first, count) in enumerate(CHUNKS):
        plane_recv, plane_prefix, axis_send, axis_recv = buffers[i][2:6]
        rows = slice(first * 8, (first + count) * 8)
        for copy in plane_copies[i]:
            copy.wait_recv()
        for k in (*FAR_Z, 0):
            b = zs[k]
            total = jnp.zeros((count * 8, L), F32)
            for q in range(NY):
                plane_prefix[q, b] = total
                total = plane_factor[q, rows, :] * total + plane_recv[q, b].astype(F32)
            if k == 0:
                axis_recv[z] = total.astype(BF16)
            else:
                axis_send[k] = total.astype(BF16)
                axis_copies[i].append(
                    push(axis_send.at[k], axis_recv.at[z], axis_s.at[i, k], axis_r.at[i, z], to_z[k])
                )
    half_queries = jnp.where(
        c == 0, queries.astype(F32), pltpu.roll(queries.astype(F32), 64, 1)
    ).astype(BF16)

    def from_z(q):
        note = pltpu.make_async_remote_copy(
            src_ref=axis_note, dst_ref=axis_notes.at[q], send_sem=note_s.at[0], recv_sem=note_r.at[q],
            device_id=at(q, y, c), device_id_type=MESH,
        )
        return [note] + [
            pltpu.make_async_remote_copy(
                src_ref=buffers[i][4].at[0], dst_ref=buffers[i][5].at[q],
                send_sem=axis_s.at[i, 0], recv_sem=axis_r.at[i, q],
                device_id=at(q, y, c), device_id_type=MESH,
            )
            for i in range(NCH)
        ]

    def back(q):
        return [
            pltpu.make_async_remote_copy(
                src_ref=buffers[i][6].at[q], dst_ref=buffers[i][7].at[z],
                send_sem=back_s.at[i, q], recv_sem=back_r.at[i, z],
                device_id=at(q, y, c), device_id_type=MESH,
            )
            for i in range(NCH)
        ]

    def from_back(q, i):
        return pltpu.make_async_remote_copy(
            src_ref=buffers[i][6].at[0], dst_ref=buffers[i][7].at[q],
            send_sem=back_s.at[i, 0], recv_sem=back_r.at[i, q],
            device_id=at(q, y, c), device_id_type=MESH,
        )

    totals = [jnp.zeros((count * 8, L), F32) for _, count in CHUNKS]
    for q in range(NZ):
        for i in range(NCH):
            buffers[i][6][q] = totals[i].astype(BF16)
        if q > 0:

            @pl.when(z != q)
            def _(q=q):
                for copy in back(q):
                    copy.start()

            @pl.when(z == q)
            def _(q=q):
                for i in range(NCH):
                    buffers[i][7][q] = buffers[i][6][q]

        if q == EARLY:
            for copy in part_copies:
                copy.wait_recv()
            my_half = [
                jnp.where(c == 0, plane_response[q, 0], pltpu.roll(plane_response[q, 0], 64, 1))[0 : 2 * M, 0:64]
                for q in range(1, NY)
            ]
            pool_rest = (pool_parts[0] + pool_parts[1]) + (pool_parts[2] + pool_parts[3])
            pool_tiles = []
            for i, (first, count) in enumerate(CHUNKS):
                plane_prefix = buffers[i][3]
                pool_tiles.append(
                    pool_rows(
                        my_half,
                        lambda m, plane_prefix=plane_prefix: [
                            plane_prefix[q, b, m * 8 : m * 8 + 8, :].astype(BF16)
                            for q in range(1, NY)
                            for b in range(NZ)
                        ],
                        first, count,
                    )
                )

        @pl.when(z != q)
        def _(q=q):
            for copy in from_z(q):
                copy.wait_recv()

        if q < NZ - 1:
            factor = spread(jnp.exp(axis_notes[q, 0:8, :]))
            for i, (first, count) in enumerate(CHUNKS):
                rows = slice(first * 8, (first + count) * 8)
                totals[i] = factor[rows, :] * totals[i] + buffers[i][5][q].astype(F32)

    @pl.when(z == 0)
    def _():
        for i in range(NCH):
            buffers[i][7][...] = jnp.zeros_like(buffers[i][7])

    lane = lax.broadcasted_iota(jnp.int32, (16, L), 1) // 8
    my_rows = jnp.zeros((16, L), F32)
    for q in range(NZ):
        turned = pltpu.roll(axis_notes[q, 8:24, :], lax.rem(2 * L + 8 * q - 64 * c - 8 * z, L), 1)
        my_rows = my_rows + jnp.where(lane == q, turned, 0.0)
    for i, (first, count) in enumerate(CHUNKS):
        axis_prefix = buffers[i][6]
        pool_tiles[i] = pool_tiles[i] + pool_rows(
            [my_rows[0 : 2 * M, 0:64]],
            lambda m, axis_prefix=axis_prefix: [
                axis_prefix[q, m * 8 : m * 8 + 8, :] for q in range(NZ)
            ],
            first, count,
        )
    pool_send[...] = pool_rest + jnp.concatenate(
        [*pool_tiles, jnp.zeros((8 - M, L), F32)], axis=0
    )
    pool_axis[z] = pool_send[...]
    pool_copies = [
        push(pool_send, pool_axis.at[z], small_s.at[17 + k], small_r.at[17 + k], to_z[k])
        for k in FAR_Z
    ]

    earlier = list(sends)
    sends.clear()
    chip_copies = [[] for _ in CHUNKS]
    for i, (first, count) in enumerate(CHUNKS):
        plane_prefix = buffers[i][3]
        start_plane, start_send, start_chip = buffers[i][7:10]
        rows = slice(first * 8, (first + count) * 8)
        for q in range(NZ):

            @pl.when((z != q) & (z > 0))
            def _(q=q, i=i):
                from_back(q, i).wait_recv()

        for k in (*FAR_Y, 0):
            g = ys[k]

            @pl.loop(0, NZ, unroll=True)
            def _(b, g=g, k=k):
                start = plane_start[g, rows, :] * start_plane[b].astype(F32) + plane_prefix[g, b]
                if k == 0:
                    start_chip[y, b] = start.astype(BF16)
                else:
                    start_send[k, b] = start.astype(BF16)

            if k:
                chip_copies[i].append(
                    push(start_send.at[k], start_chip.at[y], plane_s.at[i, 3 + k], plane_r.at[i, 3 + k], to_y[k])
                )

    for copy in earlier:
        copy.wait_send()

    for copy in pool_copies:
        copy.wait_recv()
    total = pool_axis[0]
    for q in range(1, NZ):
        total = total + pool_axis[q]
    pool_sum[...] = total
    mine = pool_plane.at[y * NC + c]
    pool_plane[y * NC + c] = total
    last_copies = (
        [push(pool_sum, mine, small_s.at[24 + k], small_r.at[24 + k], to_y[k]) for k in FAR_Y]
        + [push(pool_sum, mine, small_s.at[27 + k], small_r.at[27 + k], to_y_other[k]) for k in FAR_Y]
        + [push(pool_sum, mine, small_s.at[31], small_r.at[31], to_pair)]
    )

    half_copies = []
    for i, (first, count) in enumerate(CHUNKS):
        state = buffers[i][0]
        start_chip, carried, carried_recv = buffers[i][9:12]
        rows = slice(first * 8, (first + count) * 8)
        for copy in chip_copies[i]:
            copy.wait_recv()

        @pl.loop(0, NY)
        def _(g):
            @pl.loop(0, NZ, unroll=True)
            def _(b):
                before = start_chip[g, b].astype(F32)
                after = start_factor[g, rows, :] * before + state[0, g, b].astype(F32)
                carried[0, g, b] = start_chip[g, b]
                carried[1, g, b] = after.astype(BF16)

        half_copies.append(
            push(carried.at[other], carried_recv, pair_s.at[NCH + i], pair_r.at[NCH + i], to_pair)
        )

    stores = []

    def final(i):
        first, count = CHUNKS[i]
        carried, carried_recv = buffers[i][10:12]
        half_copies[i].wait_recv()
        for g in range(NY):
            for m in range(count):
                j = g * M + first + m
                lanes = slice(j * L, (j + 1) * L)
                tile = slice(m * 8, m * 8 + 8)
                start = jnp.concatenate(
                    [carried[c, g, b, tile, :] for b in range(NZ)]
                    + [carried_recv[g, b, tile, :] for b in range(NZ)],
                    axis=0,
                )
                full = local_out[j] + grow[j] * jnp.dot(
                    half_queries, start, preferred_element_type=F32
                )
                out_ref[:, lanes] = full.astype(BF16)
            lanes = slice((g * M + first) * L, (g * M + first + count) * L)
            store = pltpu.make_async_copy(
                out_ref.at[:, lanes], mixed_ref.at[:, lanes], out_s.at[i * NY + g]
            )
            store.start()
            stores.append(store)

    for i in range(NCH):
        final(i)

    for copy in table_copies:
        copy.wait_recv()
    loads[2].wait()
    for copy in last_copies:
        copy.wait_recv()
    pooled = [
        (pool_plane[NC * g] + pool_plane[NC * g + 1]) / (G * NZ * NY * NC) for g in range(NY)
    ]
    square = sum(jnp.sum(p * p, keepdims=True) for p in pooled) / (TILES * L)
    scale = 1.0 / jnp.sqrt(square + EPS)
    wide = jnp.concatenate(
        [
            jnp.broadcast_to((pooled[g] * scale)[m : m + 1, :], (16, L)).astype(BF16)
            for g in range(NY)
            for m in range(M)
        ],
        axis=1,
    )
    classifier = table[...].reshape(TILES * L, L)
    logits = jnp.dot(wide, classifier, preferred_element_type=F32)
    logits_ref[...] = logits[0:1, :]

    for store in stores:
        store.wait()
    for q in range(1, NZ):

        @pl.when(z != q)
        def _(q=q):
            for copy in back(q):
                copy.wait_send()

    for copy in sends:
        copy.wait_send()


def hand_over(mixed_in, logits_in, mixed_out, logits_out, mixed, logits, in_sem, out_sem):
    pairs = [(logits_in, logits, logits_out)]
    for i in range(PIECES):
        rows = slice(i * (G // PIECES), (i + 1) * (G // PIECES))
        pairs.append((mixed_in.at[rows, :], mixed.at[rows, :], mixed_out.at[rows, :]))
    loads = [pltpu.make_async_copy(a, b, in_sem.at[i]) for i, (a, b, _) in enumerate(pairs)]
    stores = [pltpu.make_async_copy(b, c, out_sem.at[i]) for i, (_, b, c) in enumerate(pairs)]
    for load in loads:
        load.start()
    for load, store in zip(loads, stores):
        load.wait()
        store.start()
    for store in stores:
        store.wait()


def local(inputs, keys_queries, log_decay, skip, classifier):
    copies, positions, channels = inputs.shape
    heads = log_decay.shape[1]
    hbm = pl.BlockSpec(memory_space=pltpu.HBM)

    def chunk(count):
        slab = (NZ, count * 8, L)
        return [
            pltpu.VMEM((3, NY, *slab), BF16),
            pltpu.VMEM((NY, *slab), BF16),
            pltpu.VMEM((NY, *slab), BF16),
            pltpu.VMEM((NY, *slab), F32),
            pltpu.VMEM(slab, BF16),
            pltpu.VMEM(slab, BF16),
            pltpu.VMEM(slab, BF16),
            pltpu.VMEM(slab, BF16),
            pltpu.VMEM((NY, *slab), BF16),
            pltpu.VMEM((NY, *slab), BF16),
            pltpu.VMEM((NC, NY, *slab), BF16),
            pltpu.VMEM((NY, *slab), BF16),
        ]

    dma = pltpu.SemaphoreType.DMA
    scratch = [
        pltpu.VMEM((positions, channels), BF16),
        pltpu.VMEM((positions, 2 * N), BF16),
        pltpu.VMEM((heads, positions), F32),
        pltpu.VMEM((positions, channels), BF16),
        pltpu.VMEM((TILES, G, L), F32),
        pltpu.VMEM((TILES, G, L), F32),
        pltpu.VMEM((NX, *classifier.shape), BF16),
        pltpu.VMEM((NY, 8, L), F32),
        pltpu.VMEM((NY, 8, L), F32),
        pltpu.VMEM((NY, 8, L), F32),
        pltpu.VMEM((NY, 8, L), F32),
        pltpu.VMEM((NY, M * 8, L), F32),
        pltpu.VMEM((NY, M * 8, L), F32),
        pltpu.VMEM((NY, M * 8, L), F32),
        pltpu.VMEM((NY, M * 8, L), F32),
        pltpu.VMEM((2, HEADS, L), F32),
        pltpu.VMEM((2, HEADS, L), F32),
        pltpu.VMEM((NY, 2, 16, L), F32),
        pltpu.VMEM((NY, 2, 16, L), F32),
        pltpu.VMEM((24, L), F32),
        pltpu.VMEM((NZ, 24, L), F32),
        pltpu.VMEM((NY, 8, L), F32),
        pltpu.VMEM((NY, 8, L), F32),
        pltpu.VMEM((8, L), F32),
        pltpu.VMEM((NZ, 8, L), F32),
        pltpu.VMEM((8, L), F32),
        pltpu.VMEM((NY * NC, 8, L), F32),
        *[ref for _, count in CHUNKS for ref in chunk(count)],
        dma((3 + NCH * NY,)), dma((NCH * NY,)),
        dma((2 * NCH,)), dma((2 * NCH,)), dma((NCH, 7)), dma((NCH, 7)),
        dma((NCH, NZ)), dma((NCH, NZ)), dma((NCH, NZ)), dma((NCH, NZ)),
        dma((NZ,)), dma((NZ,)), dma((NX,)), dma((NX,)), dma((32,)), dma((32,)),
    ]
    mixed, logits = pl.pallas_call(
        kernel,
        out_shape=(
            jax.ShapeDtypeStruct((positions, channels), BF16),
            jax.ShapeDtypeStruct((1, classifier.shape[1]), F32),
        ),
        in_specs=[hbm, hbm, hbm, pl.BlockSpec(memory_space=pltpu.SMEM), hbm],
        out_specs=(hbm, pl.BlockSpec(memory_space=pltpu.VMEM)),
        scratch_shapes=scratch,
        compiler_params=pltpu.CompilerParams(
            collective_id=0, has_side_effects=True, vmem_limit_bytes=60 << 20
        ),
    )(
        inputs.reshape(positions, channels),
        keys_queries.reshape(positions, 2 * N),
        log_decay.reshape(heads, positions),
        skip,
        classifier,
    )
    mixed, logits = pl.pallas_call(
        hand_over,
        out_shape=(
            jax.ShapeDtypeStruct(mixed.shape, mixed.dtype),
            jax.ShapeDtypeStruct(logits.shape, logits.dtype),
        ),
        in_specs=[hbm, hbm],
        out_specs=(hbm, hbm),
        scratch_shapes=[
            pltpu.VMEM(mixed.shape, mixed.dtype),
            pltpu.VMEM(logits.shape, logits.dtype),
            dma((PIECES + 1,)),
            dma((PIECES + 1,)),
        ],
        compiler_params=pltpu.CompilerParams(vmem_limit_bytes=60 << 20),
    )(mixed, logits)
    return mixed.reshape(copies, positions, channels), logits


def solution(mesh):
    return jax.shard_map(
        local,
        mesh=mesh,
        in_specs=(
            P("fsdp", "seq", None),
            P("fsdp", "seq", None),
            P("fsdp", None, "seq"),
            P(),
            P("fsdp", None),
        ),
        out_specs=(P("fsdp", "seq", None), P("fsdp", None)),
        check_vma=False,
    )
```

```python
import jax
import jax.numpy as jnp
from jax import lax
from jax.experimental import pallas as pl
from jax.experimental.pallas import tpu as pltpu
from jax.sharding import PartitionSpec as P

MESH = pl.DeviceIdType.MESH
F32, BF16 = jnp.float32, jnp.bfloat16
HIGHEST = lax.Precision.HIGHEST

N = 128
G = 128
L = 128
NZ, NY, NC, NX = 8, 4, 2, 4
HEADS = 56
TILES = 28
M = TILES // NY
CHUNKS = ((0, 4), (4, 3))
NCH = len(CHUNKS)
EPS = 1e-06
PIECES = 8
EARLY = 3
FAR_Y = (2, 1, 3)
FAR_Z = (4, 5, 3, 6, 2, 7, 1)


def spread(x):
    return jnp.concatenate(
        [jnp.broadcast_to(x[m : m + 1, :], (8, L)) for m in range(M)], axis=0
    )


def kernel(
    v_hbm, kq_hbm, ld_hbm, skip_ref, cls_ref, mixed_ref, logits_ref,
    v_ref, kq_ref, ld_ref, out_ref, grow, local_out, table,
    decay_own, decay_pair, decay_chip, decay_plane,
    pair_factor, start_factor, plane_factor, plane_start,
    response, response_pair, chip_response, plane_response, axis_note, axis_notes,
    pool_own, pool_parts, pool_send, pool_axis, pool_sum, pool_plane,
    *rest,
):
    buffers = [rest[i * 12 : (i + 1) * 12] for i in range(NCH)]
    (in_s, out_s, pair_s, pair_r, plane_s, plane_r, axis_s, axis_r,
     back_s, back_r, note_s, note_r, table_s, table_r, small_s, small_r) = rest[NCH * 12 :]
    me, x = lax.axis_index("seq"), lax.axis_index("fsdp")
    c = lax.rem(me, NC)
    y = lax.rem(me // NC, NY)
    z = me // (NC * NY)
    other = 1 - c
    ys = [lax.rem(y + k, NY) for k in range(NY)]
    zs = [lax.rem(z + k, NZ) for k in range(NZ)]

    def at(z_, y_, c_):
        return {"seq": (z_ * NY + y_) * NC + c_}

    to_pair = at(z, y, other)
    to_y = [at(z, ys[k], c) for k in range(NY)]
    to_y_other = [at(z, ys[k], other) for k in range(NY)]
    to_z = [at(zs[k], y, c) for k in range(NZ)]
    to_x = [{"fsdp": lax.rem(x + k, NX)} for k in range(NX)]

    barrier = pltpu.get_barrier_semaphore()
    partners = to_y[1:] + to_y_other[1:] + to_x[1:] + [to_pair]
    for who in partners:
        pl.semaphore_signal(barrier, inc=1, device_id=who, device_id_type=MESH)
    early = z < EARLY

    def greet_along_z(alike):
        for q in range(NZ):
            kind = early if q < EARLY else z >= EARLY
            chosen = kind & (z != q) if alike else jnp.logical_not(kind)

            @pl.when(chosen)
            def _(q=q):
                pl.semaphore_signal(
                    barrier, inc=1, device_id=at(q, y, c), device_id_type=MESH
                )

    greet_along_z(True)

    loads = [
        pltpu.make_async_copy(src, dst, in_s.at[i])
        for i, (src, dst) in enumerate(
            ((ld_hbm, ld_ref), (kq_hbm, kq_ref), (cls_ref, table.at[x]))
        )
    ]
    value_loads = []
    for i, (first, count) in enumerate(CHUNKS):
        for g in range(NY):
            lanes = slice((g * M + first) * L, (g * M + first + count) * L)
            value_loads.append(
                pltpu.make_async_copy(
                    v_hbm.at[:, lanes], v_ref.at[:, lanes], in_s.at[3 + i * NY + g]
                )
            )
    for load in (*loads[:2], *value_loads, loads[2]):
        load.start()

    sends = []

    def push(src, dst, send, recv, who):
        copy = pltpu.make_async_remote_copy(
            src_ref=src, dst_ref=dst, send_sem=send, recv_sem=recv,
            device_id=who, device_id_type=MESH,
        )
        copy.start()
        sends.append(copy)
        return copy

    loads[0].wait()
    left_half = lax.broadcasted_iota(jnp.int32, (1, L), 1) < 64
    for g in range(NY):
        even = jnp.sum(ld_ref[pl.ds(2 * M * g, M, stride=2), :], axis=1, keepdims=True)
        odd = jnp.sum(ld_ref[pl.ds(2 * M * g + 1, M, stride=2), :], axis=1, keepdims=True)
        decay_own[g, 0:M, :] = jnp.where(left_half, even, odd)
        decay_own[g, M:8, :] = jnp.zeros((8 - M, L), F32)

    row = lax.broadcasted_iota(jnp.int32, (G, G), 0)
    col = lax.broadcasted_iota(jnp.int32, (G, G), 1)
    causal = row >= col
    log_decay = ld_ref[...]
    high = log_decay.astype(BF16)
    middle = (log_decay - high.astype(F32)).astype(BF16)
    low = (log_decay - high.astype(F32) - middle.astype(F32)).astype(BF16)
    decay_parts = jnp.concatenate([high, middle, low], axis=1)
    lower = jnp.where(causal, 1.0, 0.0).astype(BF16)
    lower = jnp.concatenate([lower] * 3, axis=1)
    cum_t = lax.dot_general(
        lower, decay_parts, (((1,), (1,)), ((), ())), preferred_element_type=F32
    )
    loads[1].wait()
    keys = kq_ref[:, :N]
    queries = kq_ref[:, N:]
    keys_t = keys.T

    def pool_rows(responses, parts, first, count):
        whole = jnp.concatenate(responses, axis=1)
        high = whole.astype(BF16)
        low = (whole - high.astype(F32)).astype(BF16)
        both = jnp.concatenate([high, low], axis=0)
        made = []
        for m in range(count):
            t = 2 * (first + m)
            added = jnp.dot(both, jnp.concatenate(parts(m), axis=0), preferred_element_type=F32)
            added = added[0 : 2 * M, :] + added[2 * M : 4 * M, :]
            made.append(jnp.where(left_half, added[t : t + 1, :], added[t + 1 : t + 2, :]))
        return jnp.concatenate(made, axis=0)

    def state_of(i):
        first, count = CHUNKS[i]
        state = buffers[i][0]
        for g in range(NY):
            value_loads[i * NY + g].wait()
            for m in range(count):
                j = g * M + first + m
                lanes = slice(j * L, (j + 1) * L)
                level = jnp.where(
                    left_half, cum_t[:, 2 * j : 2 * j + 1], cum_t[:, 2 * j + 1 : 2 * j + 2]
                )
                grow[j] = level
                weight = jnp.exp(level[G - 1 : G, :] - level)
                weighted = (v_ref[:, lanes].astype(F32) * weight).astype(BF16)
                value = jnp.dot(keys_t, weighted, preferred_element_type=F32).astype(BF16)
                for half in range(NC):
                    to = jnp.where(c == half, c, 2)
                    for b in range(NZ):
                        at_row = half * 64 + b * 8
                        state[to, g, b, m * 8 : m * 8 + 8, :] = value[at_row : at_row + 8, :]

    def send_half(i):
        state = buffers[i][0]
        return push(state.at[2], state.at[c], pair_s.at[i], pair_r.at[i], to_pair)

    def inside(g):
        scores = lax.dot_general(
            queries, keys, (((1,), (1,)), ((), ())), preferred_element_type=F32
        )
        scores = jnp.where(causal, scores, 0.0)
        for m in range(M):
            j = g * M + m
            lanes = slice(j * L, (j + 1) * L)
            parts = []
            for h in (2 * j, 2 * j + 1):
                gap = jnp.minimum(cum_t[:, h : h + 1] - cum[h : h + 1, :], 0.0)
                parts.append((scores * jnp.exp(gap)).astype(BF16))
            value = v_ref[:, lanes]
            zero = jnp.zeros_like(value)
            stacked = jnp.concatenate(
                [jnp.where(left_half, value, zero), jnp.where(left_half, zero, value)], axis=0
            )
            diagonal = jnp.dot(
                jnp.concatenate(parts, axis=1), stacked, preferred_element_type=F32
            )
            direct = jnp.where(left_half, skip_ref[2 * j], skip_ref[2 * j + 1])
            result = diagonal + direct * value.astype(F32)
            local_out[j] = result
            pool_own[g, m : m + 1, :] = jnp.sum(result, axis=0, keepdims=True)
            grow[j] = jnp.exp(grow[j])

    for g in range(NY):
        pool_own[g, M:8, :] = jnp.zeros((8 - M, L), F32)
    state_of(0)
    met = len(partners)
    pl.semaphore_wait(barrier, jnp.where(early, met + EARLY - 1, met + NZ - 1))
    greet_along_z(False)
    pair_decay = push(decay_own, decay_pair, small_s.at[0], small_r.at[0], to_pair)
    pair_copies = [send_half(0)]
    for i in range(1, NCH):
        state_of(i)
        pair_copies.append(send_half(i))
    response[0] = lax.dot_general(
        jnp.exp(cum_t), queries.astype(F32), (((0,), (0,)), ((), ())),
        precision=HIGHEST, preferred_element_type=F32,
    )
    response[1] = jnp.broadcast_to(jnp.sum(log_decay, axis=1, keepdims=True), (HEADS, L))
    pair_response = push(response, response_pair, small_s.at[1], small_r.at[1], to_pair)
    cum = lax.dot_general(
        decay_parts, lower, (((1,), (1,)), ((), ())), preferred_element_type=F32
    )
    inside(0)

    pair_decay.wait_recv()
    for g in range(NY):
        mine, theirs = decay_own[g], decay_pair[g]
        decay_chip[g] = mine + theirs
        pair_factor[g] = spread(jnp.exp(jnp.where(c == 0, theirs, mine)))
        start_factor[g] = spread(jnp.exp(jnp.where(c == 0, mine, theirs)))
    plane_decays = [
        push(decay_chip.at[ys[k]], decay_plane.at[y], small_s.at[1 + k], small_r.at[1 + k], to_y[k])
        for k in FAR_Y
    ]
    decay_plane[y] = decay_chip[y]

    plane_copies = [[] for _ in CHUNKS]
    for i, (first, count) in enumerate(CHUNKS):
        state, pair_total, plane_recv = buffers[i][:3]
        rows = slice(first * 8, (first + count) * 8)
        pair_copies[i].wait_recv()
        for k in (*FAR_Y, 0):
            g = ys[k]

            @pl.loop(0, NZ, unroll=True)
            def _(b, g=g, k=k):
                total = pair_factor[g, rows, :] * state[0, g, b].astype(F32) + state[1, g, b].astype(F32)
                if k == 0:
                    plane_recv[y, b] = total.astype(BF16)
                else:
                    pair_total[k, b] = total.astype(BF16)

            if k:
                plane_copies[i].append(
                    push(pair_total.at[k], plane_recv.at[y], plane_s.at[i, k], plane_r.at[i, k], to_y[k])
                )

    pair_response.wait_recv()
    resp_0 = jnp.where(c == 0, response[0], response_pair[0])
    resp_1 = jnp.where(c == 0, response_pair[0], response[0])
    resp_0 = resp_0 + jnp.exp(jnp.where(c == 0, response[1], response_pair[1])) * resp_1
    chip_decay = response[1] + response_pair[1]
    for g in range(NY):
        heads = slice(2 * M * g, 2 * M * (g + 1))
        chip_response[g, 0, 0 : 2 * M, :] = resp_0[heads, :]
        chip_response[g, 1, 0 : 2 * M, :] = chip_decay[heads, :]
        chip_response[g, :, 2 * M : 16, :] = jnp.zeros((2, 16 - 2 * M, L), F32)
    plane_responses = [
        push(chip_response.at[ys[k]], plane_response.at[y], small_s.at[4 + k], small_r.at[4 + k], to_y[k])
        for k in FAR_Y
    ]
    plane_response[y] = chip_response[y]
    inside(1)
    for copy in (*plane_decays, *plane_responses):
        copy.wait_recv()
    run = jnp.zeros((8, L), F32)
    run_head = jnp.zeros((16, L), F32)
    summed = jnp.zeros((16, L), F32)
    for k in range(NY):
        plane_factor[k] = spread(jnp.exp(decay_plane[k]))
        plane_start[k] = spread(jnp.exp(run))
        run = run + decay_plane[k]
        summed = summed + jnp.exp(run_head) * plane_response[k, 0]
        run_head = run_head + plane_response[k, 1]
    axis_note[0:8, :] = run
    axis_note[8:24, :] = summed
    axis_notes[z, 0:8, :] = run
    axis_notes[z, 8:24, :] = summed

    @pl.when(early)
    def _():
        pl.semaphore_wait(barrier, NZ - EARLY)

    for k in FAR_Z:
        push(axis_note, axis_notes.at[z], note_s.at[k], note_r.at[z], to_z[k])
    table_copies = [
        push(cls_ref, table.at[x], table_s.at[k], table_r.at[k], to_x[k]) for k in range(1, NX)
    ]
    inside(2)
    inside(3)
    mine_1 = jnp.where(c == 0, resp_1, pltpu.roll(resp_1, 64, 1))
    for i, (first, count) in enumerate(CHUNKS):
        state = buffers[i][0]
        for g in range(NY):
            group = pool_rows(
                [mine_1[2 * M * g : 2 * M * (g + 1), 0:64]],
                lambda m, g=g, state=state: [state[0, g, b, m * 8 : m * 8 + 8, :] for b in range(NZ)],
                first, count,
            )
            tiles = slice(first, first + count)
            pool_own[g, tiles, :] = pool_own[g, tiles, :] + group
    part_copies = [
        push(pool_own.at[ys[k]], pool_parts.at[y], small_s.at[14 + k], small_r.at[14 + k], to_y[k])
        for k in FAR_Y
    ]
    pool_parts[y] = pool_own[y]

    axis_copies = [[] for _ in CHUNKS]
    for i, (first, count) in enumerate(CHUNKS):
        plane_recv, plane_prefix, axis_send, axis_recv = buffers[i][2:6]
        rows = slice(first * 8, (first + count) * 8)
        for copy in plane_copies[i]:
            copy.wait_recv()
        for k in (*FAR_Z, 0):
            b = zs[k]
            total = jnp.zeros((count * 8, L), F32)
            for q in range(NY):
                plane_prefix[q, b] = total
                total = plane_factor[q, rows, :] * total + plane_recv[q, b].astype(F32)
            if k == 0:
                axis_recv[z] = total.astype(BF16)
            else:
                axis_send[k] = total.astype(BF16)
                axis_copies[i].append(
                    push(axis_send.at[k], axis_recv.at[z], axis_s.at[i, k], axis_r.at[i, z], to_z[k])
                )
    half_queries = jnp.where(
        c == 0, queries.astype(F32), pltpu.roll(queries.astype(F32), 64, 1)
    ).astype(BF16)

    def from_z(q):
        note = pltpu.make_async_remote_copy(
            src_ref=axis_note, dst_ref=axis_notes.at[q], send_sem=note_s.at[0], recv_sem=note_r.at[q],
            device_id=at(q, y, c), device_id_type=MESH,
        )
        return [note] + [
            pltpu.make_async_remote_copy(
                src_ref=buffers[i][4].at[0], dst_ref=buffers[i][5].at[q],
                send_sem=axis_s.at[i, 0], recv_sem=axis_r.at[i, q],
                device_id=at(q, y, c), device_id_type=MESH,
            )
            for i in range(NCH)
        ]

    def back(q):
        return [
            pltpu.make_async_remote_copy(
                src_ref=buffers[i][6].at[q], dst_ref=buffers[i][7].at[z],
                send_sem=back_s.at[i, q], recv_sem=back_r.at[i, z],
                device_id=at(q, y, c), device_id_type=MESH,
            )
            for i in range(NCH)
        ]

    def from_back(q, i):
        return pltpu.make_async_remote_copy(
            src_ref=buffers[i][6].at[0], dst_ref=buffers[i][7].at[q],
            send_sem=back_s.at[i, 0], recv_sem=back_r.at[i, q],
            device_id=at(q, y, c), device_id_type=MESH,
        )

    totals = [jnp.zeros((count * 8, L), F32) for _, count in CHUNKS]
    for q in range(NZ):
        for i in range(NCH):
            buffers[i][6][q] = totals[i].astype(BF16)
        if q > 0:

            @pl.when(z != q)
            def _(q=q):
                for copy in back(q):
                    copy.start()

            @pl.when(z == q)
            def _(q=q):
                for i in range(NCH):
                    buffers[i][7][q] = buffers[i][6][q]

        if q == EARLY:
            for copy in part_copies:
                copy.wait_recv()
            my_half = [
                jnp.where(c == 0, plane_response[q, 0], pltpu.roll(plane_response[q, 0], 64, 1))[0 : 2 * M, 0:64]
                for q in range(1, NY)
            ]
            pool_rest = (pool_parts[0] + pool_parts[1]) + (pool_parts[2] + pool_parts[3])
            pool_tiles = []
            for i, (first, count) in enumerate(CHUNKS):
                plane_prefix = buffers[i][3]
                pool_tiles.append(
                    pool_rows(
                        my_half,
                        lambda m, plane_prefix=plane_prefix: [
                            plane_prefix[q, b, m * 8 : m * 8 + 8, :].astype(BF16)
                            for q in range(1, NY)
                            for b in range(NZ)
                        ],
                        first, count,
                    )
                )

        @pl.when(z != q)
        def _(q=q):
            for copy in from_z(q):
                copy.wait_recv()

        if q < NZ - 1:
            factor = spread(jnp.exp(axis_notes[q, 0:8, :]))
            for i, (first, count) in enumerate(CHUNKS):
                rows = slice(first * 8, (first + count) * 8)
                totals[i] = factor[rows, :] * totals[i] + buffers[i][5][q].astype(F32)

    @pl.when(z == 0)
    def _():
        for i in range(NCH):
            buffers[i][7][...] = jnp.zeros_like(buffers[i][7])

    lane = lax.broadcasted_iota(jnp.int32, (16, L), 1) // 8
    my_rows = jnp.zeros((16, L), F32)
    for q in range(NZ):
        turned = pltpu.roll(axis_notes[q, 8:24, :], lax.rem(2 * L + 8 * q - 64 * c - 8 * z, L), 1)
        my_rows = my_rows + jnp.where(lane == q, turned, 0.0)
    for i, (first, count) in enumerate(CHUNKS):
        axis_prefix = buffers[i][6]
        pool_tiles[i] = pool_tiles[i] + pool_rows(
            [my_rows[0 : 2 * M, 0:64]],
            lambda m, axis_prefix=axis_prefix: [
                axis_prefix[q, m * 8 : m * 8 + 8, :] for q in range(NZ)
            ],
            first, count,
        )
    pool_send[...] = pool_rest + jnp.concatenate(
        [*pool_tiles, jnp.zeros((8 - M, L), F32)], axis=0
    )
    pool_axis[z] = pool_send[...]
    pool_copies = [
        push(pool_send, pool_axis.at[z], small_s.at[17 + k], small_r.at[17 + k], to_z[k])
        for k in FAR_Z
    ]

    earlier = list(sends)
    sends.clear()
    chip_copies = [[] for _ in CHUNKS]
    for i, (first, count) in enumerate(CHUNKS):
        plane_prefix = buffers[i][3]
        start_plane, start_send, start_chip = buffers[i][7:10]
        rows = slice(first * 8, (first + count) * 8)
        for q in range(NZ):

            @pl.when((z != q) & (z > 0))
            def _(q=q, i=i):
                from_back(q, i).wait_recv()

        for k in (*FAR_Y, 0):
            g = ys[k]

            @pl.loop(0, NZ, unroll=True)
            def _(b, g=g, k=k):
                start = plane_start[g, rows, :] * start_plane[b].astype(F32) + plane_prefix[g, b]
                if k == 0:
                    start_chip[y, b] = start.astype(BF16)
                else:
                    start_send[k, b] = start.astype(BF16)

            if k:
                chip_copies[i].append(
                    push(start_send.at[k], start_chip.at[y], plane_s.at[i, 3 + k], plane_r.at[i, 3 + k], to_y[k])
                )

    for copy in earlier:
        copy.wait_send()

    for q in range(1, NZ):

        @pl.when(z != q)
        def _(q=q):
            for copy in back(q):
                copy.wait_send()

    for copy in pool_copies:
        copy.wait_recv()
    total = pool_axis[0]
    for q in range(1, NZ):
        total = total + pool_axis[q]
    pool_sum[...] = total
    mine = pool_plane.at[y * NC + c]
    pool_plane[y * NC + c] = total
    last_copies = (
        [push(pool_sum, mine, small_s.at[24 + k], small_r.at[24 + k], to_y[k]) for k in FAR_Y]
        + [push(pool_sum, mine, small_s.at[27 + k], small_r.at[27 + k], to_y_other[k]) for k in FAR_Y]
        + [push(pool_sum, mine, small_s.at[31], small_r.at[31], to_pair)]
    )

    half_copies = []
    for i, (first, count) in enumerate(CHUNKS):
        state = buffers[i][0]
        start_chip, carried, carried_recv = buffers[i][9:12]
        rows = slice(first * 8, (first + count) * 8)
        for copy in chip_copies[i]:
            copy.wait_recv()

        @pl.loop(0, NY)
        def _(g):
            @pl.loop(0, NZ, unroll=True)
            def _(b):
                before = start_chip[g, b].astype(F32)
                after = start_factor[g, rows, :] * before + state[0, g, b].astype(F32)
                carried[0, g, b] = start_chip[g, b]
                carried[1, g, b] = after.astype(BF16)

        half_copies.append(
            push(carried.at[other], carried_recv, pair_s.at[NCH + i], pair_r.at[NCH + i], to_pair)
        )

    stores = []

    def final(i):
        first, count = CHUNKS[i]
        carried, carried_recv = buffers[i][10:12]
        half_copies[i].wait_recv()
        for g in range(NY):
            for m in range(count):
                j = g * M + first + m
                lanes = slice(j * L, (j + 1) * L)
                tile = slice(m * 8, m * 8 + 8)
                start = jnp.concatenate(
                    [carried[c, g, b, tile, :] for b in range(NZ)]
                    + [carried_recv[g, b, tile, :] for b in range(NZ)],
                    axis=0,
                )
                full = local_out[j] + grow[j] * jnp.dot(
                    half_queries, start, preferred_element_type=F32
                )
                out_ref[:, lanes] = full.astype(BF16)
            lanes = slice((g * M + first) * L, (g * M + first + count) * L)
            store = pltpu.make_async_copy(
                out_ref.at[:, lanes], mixed_ref.at[:, lanes], out_s.at[i * NY + g]
            )
            store.start()
            stores.append(store)

    for i in range(NCH):
        final(i)

    for copy in table_copies:
        copy.wait_recv()
    loads[2].wait()
    for copy in last_copies:
        copy.wait_recv()
    pooled = [
        (pool_plane[NC * g] + pool_plane[NC * g + 1]) / (G * NZ * NY * NC) for g in range(NY)
    ]
    square = sum(jnp.sum(p * p, keepdims=True) for p in pooled) / (TILES * L)
    scale = 1.0 / jnp.sqrt(square + EPS)
    wide = jnp.concatenate(
        [
            jnp.broadcast_to((pooled[g] * scale)[m : m + 1, :], (16, L)).astype(BF16)
            for g in range(NY)
            for m in range(M)
        ],
        axis=1,
    )
    classifier = table[...].reshape(TILES * L, L)
    logits = jnp.dot(wide, classifier, preferred_element_type=F32)
    logits_ref[...] = logits[0:1, :]

    for store in stores:
        store.wait()

    for copy in sends:
        copy.wait_send()


def hand_over(mixed_in, logits_in, mixed_out, logits_out, mixed, logits, in_sem, out_sem):
    pairs = [(logits_in, logits, logits_out)]
    for i in range(PIECES):
        rows = slice(i * (G // PIECES), (i + 1) * (G // PIECES))
        pairs.append((mixed_in.at[rows, :], mixed.at[rows, :], mixed_out.at[rows, :]))
    loads = [pltpu.make_async_copy(a, b, in_sem.at[i]) for i, (a, b, _) in enumerate(pairs)]
    stores = [pltpu.make_async_copy(b, c, out_sem.at[i]) for i, (_, b, c) in enumerate(pairs)]
    for load in loads:
        load.start()
    for load, store in zip(loads, stores):
        load.wait()
        store.start()
    for store in stores:
        store.wait()


def local(inputs, keys_queries, log_decay, skip, classifier):
    copies, positions, channels = inputs.shape
    heads = log_decay.shape[1]
    hbm = pl.BlockSpec(memory_space=pltpu.HBM)

    def chunk(count):
        slab = (NZ, count * 8, L)
        return [
            pltpu.VMEM((3, NY, *slab), BF16),
            pltpu.VMEM((NY, *slab), BF16),
            pltpu.VMEM((NY, *slab), BF16),
            pltpu.VMEM((NY, *slab), F32),
            pltpu.VMEM(slab, BF16),
            pltpu.VMEM(slab, BF16),
            pltpu.VMEM(slab, BF16),
            pltpu.VMEM(slab, BF16),
            pltpu.VMEM((NY, *slab), BF16),
            pltpu.VMEM((NY, *slab), BF16),
            pltpu.VMEM((NC, NY, *slab), BF16),
            pltpu.VMEM((NY, *slab), BF16),
        ]

    dma = pltpu.SemaphoreType.DMA
    scratch = [
        pltpu.VMEM((positions, channels), BF16),
        pltpu.VMEM((positions, 2 * N), BF16),
        pltpu.VMEM((heads, positions), F32),
        pltpu.VMEM((positions, channels), BF16),
        pltpu.VMEM((TILES, G, L), F32),
        pltpu.VMEM((TILES, G, L), F32),
        pltpu.VMEM((NX, *classifier.shape), BF16),
        pltpu.VMEM((NY, 8, L), F32),
        pltpu.VMEM((NY, 8, L), F32),
        pltpu.VMEM((NY, 8, L), F32),
        pltpu.VMEM((NY, 8, L), F32),
        pltpu.VMEM((NY, M * 8, L), F32),
        pltpu.VMEM((NY, M * 8, L), F32),
        pltpu.VMEM((NY, M * 8, L), F32),
        pltpu.VMEM((NY, M * 8, L), F32),
        pltpu.VMEM((2, HEADS, L), F32),
        pltpu.VMEM((2, HEADS, L), F32),
        pltpu.VMEM((NY, 2, 16, L), F32),
        pltpu.VMEM((NY, 2, 16, L), F32),
        pltpu.VMEM((24, L), F32),
        pltpu.VMEM((NZ, 24, L), F32),
        pltpu.VMEM((NY, 8, L), F32),
        pltpu.VMEM((NY, 8, L), F32),
        pltpu.VMEM((8, L), F32),
        pltpu.VMEM((NZ, 8, L), F32),
        pltpu.VMEM((8, L), F32),
        pltpu.VMEM((NY * NC, 8, L), F32),
        *[ref for _, count in CHUNKS for ref in chunk(count)],
        dma((3 + NCH * NY,)), dma((NCH * NY,)),
        dma((2 * NCH,)), dma((2 * NCH,)), dma((NCH, 7)), dma((NCH, 7)),
        dma((NCH, NZ)), dma((NCH, NZ)), dma((NCH, NZ)), dma((NCH, NZ)),
        dma((NZ,)), dma((NZ,)), dma((NX,)), dma((NX,)), dma((32,)), dma((32,)),
    ]
    mixed, logits = pl.pallas_call(
        kernel,
        out_shape=(
            jax.ShapeDtypeStruct((positions, channels), BF16),
            jax.ShapeDtypeStruct((1, classifier.shape[1]), F32),
        ),
        in_specs=[hbm, hbm, hbm, pl.BlockSpec(memory_space=pltpu.SMEM), hbm],
        out_specs=(hbm, pl.BlockSpec(memory_space=pltpu.VMEM)),
        scratch_shapes=scratch,
        compiler_params=pltpu.CompilerParams(
            collective_id=0, has_side_effects=True, vmem_limit_bytes=60 << 20
        ),
    )(
        inputs.reshape(positions, channels),
        keys_queries.reshape(positions, 2 * N),
        log_decay.reshape(heads, positions),
        skip,
        classifier,
    )
    mixed, logits = pl.pallas_call(
        hand_over,
        out_shape=(
            jax.ShapeDtypeStruct(mixed.shape, mixed.dtype),
            jax.ShapeDtypeStruct(logits.shape, logits.dtype),
        ),
        in_specs=[hbm, hbm],
        out_specs=(hbm, hbm),
        scratch_shapes=[
            pltpu.VMEM(mixed.shape, mixed.dtype),
            pltpu.VMEM(logits.shape, logits.dtype),
            dma((PIECES + 1,)),
            dma((PIECES + 1,)),
        ],
        compiler_params=pltpu.CompilerParams(vmem_limit_bytes=60 << 20),
    )(mixed, logits)
    return mixed.reshape(copies, positions, channels), logits


def solution(mesh):
    return jax.shard_map(
        local,
        mesh=mesh,
        in_specs=(
            P("fsdp", "seq", None),
            P("fsdp", "seq", None),
            P("fsdp", None, "seq"),
            P(),
            P("fsdp", None),
        ),
        out_specs=(P("fsdp", "seq", None), P("fsdp", None)),
        check_vma=False,
    )
```
